32 devices in a mesh: segment: 2 (over core), expert: 16 (over z, y, x).
Axes of the slice: x: 2, y: 2, z: 4, core: 2. Of those that a mesh axis runs over, the one named last changes fastest.
Arguments:
- rollout: bfloat16 [2048, 4096], P('expert', 'segment'), may hold values from -6 to 6
- norm_gain: bfloat16 [2, 4096], P('segment'), may hold values from 0.25 to 1.75
- router_first: bfloat16 [2, 4096, 28], P('segment')
- gain_second: bfloat16 [2, 4096], P('segment'), may hold values from 0.25 to 1.75
- router_second: bfloat16 [2, 4096, 28], P('segment')
- expert_ids: int32 [2048, 8], P('expert'), may hold values from 0 to 27, as said below
- copy_pick: int32 [2048, 8], P('expert'), may hold values from 0 to 5
- later_ids: int32 [2048, 8], P('expert'), may hold values from 0 to 27, all different within a row
- slot_table: int32 [32], replicated, may hold values from 0 to 27, as said below
- expert_in: bfloat16 [32, 4096, 1536], P(('segment', 'expert'))
- expert_out: bfloat16 [32, 768, 4096], P(('segment', 'expert'))
Outputs:
- states: bfloat16 [2, 2048, 4096], P('segment', 'expert')
- log_ratio: float32 [1024, 2], P('expert', 'segment')
The draws below stay inside these ranges and needn't reach their ends.
Inputs may be any that keep to these rules, and one draw needn't show every extreme that they name: `expert_ids`: each row names 8 different experts. `slot_table`: every expert is held by one, two or three slots.
All inputs are finite; a program needn't handle non-finite values.
Results may differ from the reference program's by a relative error of at most 0.013.
The reference program's roundings to bfloat16 on the way count: a program that leaves them out, or rounds other values in their place, can miss the bound.
Values may be sent and summed in bfloat16 or wider, within the bound.
A program may use at most 192 MiB of HBM per device.

```python
import jax
import jax.numpy as jnp
from jax import lax

D = 4096
FF = 768
TOP = 8
TOK_DEV = 128
SLOTS = 32
HOT = 2
EXPERTS = 28
CAP = 48
TOKENS = 2048
N_EXPERT = 16


def slot_plan(key):
    hot = jax.random.permutation(jax.random.fold_in(key, 11), EXPERTS)[:HOT].astype(jnp.int32)
    base = jnp.concatenate([jnp.arange(EXPERTS, dtype=jnp.int32), hot, hot])
    order = jax.random.permutation(jax.random.fold_in(key, 12), SLOTS)
    table = base[order].astype(jnp.int32)
    is_hot = jnp.sum((jnp.arange(EXPERTS, dtype=jnp.int32)[:, None] == hot[None, :]).astype(jnp.int32), axis=1)
    return (table, is_hot)


def draw_slot_table(key, part):
    return slot_plan(key)[0]


def draw_expert_ids(key, part):
    table, is_hot = slot_plan(key)
    scores = jax.random.randint(jax.random.fold_in(key, 13), (TOKENS, EXPERTS), 0, 1000) + 200 * is_hot[None, :]
    ranks = jax.random.permutation(jax.random.fold_in(key, 14), EXPERTS).astype(jnp.int32)
    distinct = scores * EXPERTS + ranks[None, :]
    return lax.top_k(distinct, TOP)[1].astype(jnp.int32)


def expert_draw(key, salt, rows, cols):
    table = slot_plan(key)[0]
    base = jax.random.fold_in(key, salt)

    def one(expert):
        values = jax.random.normal(jax.random.fold_in(base, expert), (rows, cols), jnp.float32)
        return (values * rows ** (-0.5)).astype(jnp.bfloat16)
    return lax.map(one, table)


def draw_expert_in(key, part):
    return expert_draw(key, 21, D, 2 * FF)


def draw_expert_out(key, part):
    return expert_draw(key, 22, FF, D)


def router_draw(key, salt):
    values = jax.random.normal(jax.random.fold_in(key, salt), (2, D, EXPERTS), jnp.float32) * D ** (-0.5)
    spread = jax.random.uniform(jax.random.fold_in(key, salt + 1), (2, 1, EXPERTS), jnp.float32, 0.5, 2.5)
    values = values * spread
    return values.astype(jnp.bfloat16)


def draw_router_first(key, part):
    return router_draw(key, 31)


def draw_router_second(key, part):
    return router_draw(key, 41)


def plant(values, key, least, top_value):
    place = [jax.random.randint(jax.random.fold_in(key, axis), (), 0, length) for axis, length in enumerate(values.shape)]
    main_axis = values.shape.index(max(values.shape))
    next_to = place[:main_axis] + [(place[main_axis] + 1) % values.shape[main_axis]] + place[main_axis + 1:]
    return values.at[tuple(place)].set(least).at[tuple(next_to)].set(top_value)


def block_scale(rng, dims, shards, low, high):
    level = 1.0
    for position, blocks in shards:
        steps = jax.random.uniform(jax.random.fold_in(jax.random.fold_in(rng, 6), position), (blocks,), jnp.float32, low / len(shards), high / len(shards))
        level = level * jnp.repeat(jnp.exp(steps), dims[position] // blocks).reshape((-1,) + (1,) * (len(dims) - 1 - position))
    return level


def choose_distinct(own_key, rows, number_of, top, lift):
    ranking = jax.random.permutation(jax.random.fold_in(own_key, 1), number_of)
    pull = ranking
    for power in range(3):
        pull = pull * pull // number_of
    pull = pull * lift // number_of
    lots = jax.random.randint(jax.random.fold_in(own_key, 2), (rows, number_of), 0, 4096) + pull
    sure = jax.random.permutation(jax.random.fold_in(own_key, 3), rows)[jnp.arange(number_of) % rows]
    lots = jnp.where(jnp.arange(rows)[:, None] == sure[None, :], 1 << 14, lots)
    score = lots * number_of + jnp.arange(number_of)
    return lax.top_k(score.astype(jnp.int32), top)[1].astype(jnp.int32)


def scatter_about(key, dims, scale, most, pieces=(), held_as=jnp.bfloat16):
    level = block_scale(key, dims, pieces, -0.22, 0.18) if pieces else 1.0
    values = jax.random.normal(key, dims, jnp.float32) * scale * level
    return jnp.minimum(jnp.maximum(values, -most), most).astype(held_as)


def setup_inputs(seed: int = 0) -> dict:
    key_list = jax.random.split(jax.random.key(seed), 12)
    rollout = scatter_about(key_list[0], (TOKENS, D), 1.0, 6.0, ((0, 16), (1, 2)))
    norm_gain = jnp.clip(1.0 + 0.15 * jax.random.normal(key_list[1], (2, D), jnp.float32), 0.25, 1.75).astype(jnp.bfloat16)
    router_first = draw_router_first(jax.random.fold_in(key_list[11], 71), 0)
    gain_second = jnp.clip(1.0 + 0.15 * jax.random.normal(key_list[3], (2, D), jnp.float32), 0.25, 1.75).astype(jnp.bfloat16)
    router_second = draw_router_second(jax.random.fold_in(key_list[11], 71), 0)
    expert_ids = draw_expert_ids(jax.random.fold_in(key_list[11], 71), 0)
    copy_pick = plant(jax.random.randint(key_list[6], (TOKENS, TOP), 0, 6), jax.random.fold_in(key_list[6], 1), 0, 5).astype(jnp.int32)
    later_ids = choose_distinct(key_list[7], TOKENS, EXPERTS, TOP, 2340)
    slot_table = draw_slot_table(jax.random.fold_in(key_list[11], 71), 0)
    expert_in = draw_expert_in(jax.random.fold_in(key_list[11], 71), 0)
    expert_out = draw_expert_out(jax.random.fold_in(key_list[11], 71), 0)
    return dict(rollout=rollout, norm_gain=norm_gain, router_first=router_first, gain_second=gain_second, router_second=router_second, expert_ids=expert_ids, copy_pick=copy_pick, later_ids=later_ids, slot_table=slot_table, expert_in=expert_in, expert_out=expert_out)


def rms_scale(values, gain):
    return values * lax.rsqrt(lax.optimization_barrier(jnp.mean(values * values, axis=-1, keepdims=True)) + 1e-06) * gain.astype(jnp.float32)

def slot_routes(expert_ids, copy_pick, slot_table):
    slot_ids = jnp.arange(SLOTS, dtype=jnp.int32)
    same = slot_table[:, None] == slot_table[None, :]
    earlier = slot_ids[:, None] < slot_ids[None, :]
    copy_rank = lax.optimization_barrier(jnp.sum((same & earlier).astype(jnp.int32), axis=0))
    holders = lax.optimization_barrier(jnp.sum((slot_table[None, :] == jnp.arange(EXPERTS, dtype=jnp.int32)[:, None]).astype(jnp.int32), axis=1))
    picked = (expert_ids[..., None] == jnp.arange(EXPERTS, dtype=jnp.int32)).astype(jnp.int32)
    copies = lax.optimization_barrier(jnp.sum(picked * holders, axis=-1))
    wanted = copy_pick % copies
    match = ((slot_table == expert_ids[..., None]) & (copy_rank == wanted[..., None])).astype(jnp.int32)
    slot = lax.optimization_barrier(jnp.sum(match * slot_ids, axis=-1)).astype(jnp.int32)
    return (slot, match)

def reference(rollout, norm_gain, router_first, gain_second, router_second, expert_ids, copy_pick, later_ids, slot_table, expert_in, expert_out):
    states_in = rollout.astype(jnp.float32)
    slot, match = slot_routes(expert_ids, copy_pick, slot_table)
    blocks = match.reshape(N_EXPERT, TOK_DEV * TOP, SLOTS)
    before = jnp.cumsum(blocks, axis=1) - blocks
    rank = lax.optimization_barrier(jnp.sum(before * blocks, axis=-1)).reshape(TOKENS, TOP).astype(jnp.int32)
    kept = rank < CAP
    rank_c = jnp.where(kept, rank, CAP).astype(jnp.int32)
    token_ids = jnp.arange(TOKENS, dtype=jnp.int32)
    source = jnp.broadcast_to((token_ids // TOK_DEV)[:, None], (TOKENS, TOP)).astype(jnp.int32)
    local = jnp.broadcast_to((token_ids % TOK_DEV)[:, None], (TOKENS, TOP)).astype(jnp.int32)
    normed_all = []
    gates_all = []
    for section in range(2):
        normed = rms_scale(states_in, norm_gain[section]).astype(jnp.bfloat16)
        logits = jnp.dot(normed, router_first[section], preferred_element_type=jnp.float32)
        chosen = jnp.take_along_axis(logits, expert_ids, axis=1)
        lifted = jnp.exp(chosen - lax.optimization_barrier(jnp.max(chosen, axis=1, keepdims=True)))
        gates = (lifted / lax.optimization_barrier(jnp.sum(lifted, axis=1, keepdims=True))).astype(jnp.bfloat16)
        normed_all.append(normed)
        gates_all.append(gates)
    normed_all = jnp.stack(normed_all)
    gates_all = jnp.stack(gates_all).astype(jnp.float32)
    inverse = jnp.full((N_EXPERT, SLOTS, CAP), TOK_DEV, jnp.int32).at[source, slot, rank_c].set(local, mode='drop')
    gate_slots = jnp.zeros((2, N_EXPERT, SLOTS, CAP), jnp.float32).at[:, source, slot, rank_c].set(gates_all, mode='drop')
    padded = jnp.concatenate([normed_all.reshape(2, N_EXPERT, TOK_DEV, D), jnp.zeros((2, N_EXPERT, 1, D), jnp.bfloat16)], axis=2)
    block_ids = jnp.arange(N_EXPERT, dtype=jnp.int32)[:, None]

    def one_slot(total, inputs):
        index, weight, w_in, w_out = inputs
        rows = padded[:, block_ids, index]
        hidden = jnp.dot(rows.reshape(-1, D), w_in, preferred_element_type=jnp.float32)
        active = (jax.nn.silu(hidden[:, :FF]) * hidden[:, FF:]).astype(jnp.bfloat16)
        result = jnp.dot(active, w_out, preferred_element_type=jnp.float32).astype(jnp.bfloat16)
        result = lax.optimization_barrier(result).astype(jnp.float32).reshape(2, N_EXPERT, CAP, D)
        total = total.at[:, block_ids, index].add(weight[..., None] * result)
        return (total, None)
    start = jnp.zeros((2, N_EXPERT, TOK_DEV + 1, D), jnp.float32)
    total, _ = lax.scan(one_slot, start, (inverse.transpose(1, 0, 2), gate_slots.transpose(2, 0, 1, 3), expert_in, expert_out))
    mixed = states_in[None] + total[:, :, :TOK_DEV].reshape(2, TOKENS, D)
    states = mixed.astype(jnp.bfloat16)
    scores = []
    for section in range(2):
        later = rms_scale(mixed[section], gain_second[section]).astype(jnp.bfloat16)
        logits = jnp.dot(later, router_second[section], preferred_element_type=jnp.float32)
        logp = jax.nn.log_softmax(logits, axis=-1)
        scores.append(lax.optimization_barrier(jnp.sum(jnp.take_along_axis(logp, later_ids, axis=1), axis=1)))
    return (states, (scores[1] - scores[0]).reshape(TOKENS // 2, 2))
```

```python
import functools
import math

import jax
import jax.numpy as jnp
from jax import lax
from jax.experimental import pallas as pl
from jax.experimental.pallas import tpu as pltpu
from jax.sharding import PartitionSpec as P

LANES = 128
VMEM_BUDGET = 26 << 20
VMEM_LIMIT = 60 * 1024 * 1024
MESH = pl.DeviceIdType.MESH
INFO_ROWS = 16
FACTOR_ROW = 12


def grid_sides(count):
    outer = 1
    while outer**3 < count:
        outer *= 2
    rest = count // outer
    middle = 1
    while middle**2 < rest:
        middle *= 2
    return outer, middle, rest // middle


class Plan:
    def __init__(self, sides):
        logs = [side.bit_length() - 1 for side in sides]
        n_a, n_b, n_c = logs
        bits_c = list(range(n_c))
        bits_b = list(range(n_c, n_c + n_b))
        bits_a = list(range(n_c + n_b, n_c + n_b + n_a))
        self.count = n_a + n_b + n_c
        self.blocks = 1 << self.count
        self.leaf = (bits_c[0], bits_b[0])
        orders = (
            (bits_c + bits_a + bits_b, bits_c + bits_b + bits_a),
            (bits_b + bits_a + bits_c, bits_b + bits_c + bits_a),
        )
        self.rest = [[order[1:] for order in pair] for pair in orders]
        self.stages = self.count - 1

    def dims(self, which, order, done):
        used = [self.leaf[which]] + self.rest[which][order][:done]
        return [bit for bit in reversed(range(self.count)) if bit not in used]


def bit_of(index, bit):
    return (index // (1 << bit)) % 2


def flip(index, bit):
    return index + (1 << bit) * (1 - 2 * bit_of(index, bit))


def digits(value, count):
    return [(value // (1 << (count - 1 - i))) % 2 for i in range(count)]


def spread_index(value, bit, own):
    low = 1 << bit
    return (value // low) * (2 * low) + own * low + value % low


def remote(src, dst, send, recv, peer):
    return pltpu.make_async_remote_copy(
        src_ref=src,
        dst_ref=dst,
        send_sem=send,
        recv_sem=recv,
        device_id=peer,
        device_id_type=MESH,
    )


def run_stages(chunks, stages, after_first=None):
    depth = max(lag for lag, _ in stages)

    @pl.loop(0, chunks + depth)
    def _(step):
        for lag, stage in stages:

            @pl.when((step >= lag) & (step - lag < chunks))
            def _():
                stage(step - lag)

        if after_first is not None:

            @pl.when(step == 0)
            def _():
                after_first()


def by_parity(stage):
    def run(j):
        for which in range(2):

            @pl.when(j % 2 == which)
            def _():
                stage(which, j)

    return run


def return_kernel(plan, chunks, act, w_out, told, out, wts, ys, leaf, swapped, *rest):
    stages = plan.stages
    parts, arrived, sems = rest[:stages], rest[stages : 2 * stages], rest[2 * stages :]
    seg = lax.axis_index("segment")
    me = lax.axis_index("expert")
    side = plan.blocks // 2
    room = ys.shape[-2]
    wide = ys.shape[-1]
    slot_rows = plan.blocks * room
    tok_rows = out.shape[0]
    half_rows = tok_rows // 2
    mine = [bit_of(me, bit) for bit in range(plan.count)]

    barrier = pltpu.get_barrier_semaphore()
    friends = [(1 - seg, me)]
    friends += [(seg, flip(me, bit)) for bit in range(plan.count)]
    friends += [(1 - seg, flip(me, bit)) for bit in plan.leaf]
    for friend in friends:
        pl.semaphore_signal(barrier, inc=1, device_id=friend, device_id_type=MESH)
    pl.semaphore_wait(barrier, len(friends))

    def region(which, own):
        bit = plan.leaf[which]
        place = plan.count - 1 - bit
        return tuple(
            (mine[bit] if own else 1 - mine[bit]) if i == place else slice(None)
            for i in range(plan.count)
        )

    def first_copies(which, j):
        slot = j % 3
        nbr = flip(me, plan.leaf[which])
        sources = (
            (ys.at[(slot, 1) + region(which, False)], leaf.at[j, 0], (seg, nbr)),
            (ys.at[(slot, 0) + region(which, False)], leaf.at[j, 1], (1 - seg, nbr)),
            (ys.at[(slot, 0) + region(which, True)], swapped.at[j], (1 - seg, me)),
        )
        return [
            remote(src, dst, sems[0].at[slot, k], sems[1].at[j, k], peer)
            for k, (src, dst, peer) in enumerate(sources)
        ]

    def send(which, t, r, j):
        bit = plan.rest[which][r][t]
        dims = plan.dims(which, r, t)
        index = tuple(1 - mine[d] if d == bit else slice(None) for d in dims)
        if t == 0:
            src = parts[0].at[(j % 2,) + index + (pl.ds(r * half_rows, half_rows),)]
        else:
            src = parts[t].at[(j % 2, r) + index]
        return remote(
            src,
            arrived[t].at[j, r],
            sems[2 + 2 * t].at[j % 2, r],
            sems[3 + 2 * t].at[j, r],
            (seg, flip(me, bit)),
        )

    def project(which, j):
        columns = pl.ds(pl.multiple_of(j * wide, wide), wide)
        blocks = (2,) * plan.count
        for section in range(2):
            result = jnp.dot(
                act[pl.ds(section * slot_rows, slot_rows), :],
                w_out[:, columns],
                preferred_element_type=jnp.float32,
            ).astype(jnp.bfloat16)
            ys[j % 3, section] = result.reshape(blocks + (room, wide))
        for copy in first_copies(which, j):
            copy.start()

    def make_weights():
        row = lax.broadcasted_iota(jnp.int32, (room, tok_rows), 0).astype(jnp.float32)
        for which in range(2):

            @pl.loop(0, side)
            def _(q):
                info = told[spread_index(q, plan.leaf[which], mine[plan.leaf[which]])]
                pieces = []
                for k in (0, 1, 2 + 2 * which, 3 + 2 * which):
                    hit = info[k : k + 1, :] == row
                    pieces.append(jnp.where(hit, info[6 + k : 7 + k, :], 0.0))
                pad = -(4 * room) % LANES
                if pad:
                    pieces.append(jnp.zeros((pad, tok_rows), jnp.float32))
                turned = jnp.concatenate(pieces, axis=0).T
                wts[which, q] = turned[:, : 4 * room].astype(jnp.bfloat16)

    def combine(which, j):
        for copy in first_copies(which, j):
            copy.wait()
        own = mine[plan.leaf[which]]
        place = plan.count - 1 - plan.leaf[which]

        @pl.loop(0, side, unroll=4)
        def _(q):
            ix = digits(q, plan.stages)
            full = tuple(ix[:place] + [own] + ix[place:])
            both = jnp.concatenate(
                [
                    ys[(j % 3, 1) + full],
                    swapped[(j,) + tuple(ix)],
                    leaf[(j, 0) + tuple(ix)],
                    leaf[(j, 1) + tuple(ix)],
                ],
                axis=0,
            )
            part = jnp.dot(wts[which, q], both, preferred_element_type=jnp.float32)
            parts[0][(j % 2,) + tuple(ix)] = part.astype(jnp.bfloat16)

        for r in range(2):
            send(which, 0, r, j).start()

    def reduce_stage(t, which, j):
        last = t == stages - 1
        for r in range(2):
            send(which, t, r, j).wait()
            bit = plan.rest[which][r][t]
            place = plan.dims(which, r, t).index(bit)
            left = stages - 1 - t

            def total(ix):
                full = tuple(ix[:place] + [mine[bit]] + ix[place:])
                if t == 0:
                    held = parts[0][(j % 2,) + full + (pl.ds(r * half_rows, half_rows),)]
                else:
                    held = parts[t][(j % 2, r) + full]
                return held.astype(jnp.float32) + arrived[t][(j, r) + tuple(ix)].astype(jnp.float32)

            if last:
                columns = pl.ds(pl.multiple_of(j * wide, wide), wide)
                out[pl.ds(r * half_rows, half_rows), columns] = total([])
            else:

                @pl.loop(0, 1 << left)
                def _(e):
                    ix = digits(e, left)
                    parts[t + 1][(j % 2, r) + tuple(ix)] = total(ix).astype(jnp.bfloat16)

            if not last:
                send(which, t + 1, r, j).start()

    steps = [(0, by_parity(project)), (2, by_parity(combine))]
    for t in range(stages):
        steps.append((3 + t, by_parity(functools.partial(reduce_stage, t))))
    run_stages(chunks, steps, make_weights)


def return_call(plan, room, act, w_out, told):
    tok_rows = told.shape[2]
    wide = 2 * LANES
    side = plan.blocks // 2
    chunk_bytes = 2 * wide * (3 * side * room + sum(side >> t for t in range(1, plan.count)) * tok_rows)
    chunks = w_out.shape[1] // wide
    while chunks % 4 == 0 and chunks * chunk_bytes > VMEM_BUDGET:
        chunks //= 2

    def bf(*shape):
        return pltpu.VMEM(shape, jnp.bfloat16)

    def dma(*shape):
        return pltpu.SemaphoreType.DMA(shape)

    two = (2,)
    scratch = [
        bf(2, side, tok_rows, 4 * room),
        bf(3, 2, *(two * plan.count), room, wide),
        bf(chunks, 2, *(two * plan.stages), room, wide),
        bf(chunks, *(two * plan.stages), room, wide),
        bf(2, *(two * plan.stages), tok_rows, wide),
    ]
    for t in range(1, plan.stages):
        scratch.append(bf(2, 2, *(two * (plan.stages - t)), tok_rows // 2, wide))
    sems = [dma(3, 3), dma(chunks, 3)]
    for t in range(plan.stages):
        scratch.append(bf(chunks, 2, *(two * (plan.stages - 1 - t)), tok_rows // 2, wide))
        sems += [dma(2, 2), dma(chunks, 2)]
    piece = chunks * wide
    call = pl.pallas_call(
        functools.partial(return_kernel, plan, chunks),
        out_shape=jax.ShapeDtypeStruct((tok_rows, piece), jnp.float32),
        in_specs=[pl.BlockSpec(memory_space=pltpu.VMEM)] * 3,
        out_specs=pl.BlockSpec(memory_space=pltpu.VMEM),
        scratch_shapes=scratch + sems,
        compiler_params=pltpu.CompilerParams(
            collective_id=0, has_side_effects=True, vmem_limit_bytes=VMEM_LIMIT
        ),
        name="return_sum",
    )
    pieces = [
        call(act, w_out[:, start : start + piece], told)
        for start in range(0, w_out.shape[1], piece)
    ]
    return pieces[0] if len(pieces) == 1 else jnp.concatenate(pieces, axis=1)


def gather_kernel(plan, chunks, x, info, gains, w_in, act, info_out, *rest):
    (held, info_got, picks, scale, keep, give, got, lhs, hid, w_buf) = rest[:10]
    sems = rest[10:]
    blocks = plan.blocks
    side = blocks // 2
    seg = lax.axis_index("segment")
    me = lax.axis_index("expert")
    mine = [bit_of(me, bit) for bit in range(plan.count)]
    tok_rows, half = x.shape
    half_rows = tok_rows // 2
    wide = half // chunks
    room = keep.shape[-2]
    slot_rows = blocks * room
    units = act.shape[1]

    barrier = pltpu.get_barrier_semaphore()
    friends = [(1 - seg, me)] + [(1 - seg, flip(me, bit)) for bit in plan.leaf]
    for friend in friends:
        pl.semaphore_signal(barrier, inc=1, device_id=friend, device_id_type=MESH)

    @pl.loop(1, blocks)
    def _(k):
        pl.semaphore_signal(
            barrier, inc=1, device_id=(seg, (me + k) % blocks), device_id_type=MESH
        )

    pl.semaphore_wait(barrier, blocks - 1 + len(friends))

    def tell(k):
        to = (me + k) % blocks
        return remote(
            info.at[to], info_got.at[me], sems[0].at[k - 1], sems[1].at[k - 1], (seg, to)
        )

    def columns(j):
        return pl.ds(pl.multiple_of(j * wide, wide), wide)

    def send(which, t, r, j):
        order = plan.rest[which][r]
        bit = order[plan.stages - 1 - t]
        free = order[plan.stages - t :]
        rows = pl.ds(r * half_rows, half_rows)
        index = tuple(slice(None) if d in free else mine[d] for d in plan.dims(which, r, 0))
        dst = held.at[(j,) + index + (rows,)]
        return remote(
            x.at[rows, columns(j)] if t == 0 else dst,
            dst,
            sems[6 + 2 * t].at[j % 2, r],
            sems[7 + 2 * t].at[j, r],
            (seg, flip(me, bit)),
        )

    def first_send(which, j):
        for r in range(2):
            send(which, 0, r, j).start()
        index = tuple(mine[d] for d in plan.dims(which, 0, 0))
        held[(j,) + index] = x[:, columns(j)]

    def relay(t, which, j):
        for r in range(2):
            send(which, t - 1, r, j).wait()
            send(which, t, r, j).start()

    def last_copies(which, j):
        nbr = flip(me, plan.leaf[which])
        peers = ((1 - seg, me), (seg, nbr), (1 - seg, nbr))
        return [
            remote(
                give.at[j % 3, k],
                got.at[j, k],
                sems[2].at[j % 3, k],
                sems[3].at[j, k],
                peer,
            )
            for k, peer in enumerate(peers)
        ]

    def weight_copies(j):
        copies = []
        for which, owner in enumerate((seg, 1 - seg)):
            rows = pl.ds(pl.multiple_of(owner * half + j * wide, wide), wide)
            copies.append(
                pltpu.make_async_copy(
                    w_in.at[rows, :],
                    w_buf.at[j % 3, pl.ds(which * wide, wide)],
                    sems[4].at[j % 3, which],
                )
            )
        return copies

    def read_info():
        info_got[me] = info[me]

        @pl.loop(1, blocks)
        def _(k):
            tell(k).wait()

        row = lax.broadcasted_iota(jnp.int32, (room, tok_rows), 0).astype(jnp.float32)

        @pl.loop(0, blocks)
        def _(d):
            told = info_got[d]
            info_out[d] = told
            own = told[0:1, :] == row
            factor = jnp.sum(
                jnp.where(own, told[FACTOR_ROW : FACTOR_ROW + 1, :], 0.0), axis=1, keepdims=True
            )
            rows = pl.ds(pl.multiple_of(d * room, room), room)
            scale[rows, :] = jnp.broadcast_to(factor, (room, wide))

        for which in range(2):

            @pl.loop(0, side)
            def _(q):
                told = info_got[spread_index(q, plan.leaf[which], mine[plan.leaf[which]])]
                picks[which, q] = jnp.concatenate(
                    [
                        jnp.where(told[k : k + 1, :] == row, 1.0, 0.0)
                        for k in (0, 1, 2 + 2 * which, 3 + 2 * which)
                    ],
                    axis=0,
                ).astype(jnp.bfloat16)

    def pick(which, j):
        for copy in weight_copies(j):
            copy.start()
        for r in range(2):
            send(which, plan.stages - 1, r, j).wait()

        @pl.when(j == 0)
        def _():
            read_info()

        @pl.loop(0, side, unroll=4)
        def _(q):
            there = held[(j,) + tuple(digits(q, plan.stages))]
            taken = jnp.dot(picks[which, q], there, preferred_element_type=jnp.float32)
            taken = taken.astype(jnp.bfloat16)
            keep[j % 3, q] = taken[:room]
            for k in range(3):
                give[j % 3, k, q] = taken[(k + 1) * room : (k + 2) * room]

        for copy in last_copies(which, j):
            copy.start()

    def multiply(which, j):
        for copy in last_copies(which, j):
            copy.wait()
        for copy in weight_copies(j):
            copy.wait()
        bit = plan.leaf[which]
        places = [
            pl.ds(pl.multiple_of(owner * half + j * wide, wide), wide) for owner in (seg, 1 - seg)
        ]
        factors = [[gains[pl.ds(section, 1), place] for place in places] for section in range(2)]

        @pl.loop(0, side, unroll=2)
        def _(q):
            for own, sources in (
                (mine[bit], (keep.at[j % 3, q], got.at[j, 0, q])),
                (1 - mine[bit], (got.at[j, 1, q], got.at[j, 2, q])),
            ):
                base = spread_index(q, bit, own) * room
                factor = scale[pl.ds(pl.multiple_of(base, room), room), :]
                for f, source in enumerate(sources):
                    scaled = source[...].astype(jnp.float32) * factor
                    for section in range(2):
                        to = pl.ds(pl.multiple_of(section * slot_rows + base, room), room)
                        lhs[to, pl.ds(f * wide, wide)] = (scaled * factors[section][f]).astype(
                            jnp.bfloat16
                        )

        for section in range(2):
            rows = pl.ds(section * slot_rows, slot_rows)
            hid[rows, :] += jnp.dot(
                lhs[rows, :], w_buf[j % 3], preferred_element_type=jnp.float32
            )

    tile = math.gcd(slot_rows, 256)

    def clear():
        @pl.loop(0, 2 * slot_rows // tile)
        def _(r):
            rows = pl.ds(pl.multiple_of(r * tile, tile), tile)
            hid[rows, :] = jnp.zeros((tile, 2 * units), jnp.float32)

    @pl.loop(1, blocks)
    def _(k):
        tell(k).start()

    steps = [(0, by_parity(first_send))]
    for t in range(1, plan.stages):
        steps.append((t, by_parity(functools.partial(relay, t))))
    steps += [(plan.stages, by_parity(pick)), (plan.stages + 2, by_parity(multiply))]
    run_stages(chunks, steps, clear)

    @pl.loop(0, 2 * slot_rows // tile)
    def _(r):
        rows = pl.ds(pl.multiple_of(r * tile, tile), tile)
        gate = hid[rows, :units]
        act[rows, :] = (gate / (1.0 + jnp.exp(-gate)) * hid[rows, units:]).astype(jnp.bfloat16)


def gather_call(plan, room, x, info, gains, w_in):
    blocks = plan.blocks
    side = blocks // 2
    tok_rows, half = x.shape
    wide = LANES
    chunks = half // wide
    slot_rows = blocks * room
    units = w_in.shape[1] // 2

    def bf(*shape):
        return pltpu.VMEM(shape, jnp.bfloat16)

    def f32(*shape):
        return pltpu.VMEM(shape, jnp.float32)

    def dma(*shape):
        return pltpu.SemaphoreType.DMA(shape)

    scratch = [
        bf(chunks, *((2,) * plan.stages), tok_rows, wide),
        f32(*info.shape),
        bf(2, side, 4 * room, tok_rows),
        f32(slot_rows, wide),
        bf(3, side, room, wide),
        bf(3, 3, side, room, wide),
        bf(chunks, 3, side, room, wide),
        bf(2 * slot_rows, 2 * wide),
        f32(2 * slot_rows, 2 * units),
        bf(3, 2 * wide, 2 * units),
    ]
    sems = [dma(blocks - 1), dma(blocks - 1), dma(3, 3), dma(chunks, 3), dma(3, 2), dma(1)]
    for _ in range(plan.stages):
        sems += [dma(2, 2), dma(chunks, 2)]
    vmem = pl.BlockSpec(memory_space=pltpu.VMEM)
    return pl.pallas_call(
        functools.partial(gather_kernel, plan, chunks),
        out_shape=(
            jax.ShapeDtypeStruct((2 * slot_rows, units), jnp.bfloat16),
            jax.ShapeDtypeStruct(info.shape, jnp.float32),
        ),
        in_specs=[vmem, vmem, vmem, pl.BlockSpec(memory_space=pl.ANY)],
        out_specs=(vmem, vmem),
        scratch_shapes=scratch + sems,
        compiler_params=pltpu.CompilerParams(
            collective_id=1, has_side_effects=True, vmem_limit_bytes=VMEM_LIMIT
        ),
        name="gather_hidden",
    )(x, info, gains, w_in)


def swap_cores(x):
    count = lax.axis_size("segment")
    return lax.ppermute(x, "segment", [(i, count - 1 - i) for i in range(count)])


def inverse_rms(values):
    return lax.rsqrt(jnp.mean(values * values, axis=-1, keepdims=True) + 1e-06)


def per_device(
    rollout,
    norm_gain,
    router_first,
    gain_second,
    router_second,
    expert_ids,
    copy_pick,
    later_ids,
    slot_table,
    expert_in,
    expert_out,
):
    position = lax.axis_index("segment")
    segment_count = lax.axis_size("segment")
    chip_count = lax.axis_size("expert")
    tok_rows, half = rollout.shape
    top_count = expert_ids.shape[1]
    experts_all = router_first.shape[2]
    slot_count = slot_table.shape[0]
    capacity = 3 * tok_rows * top_count // (2 * segment_count * chip_count)

    expert_cols = jnp.arange(experts_all, dtype=jnp.int32)
    slot_ids = jnp.arange(slot_count, dtype=jnp.int32)
    same = slot_table[:, None] == slot_table[None, :]
    earlier = slot_ids[:, None] < slot_ids[None, :]
    copy_rank = jnp.sum((same & earlier).astype(jnp.int32), axis=0)
    slot_holders = jnp.sum(same.astype(jnp.int32), axis=0)
    here = slot_table == expert_ids[..., None]
    copies = jnp.max(jnp.where(here, slot_holders, 1), axis=-1)
    wanted = copy_pick % copies
    match = here & (copy_rank == wanted[..., None])
    hit = jnp.sum(match.astype(jnp.bfloat16), axis=1)
    order = jnp.arange(tok_rows, dtype=jnp.int32)
    before_mask = (order[None, :] < order[:, None]).astype(jnp.bfloat16)
    before = jnp.dot(before_mask, hit, preferred_element_type=jnp.float32).astype(jnp.int32)
    other_half = swap_cores(rollout)
    first = position == 0
    left = jnp.where(first, rollout, other_half)
    right = jnp.where(first, other_half, rollout)
    whole = jnp.concatenate([left, right], axis=1)
    states_in = whole.astype(jnp.float32)
    factor = inverse_rms(states_in)
    normed = (states_in * factor * norm_gain[0].astype(jnp.float32)).astype(
        jnp.bfloat16
    )
    logits = jnp.dot(normed, router_first[0], preferred_element_type=jnp.float32)
    picked = expert_ids[..., None] == expert_cols
    chosen = jnp.sum(jnp.where(picked, logits[:, None, :], 0.0), axis=-1)
    lifted = jnp.exp(chosen - jnp.max(chosen, axis=1, keepdims=True))
    gates = (lifted / jnp.sum(lifted, axis=1, keepdims=True)).astype(jnp.bfloat16)
    place = jnp.where((hit > 0) & (before < capacity), before, -1).astype(jnp.float32)
    gate = jnp.sum(jnp.where(match, gates.astype(jnp.float32)[..., None], 0.0), axis=1)

    plan = Plan(grid_sides(chip_count))

    def by_core(values):
        cores = values.T.reshape(segment_count, chip_count, tok_rows)
        own = jnp.where(first, cores[0], cores[1])
        other = jnp.where(first, cores[1], cores[0])
        rows = [own, other]
        for bit in plan.leaf:
            for core in (own, other):
                paired = core.reshape(-1, 2, 1 << bit, tok_rows)
                rows.append(paired[:, ::-1].reshape(chip_count, tok_rows))
        return rows

    factors = jnp.broadcast_to(factor[:, 0], (chip_count, tok_rows))
    blank = jnp.zeros((chip_count, tok_rows), jnp.float32)
    info = jnp.stack(by_core(place) + by_core(gate) + [factors, blank, blank, blank], axis=1)
    gains = jnp.concatenate([swap_cores(norm_gain), norm_gain], axis=0).astype(jnp.float32)
    room = -(-capacity // 16) * 16
    active, told = gather_call(plan, room, rollout, info, gains, expert_in[0])
    summed = return_call(plan, room, active, expert_out[0], told)
    mixed = states_in + summed
    later = (mixed * inverse_rms(mixed) * gain_second[0].astype(jnp.float32)).astype(jnp.bfloat16)
    logp = jax.nn.log_softmax(
        jnp.dot(later, router_second[0], preferred_element_type=jnp.float32), axis=-1
    )
    later_pick = later_ids[..., None] == expert_cols
    score = jnp.sum(jnp.where(later_pick, logp[:, None, :], 0.0), axis=(1, 2))
    partner = swap_cores(score)
    ratio = jnp.where(position == 1, score - partner, partner - score)
    paired = ratio.reshape(tok_rows // 2, 2)
    column = lax.dynamic_slice_in_dim(paired, position, 1, 1)
    return (mixed.astype(jnp.bfloat16)[None], column)


def solution(mesh):
    in_specs = (
        P("expert", "segment"),
        P("segment", None),
        P("segment", None, None),
        P("segment", None),
        P("segment", None, None),
        P("expert", None),
        P("expert", None),
        P("expert", None),
        P(),
        P(("segment", "expert"), None, None),
        P(("segment", "expert"), None, None),
    )
    out_specs = (P("segment", "expert", None), P("expert", "segment"))
    return jax.shard_map(
        per_device, mesh=mesh, in_specs=in_specs, out_specs=out_specs, check_vma=False
    )
```

```python
import functools
import math

import jax
import jax.numpy as jnp
from jax import lax
from jax.experimental import pallas as pl
from jax.experimental.pallas import tpu as pltpu
from jax.sharding import PartitionSpec as P

LANES = 128
VMEM_BUDGET = 26 << 20
VMEM_LIMIT = 60 * 1024 * 1024
VMEM_MOST = 67043328
VMEM_SPARE = 4 << 20
MESH = pl.DeviceIdType.MESH
INFO_ROWS = 16
FACTOR_ROW = 12
EPS = 1e-06


def grid_sides(count):
    outer = 1
    while outer**3 < count:
        outer *= 2
    rest = count // outer
    middle = 1
    while middle**2 < rest:
        middle *= 2
    return outer, middle, rest // middle


class Plan:
    def __init__(self, sides):
        logs = [side.bit_length() - 1 for side in sides]
        n_a, n_b, n_c = logs
        bits_c = list(range(n_c))
        bits_b = list(range(n_c, n_c + n_b))
        bits_a = list(range(n_c + n_b, n_c + n_b + n_a))
        self.count = n_a + n_b + n_c
        self.blocks = 1 << self.count
        self.leaf = (bits_c[0], bits_b[0])
        orders = (
            (bits_c + bits_a + bits_b, bits_c + bits_b + bits_a),
            (bits_b + bits_a + bits_c, bits_b + bits_c + bits_a),
        )
        self.rest = [[order[1:] for order in pair] for pair in orders]
        self.stages = self.count - 1

    def split(self, rows):
        part = max(3 * rows // 8 // 16 * 16, 16)
        return part, rows - part

    def dims(self, which, order, done):
        used = [self.leaf[which]] + self.rest[which][order][:done]
        return [bit for bit in reversed(range(self.count)) if bit not in used]


def bit_of(index, bit):
    return (index // (1 << bit)) % 2


def flip(index, bit):
    return index + (1 << bit) * (1 - 2 * bit_of(index, bit))


def digits(value, count):
    return [(value // (1 << (count - 1 - i))) % 2 for i in range(count)]


def spread_index(value, bit, own):
    low = 1 << bit
    return (value // low) * (2 * low) + own * low + value % low


def remote(src, dst, send, recv, peer):
    return pltpu.make_async_remote_copy(
        src_ref=src,
        dst_ref=dst,
        send_sem=send,
        recv_sem=recv,
        device_id=peer,
        device_id_type=MESH,
    )


def run_stages(chunks, stages, hooks):
    depth = max(lag for lag, _ in stages)

    @pl.loop(0, chunks + depth)
    def _(step):
        for lag, stage in stages:

            @pl.when((step >= lag) & (step - lag < chunks))
            def _():
                stage(step - lag)

        for when, hook in hooks.items():

            @pl.when(step == when)
            def _():
                hook()


def by_parity(stage):
    def run(j):
        for which in range(2):

            @pl.when(j % 2 == which)
            def _():
                stage(which, j)

    return run


def meet(plan, seg, me, friends, everyone):
    barrier = pltpu.get_barrier_semaphore()
    for friend in friends:
        pl.semaphore_signal(barrier, inc=1, device_id=friend, device_id_type=MESH)
    if everyone:

        @pl.loop(1, plan.blocks)
        def _(k):
            pl.semaphore_signal(
                barrier, inc=1, device_id=(seg, (me + k) % plan.blocks), device_id_type=MESH
            )

    pl.semaphore_wait(barrier, len(friends) + (plan.blocks - 1 if everyone else 0))


def cross_friends(plan, seg, me):
    return [(1 - seg, me)] + [(1 - seg, flip(me, bit)) for bit in plan.leaf]


def make_weights(plan, seg, me, room, told, wts):
    tok_rows = told.shape[-1]
    row = lax.broadcasted_iota(jnp.int32, (room, tok_rows), 0).astype(jnp.float32)
    for which in range(2):
        bit = plan.leaf[which]

        @pl.loop(0, plan.blocks // 2)
        def _(q):
            info = told[spread_index(q, bit, bit_of(me, bit))]
            pieces = []
            for k in (0, 1, 2 + 2 * which, 3 + 2 * which):
                hit = info[k : k + 1, :] == row
                pieces.append(jnp.where(hit, info[6 + k : 7 + k, :], 0.0))
            pad = -(4 * room) % LANES
            if pad:
                pieces.append(jnp.zeros((pad, tok_rows), jnp.float32))
            turned = jnp.concatenate(pieces, axis=0).T
            wts[which, q] = turned[:, : 4 * room].astype(jnp.bfloat16)


def return_scratch(plan, room, tok_rows, chunks):
    def bf(*shape):
        return pltpu.VMEM(shape, jnp.bfloat16)

    def dma(*shape):
        return pltpu.SemaphoreType.DMA(shape)

    side = plan.blocks // 2
    low = (2,) * plan.stages
    split = plan.split(tok_rows)
    scratch = [
        bf(2, side, tok_rows, 4 * room),
        bf(2, 2, 2, *((2,) * plan.count), room, LANES),
        bf(chunks, 2, 2, *low, room, LANES),
        bf(chunks, 2, *low, room, LANES),
        bf(2, 2, *low, tok_rows, LANES),
    ]
    sems = [dma(2, 2, 3), dma(chunks, 2, 3)]
    for t in range(plan.stages):
        for rows in split:
            left = (2,) * (plan.stages - 1 - t)
            scratch.append(bf(chunks, 2, *left, rows, LANES))
            if t + 1 < plan.stages:
                scratch.append(bf(2, 2, *left, rows, LANES))
        sems += [dma(2, 2, 2), dma(chunks, 2, 2)]
    return scratch, sems


def return_steps(plan, seg, me, act, w_out, finish, scratch, sems):
    wts, ys, leaf, swapped, first = scratch[:5]
    more = list(scratch[5:])
    stages = plan.stages
    arrived, parts = [], []
    for t in range(stages):
        arrived.append([])
        parts.append([])
        for _ in range(2):
            arrived[t].append(more.pop(0))
            if t + 1 < stages:
                parts[t].append(more.pop(0))
    side = plan.blocks // 2
    room = ys.shape[-2]
    slot_rows = plan.blocks * room
    tok_rows = first.shape[-2]
    split = plan.split(tok_rows)
    spans = (pl.ds(0, split[0]), pl.ds(split[0], split[1]))
    mine = [bit_of(me, bit) for bit in range(plan.count)]

    def region(which, own):
        bit = plan.leaf[which]
        place = plan.count - 1 - bit
        return tuple(
            (mine[bit] if own else 1 - mine[bit]) if i == place else slice(None)
            for i in range(plan.count)
        )

    def first_copies(which, j):
        nbr = flip(me, plan.leaf[which])
        sources = (
            (ys.at[(j % 2, which, 1) + region(which, False)], leaf.at[j, which, 0], (seg, nbr)),
            (ys.at[(j % 2, which, 0) + region(which, False)], leaf.at[j, which, 1], (1 - seg, nbr)),
            (ys.at[(j % 2, which, 0) + region(which, True)], swapped.at[j, which], (1 - seg, me)),
        )
        return [
            remote(src, dst, sems[0].at[j % 2, which, k], sems[1].at[j, which, k], peer)
            for k, (src, dst, peer) in enumerate(sources)
        ]

    def held_at(which, t, r, j, index):
        if t == 0:
            return (j % 2, which) + index + (spans[r],)
        return (j % 2, which) + index

    def send(which, t, r, j):
        bit = plan.rest[which][r][t]
        dims = plan.dims(which, r, t)
        index = tuple(1 - mine[d] if d == bit else slice(None) for d in dims)
        source = first if t == 0 else parts[t - 1][r]
        return remote(
            source.at[held_at(which, t, r, j, index)],
            arrived[t][r].at[j, which],
            sems[2 + 2 * t].at[j % 2, which, r],
            sems[3 + 2 * t].at[j, which, r],
            (seg, flip(me, bit)),
        )

    def project(j):
        wide = 2 * LANES
        columns = pl.ds(pl.multiple_of(j * wide, wide), wide)
        blocks = (2,) * plan.count
        for section in range(2):
            result = jnp.dot(
                act[pl.ds(section * slot_rows, slot_rows), :],
                w_out[:, columns],
                preferred_element_type=jnp.float32,
            ).astype(jnp.bfloat16)
            for which in range(2):
                half = result[:, which * LANES : (which + 1) * LANES]
                ys[j % 2, which, section] = half.reshape(blocks + (room, LANES))
        for which in range(2):
            for copy in first_copies(which, j):
                copy.start()

    def combine(j):
        for which in range(2):
            for copy in first_copies(which, j):
                copy.wait()
            own = mine[plan.leaf[which]]
            place = plan.count - 1 - plan.leaf[which]

            @pl.loop(0, side, unroll=8)
            def _(q):
                ix = digits(q, stages)
                full = tuple(ix[:place] + [own] + ix[place:])
                ix = tuple(ix)
                both = jnp.concatenate(
                    [
                        ys[(j % 2, which, 1) + full],
                        swapped[(j, which) + ix],
                        leaf[(j, which, 0) + ix],
                        leaf[(j, which, 1) + ix],
                    ],
                    axis=0,
                )
                part = jnp.dot(wts[which, q], both, preferred_element_type=jnp.float32)
                first[(j % 2, which) + ix] = part.astype(jnp.bfloat16)

            for r in range(2):
                send(which, 0, r, j).start()

    def reduce_stage(t, j):
        last = t == stages - 1
        left = stages - 1 - t
        for which in range(2):
            for r in range(2):
                send(which, t, r, j).wait()
                bit = plan.rest[which][r][t]
                place = plan.dims(which, r, t).index(bit)
                source = first if t == 0 else parts[t - 1][r]

                def total(ix):
                    full = tuple(ix[:place] + [mine[bit]] + ix[place:])
                    held = source[held_at(which, t, r, j, full)]
                    came = arrived[t][r][(j, which) + tuple(ix)]
                    return held.astype(jnp.float32) + came.astype(jnp.float32)

                if last:
                    start = pl.multiple_of((2 * j + which) * LANES, LANES)
                    finish(spans[r], pl.ds(start, LANES), total([]))
                else:

                    @pl.loop(0, 1 << left, unroll=2)
                    def _(e):
                        ix = digits(e, left)
                        parts[t][r][(j % 2, which) + tuple(ix)] = total(ix).astype(jnp.bfloat16)

                    send(which, t + 1, r, j).start()

    steps = [(0, project), (1, combine)]
    for t in range(stages):
        steps.append((2 + t, functools.partial(reduce_stage, t)))
    return steps


def return_kernel(plan, chunks, act, w_out, told, out, *rest):
    count = 5 + 4 * plan.stages - 2
    scratch, sems = rest[:count], rest[count:]
    seg = lax.axis_index("segment")
    me = lax.axis_index("expert")
    friends = cross_friends(plan, seg, me)
    meet(plan, seg, me, friends + [(seg, flip(me, bit)) for bit in range(plan.count)], False)

    def finish(rows, columns, total):
        out[rows, columns] = total

    def weights():
        make_weights(plan, seg, me, scratch[1].shape[-2], told, scratch[0])

    steps = return_steps(plan, seg, me, act, w_out, finish, scratch, sems)
    run_stages(chunks, steps, {0: weights})


def return_call(plan, room, act, w_out, told):
    tok_rows = told.shape[2]
    wide = 2 * LANES
    side = plan.blocks // 2
    chunk_bytes = (
        2 * wide * (3 * side * room + sum(side >> t for t in range(1, plan.count)) * tok_rows)
    )
    chunks = w_out.shape[1] // wide
    while chunks % 2 == 0 and chunks * chunk_bytes > VMEM_BUDGET:
        chunks //= 2
    scratch, sems = return_scratch(plan, room, tok_rows, chunks)
    piece = chunks * wide
    call = pl.pallas_call(
        functools.partial(return_kernel, plan, chunks),
        out_shape=jax.ShapeDtypeStruct((tok_rows, piece), jnp.float32),
        in_specs=[pl.BlockSpec(memory_space=pltpu.VMEM)] * 3,
        out_specs=pl.BlockSpec(memory_space=pltpu.VMEM),
        scratch_shapes=scratch + sems,
        compiler_params=pltpu.CompilerParams(
            collective_id=0, has_side_effects=True, vmem_limit_bytes=VMEM_LIMIT
        ),
        name="return_sum",
    )
    pieces = [
        call(act, w_out[:, start : start + piece], told)
        for start in range(0, w_out.shape[1], piece)
    ]
    return pieces[0] if len(pieces) == 1 else jnp.concatenate(pieces, axis=1)


def gather_scratch(plan, room, tok_rows, chunks, units):
    def bf(*shape):
        return pltpu.VMEM(shape, jnp.bfloat16)

    def f32(*shape):
        return pltpu.VMEM(shape, jnp.float32)

    def dma(*shape):
        return pltpu.SemaphoreType.DMA(shape)

    blocks = plan.blocks
    side = blocks // 2
    slot_rows = blocks * room
    scratch = [
        bf(chunks, *((2,) * plan.stages), tok_rows, LANES),
        f32(blocks, INFO_ROWS, tok_rows),
        bf(2, side, 4 * room, tok_rows),
        f32(slot_rows, LANES),
        bf(3, side, room, LANES),
        bf(3, 3, side, room, LANES),
        bf(chunks, 3, side, room, LANES),
        bf(2 * slot_rows, 2 * LANES),
        f32(2 * slot_rows, 2 * units),
        bf(3, 2 * LANES, 2 * units),
    ]
    sems = [dma(blocks - 1), dma(blocks - 1), dma(3, 3), dma(chunks, 3), dma(3, 2)]
    for _ in range(plan.stages):
        sems += [dma(chunks, 2), dma(chunks, 2)]
    return scratch, sems


def gather_steps(plan, seg, me, x, info, gains, w_in, act, info_out, scratch, sems):
    (held, info_got, picks, scale, keep, give, got, lhs, hid, w_buf) = scratch
    blocks = plan.blocks
    side = blocks // 2
    mine = [bit_of(me, bit) for bit in range(plan.count)]
    tok_rows, half = x.shape
    half_rows = tok_rows // 2
    wide = LANES
    room = keep.shape[-2]
    slot_rows = blocks * room
    units = act.shape[1]
    tile = math.gcd(slot_rows, 256)

    def tell(k):
        to = (me + k) % blocks
        return remote(
            info.at[to], info_got.at[me], sems[0].at[k - 1], sems[1].at[k - 1], (seg, to)
        )

    def columns(j):
        return pl.ds(pl.multiple_of(j * wide, wide), wide)

    def send(which, t, r, j):
        order = plan.rest[which][r]
        bit = order[plan.stages - 1 - t]
        free = order[plan.stages - t :]
        rows = pl.ds(r * half_rows, half_rows)
        index = tuple(slice(None) if d in free else mine[d] for d in plan.dims(which, r, 0))
        dst = held.at[(j,) + index + (rows,)]
        return remote(
            x.at[rows, columns(j)] if t == 0 else dst,
            dst,
            sems[5 + 2 * t].at[j, r],
            sems[6 + 2 * t].at[j, r],
            (seg, flip(me, bit)),
        )

    def first_send(which, j):
        for r in range(2):
            send(which, 0, r, j).start()
        index = tuple(mine[d] for d in plan.dims(which, 0, 0))
        held[(j,) + index] = x[:, columns(j)]

    def relay(t, which, j):
        for r in range(2):
            send(which, t - 1, r, j).wait()
            send(which, t, r, j).start()

    def last_copies(which, j):
        nbr = flip(me, plan.leaf[which])
        peers = ((1 - seg, me), (seg, nbr), (1 - seg, nbr))
        return [
            remote(
                give.at[j % 3, k],
                got.at[j, k],
                sems[2].at[j % 3, k],
                sems[3].at[j, k],
                peer,
            )
            for k, peer in enumerate(peers)
        ]

    def weight_copies(j):
        copies = []
        for which, owner in enumerate((seg, 1 - seg)):
            rows = pl.ds(pl.multiple_of(owner * half + j * wide, wide), wide)
            copies.append(
                pltpu.make_async_copy(
                    w_in.at[rows, :],
                    w_buf.at[j % 3, pl.ds(which * wide, wide)],
                    sems[4].at[j % 3, which],
                )
            )
        return copies

    def tell_all():
        @pl.loop(1, blocks)
        def _(k):
            tell(k).start()

    def read_info():
        info_got[me] = info[me]

        @pl.loop(1, blocks)
        def _(k):
            tell(k).wait()

        row = lax.broadcasted_iota(jnp.int32, (room, tok_rows), 0).astype(jnp.float32)

        @pl.loop(0, blocks)
        def _(d):
            told = info_got[d]
            if info_out is not None:
                info_out[d] = told
            own = told[0:1, :] == row
            factor = jnp.sum(
                jnp.where(own, told[FACTOR_ROW : FACTOR_ROW + 1, :], 0.0), axis=1, keepdims=True
            )
            rows = pl.ds(pl.multiple_of(d * room, room), room)
            scale[rows, :] = jnp.broadcast_to(factor, (room, wide))

        for which in range(2):

            @pl.loop(0, side)
            def _(q):
                told = info_got[spread_index(q, plan.leaf[which], mine[plan.leaf[which]])]
                picks[which, q] = jnp.concatenate(
                    [
                        jnp.where(told[k : k + 1, :] == row, 1.0, 0.0)
                        for k in (0, 1, 2 + 2 * which, 3 + 2 * which)
                    ],
                    axis=0,
                ).astype(jnp.bfloat16)

    def pick(which, j):
        for copy in weight_copies(j):
            copy.start()
        for r in range(2):
            send(which, plan.stages - 1, r, j).wait()

        @pl.when(j == 0)
        def _():
            read_info()

        @pl.loop(0, side, unroll=4)
        def _(q):
            there = held[(j,) + tuple(digits(q, plan.stages))]
            taken = jnp.dot(picks[which, q], there, preferred_element_type=jnp.float32)
            taken = taken.astype(jnp.bfloat16)
            keep[j % 3, q] = taken[:room]
            for k in range(3):
                give[j % 3, k, q] = taken[(k + 1) * room : (k + 2) * room]

        for copy in last_copies(which, j):
            copy.start()

    def multiply(which, j):
        for copy in last_copies(which, j):
            copy.wait()
        for copy in weight_copies(j):
            copy.wait()
        bit = plan.leaf[which]
        places = [
            pl.ds(pl.multiple_of(owner * half + j * wide, wide), wide) for owner in (seg, 1 - seg)
        ]
        factors = [[gains[pl.ds(section, 1), place] for place in places] for section in range(2)]

        @pl.loop(0, side, unroll=2)
        def _(q):
            for own, sources in (
                (mine[bit], (keep.at[j % 3, q], got.at[j, 0, q])),
                (1 - mine[bit], (got.at[j, 1, q], got.at[j, 2, q])),
            ):
                base = spread_index(q, bit, own) * room
                factor = scale[pl.ds(pl.multiple_of(base, room), room), :]
                for f, source in enumerate(sources):
                    scaled = source[...].astype(jnp.float32) * factor
                    for section in range(2):
                        to = pl.ds(pl.multiple_of(section * slot_rows + base, room), room)
                        lhs[to, pl.ds(f * wide, wide)] = (scaled * factors[section][f]).astype(
                            jnp.bfloat16
                        )

        for section in range(2):
            rows = pl.ds(section * slot_rows, slot_rows)
            hid[rows, :] += jnp.dot(
                lhs[rows, :], w_buf[j % 3], preferred_element_type=jnp.float32
            )

    def clear():
        @pl.loop(0, 2 * slot_rows // tile)
        def _(r):
            rows = pl.ds(pl.multiple_of(r * tile, tile), tile)
            hid[rows, :] = jnp.zeros((tile, 2 * units), jnp.float32)

    def activate():
        @pl.loop(0, 2 * slot_rows // tile)
        def _(r):
            rows = pl.ds(pl.multiple_of(r * tile, tile), tile)
            gate = hid[rows, :units]
            act[rows, :] = (gate / (1.0 + jnp.exp(-gate)) * hid[rows, units:]).astype(jnp.bfloat16)

    steps = [(0, by_parity(first_send))]
    for t in range(1, plan.stages):
        steps.append((t, by_parity(functools.partial(relay, t))))
    steps += [(plan.stages, by_parity(pick)), (plan.stages + 2, by_parity(multiply))]
    return steps, tell_all, clear, activate


def gather_kernel(plan, chunks, x, info, gains, w_in, act, info_out, *rest):
    scratch, sems = rest[:10], rest[10:]
    seg = lax.axis_index("segment")
    me = lax.axis_index("expert")
    meet(plan, seg, me, cross_friends(plan, seg, me), True)
    steps, tell_all, clear, activate = gather_steps(
        plan, seg, me, x, info, gains, w_in, act, info_out, scratch, sems
    )
    tell_all()
    run_stages(chunks, steps, {0: clear})
    activate()


def gather_call(plan, room, x, info, gains, w_in):
    tok_rows, half = x.shape
    chunks = half // LANES
    slot_rows = plan.blocks * room
    units = w_in.shape[1] // 2
    scratch, sems = gather_scratch(plan, room, tok_rows, chunks, units)
    vmem = pl.BlockSpec(memory_space=pltpu.VMEM)
    return pl.pallas_call(
        functools.partial(gather_kernel, plan, chunks),
        out_shape=(
            jax.ShapeDtypeStruct((2 * slot_rows, units), jnp.bfloat16),
            jax.ShapeDtypeStruct(info.shape, jnp.float32),
        ),
        in_specs=[vmem, vmem, vmem, pl.BlockSpec(memory_space=pl.ANY)],
        out_specs=(vmem, vmem),
        scratch_shapes=scratch + sems,
        compiler_params=pltpu.CompilerParams(
            collective_id=1, has_side_effects=True, vmem_limit_bytes=VMEM_LIMIT
        ),
        name="gather_hidden",
    )(x, info, gains, w_in)


def column_sum(values):
    return jnp.sum(values, axis=1, keepdims=True)


def fused_kernel(plan, room, capacity, sizes, *refs):
    (x, gain, router, gain2, router2, ids, copies, later_ids, table, w_in, w_out) = refs[:11]
    states, ratio = refs[11:13]
    n_gather, n_return, n_gather_sems = sizes
    own = refs[13:25]
    (whole, gain_got, gains, slots, info, act, w_out_v, mixed, squares, normed, score, score_got) = own
    gather_refs = refs[25 : 25 + n_gather]
    return_refs = refs[25 + n_gather : 25 + n_gather + n_return]
    sems = refs[25 + n_gather + n_return :]
    swap_sems, sems = sems[:2], sems[2:]
    gather_sems, return_sems = sems[:n_gather_sems], sems[n_gather_sems:]
    seg = lax.axis_index("segment")
    me = lax.axis_index("expert")
    blocks = plan.blocks
    tok_rows, half = x.shape
    full = 2 * half
    top = ids.shape[0]
    tiles = full // LANES
    f32 = jnp.float32
    partner = (1 - seg, me)

    def tile_at(i):
        return pl.ds(pl.multiple_of(i * LANES, LANES), LANES)

    own_columns = pl.ds(pl.multiple_of(seg * half, half), half)
    swap_x = remote(x, whole.at[:, own_columns], swap_sems[0].at[0], swap_sems[1].at[0], partner)
    swap_gain = remote(gain, gain_got, swap_sems[0].at[1], swap_sems[1].at[1], partner)
    swap_score = remote(score, score_got, swap_sems[0].at[2], swap_sems[1].at[2], partner)
    load_w_out = pltpu.make_async_copy(w_out, w_out_v, swap_sems[0].at[3])

    meet(plan, seg, me, cross_friends(plan, seg, me), True)
    swap_x.start()
    swap_gain.start()
    load_w_out.start()
    steps, tell_all, clear, activate = gather_steps(
        plan, seg, me, x, info, gains, w_in, act, None, gather_refs, gather_sems
    )

    def normalize():
        total = jnp.zeros((tok_rows, LANES), f32)
        for i in range(tiles):
            part = whole[:, i * LANES : (i + 1) * LANES].astype(f32)
            total += part * part
        return lax.rsqrt(column_sum(total) / full + EPS)

    def prologue():
        whole[:, own_columns] = x[...]
        gains[1:2, :] = gain[...].astype(f32)
        swap_gain.wait()
        gains[0:1, :] = gain_got[...].astype(f32)
        swap_x.wait()
        factor = jnp.broadcast_to(normalize(), (tok_rows, LANES))
        squares[...] = factor

        @pl.loop(0, tiles)
        def _(i):
            part = whole[:, tile_at(i)].astype(f32) * squares[...]
            normed[:, tile_at(i)] = (part * gains[1:2, tile_at(i)]).astype(jnp.bfloat16)

    def route():
        slot_count = table.shape[1]
        line = table[...].astype(f32)
        i_row = lax.broadcasted_iota(jnp.int32, (slot_count, slot_count), 0)
        i_col = lax.broadcasted_iota(jnp.int32, (slot_count, slot_count), 1)
        column = column_sum(jnp.where(i_row == i_col, line, 0.0))
        same = column == line
        rank = column_sum(jnp.where(same & (i_col < i_row), 1.0, 0.0))
        holders = column_sum(jnp.where(same, 1.0, 0.0))
        wanted = ids[...].astype(f32)
        choice = copies[...].astype(f32)
        of_two = choice - 2.0 * jnp.floor(choice * 0.5)
        of_three = choice - 3.0 * jnp.floor((choice + 0.5) * (1.0 / 3.0))
        logits = lax.dot_general(
            router[...], normed[...], (((1,), (1,)), ((), ())), preferred_element_type=f32
        )
        names = lax.broadcasted_iota(jnp.int32, logits.shape, 0).astype(f32)
        matches, chosen = [], []
        for k in range(top):
            turn = jnp.where(
                holders == 1.0,
                0.0,
                jnp.where(holders == 2.0, of_two[k : k + 1, :], of_three[k : k + 1, :]),
            )
            matches.append((column == wanted[k : k + 1, :]) & (rank == turn))
            chosen.append(
                jnp.sum(
                    jnp.where(names == wanted[k : k + 1, :], logits, 0.0), axis=0, keepdims=True
                )
            )
        most = functools.reduce(jnp.maximum, chosen)
        lifted = [jnp.exp(value - most) for value in chosen]
        weight = functools.reduce(jnp.add, lifted)
        hit = jnp.zeros((slot_count, tok_rows), f32)
        gate = jnp.zeros((slot_count, tok_rows), f32)
        for k in range(top):
            rounded = (lifted[k] / weight).astype(jnp.bfloat16).astype(f32)
            hit += jnp.where(matches[k], 1.0, 0.0)
            gate += jnp.where(matches[k], rounded, 0.0)
        t_row = lax.broadcasted_iota(jnp.int32, (tok_rows, tok_rows), 0)
        t_col = lax.broadcasted_iota(jnp.int32, (tok_rows, tok_rows), 1)
        earlier = jnp.where(t_row < t_col, 1.0, 0.0).astype(jnp.bfloat16)
        before = jnp.dot(hit.astype(jnp.bfloat16), earlier, preferred_element_type=f32)
        slots[0] = jnp.where((hit > 0.0) & (before < capacity), before, -1.0)
        slots[1] = gate
        factor_row = squares[...].T[0:1, :]

        @pl.loop(0, blocks)
        def _(c):
            chips = (c, flip(c, plan.leaf[0]), flip(c, plan.leaf[1]))
            for kind in range(2):
                for n, chip in enumerate(chips):
                    for core, which in enumerate((seg, 1 - seg)):
                        info[c, 6 * kind + 2 * n + core, :] = slots[kind, which * blocks + chip, :]
            info[c, FACTOR_ROW : FACTOR_ROW + 1, :] = factor_row
            info[c, FACTOR_ROW + 1 :, :] = jnp.zeros((INFO_ROWS - FACTOR_ROW - 1, tok_rows), f32)

        tell_all()

    def weights():
        make_weights(plan, seg, me, room, gather_refs[1], return_refs[0])

    chunks = half // LANES
    run_stages(chunks, steps, {0: prologue, 1: route, 2: clear, plan.stages + 4: weights})
    activate()
    load_w_out.wait()
    squares[...] = jnp.zeros((tok_rows, LANES), f32)

    def finish(rows, columns, total):
        value = whole[rows, columns].astype(f32) + total
        mixed[rows, columns] = value
        states[rows, columns] = value.astype(jnp.bfloat16)
        squares[rows, :] += value * value

    steps = return_steps(plan, seg, me, act, w_out_v, finish, return_refs, return_sems)
    run_stages(full // (2 * LANES), steps, {})
    inverse = lax.rsqrt(column_sum(squares[...]) / full + EPS)
    squares[...] = jnp.broadcast_to(inverse, (tok_rows, LANES))

    @pl.loop(0, tiles)
    def _(i):
        part = mixed[:, tile_at(i)] * squares[...]
        normed[:, tile_at(i)] = (part * gain2[:, tile_at(i)].astype(f32)).astype(jnp.bfloat16)

    logits = lax.dot_general(
        router2[...], normed[...], (((1,), (1,)), ((), ())), preferred_element_type=f32
    )
    shifted = logits - jnp.max(logits, axis=0, keepdims=True)
    logp = shifted - jnp.log(jnp.sum(jnp.exp(shifted), axis=0, keepdims=True))
    names = lax.broadcasted_iota(jnp.int32, logits.shape, 0).astype(f32)
    wanted = later_ids[...].astype(f32)
    total = jnp.zeros((1, tok_rows), f32)
    for k in range(top):
        total += jnp.sum(jnp.where(names == wanted[k : k + 1, :], logp, 0.0), axis=0, keepdims=True)
    score[...] = jnp.broadcast_to(total, score.shape)
    swap_score.start()
    swap_score.wait()
    sign = (2 * seg - 1).astype(f32)
    difference = (score[0:1, :] - score_got[0:1, :]) * sign
    turned = jnp.broadcast_to(difference, (tok_rows, tok_rows)).T
    t_row = lax.broadcasted_iota(jnp.int32, (tok_rows, tok_rows), 0)
    t_col = lax.broadcasted_iota(jnp.int32, (tok_rows, tok_rows), 1)
    picked = jnp.sum(jnp.where(t_row == 2 * t_col + seg, turned, 0.0), axis=0, keepdims=True)
    ratio[...] = picked[:, : tok_rows // 2]


def fused_scratch(plan, room, tok_rows, half, slot_count, units):
    chunks = half // LANES
    full = 2 * half
    rows = 2 * plan.blocks * room
    own = [
        pltpu.VMEM((tok_rows, full), jnp.bfloat16),
        pltpu.VMEM((1, full), jnp.bfloat16),
        pltpu.VMEM((2, full), jnp.float32),
        pltpu.VMEM((2, slot_count, tok_rows), jnp.float32),
        pltpu.VMEM((plan.blocks, INFO_ROWS, tok_rows), jnp.float32),
        pltpu.VMEM((rows, units), jnp.bfloat16),
        pltpu.VMEM((units, full), jnp.bfloat16),
        pltpu.VMEM((tok_rows, full), jnp.float32),
        pltpu.VMEM((tok_rows, LANES), jnp.float32),
        pltpu.VMEM((tok_rows, full), jnp.bfloat16),
        pltpu.VMEM((8, tok_rows), jnp.float32),
        pltpu.VMEM((8, tok_rows), jnp.float32),
    ]
    gather, gather_sems = gather_scratch(plan, room, tok_rows, chunks, units)
    back, back_sems = return_scratch(plan, room, tok_rows, full // (2 * LANES))
    swap = [pltpu.SemaphoreType.DMA((4,)), pltpu.SemaphoreType.DMA((3,))]
    sizes = (len(gather), len(back), len(gather_sems))
    return own + gather + back, swap + gather_sems + back_sems, sizes


def held_bytes(scratch):
    total = 0
    for ref in scratch:
        *outer, rows, lanes = ref.shape
        size = jnp.dtype(ref.dtype).itemsize
        pack = 32 // size
        total += math.prod(outer) * -(-rows // pack) * pack * -(-lanes // LANES) * LANES * size
    return total


def fused_call(plan, room, capacity, scratch, sems, sizes, *args):
    tok_rows, half = args[0].shape
    vmem = pl.BlockSpec(memory_space=pltpu.VMEM)
    anywhere = pl.BlockSpec(memory_space=pl.ANY)
    return pl.pallas_call(
        functools.partial(fused_kernel, plan, room, capacity, sizes),
        out_shape=(
            jax.ShapeDtypeStruct((tok_rows, 2 * half), jnp.bfloat16),
            jax.ShapeDtypeStruct((1, tok_rows // 2), jnp.float32),
        ),
        in_specs=[vmem] * 9 + [anywhere] * 2,
        out_specs=(vmem, vmem),
        scratch_shapes=scratch + sems,
        compiler_params=pltpu.CompilerParams(
            collective_id=2, has_side_effects=True, vmem_limit_bytes=VMEM_MOST
        ),
        name="fused_layer",
    )(*args)


def swap_cores(x):
    count = lax.axis_size("segment")
    return lax.ppermute(x, "segment", [(i, count - 1 - i) for i in range(count)])


def inverse_rms(values):
    return lax.rsqrt(jnp.mean(values * values, axis=-1, keepdims=True) + 1e-06)


def per_device(
    rollout,
    norm_gain,
    router_first,
    gain_second,
    router_second,
    expert_ids,
    copy_pick,
    later_ids,
    slot_table,
    expert_in,
    expert_out,
):
    position = lax.axis_index("segment")
    segment_count = lax.axis_size("segment")
    chip_count = lax.axis_size("expert")
    tok_rows, half = rollout.shape
    top_count = expert_ids.shape[1]
    experts_all = router_first.shape[2]
    slot_count = slot_table.shape[0]
    capacity = 3 * tok_rows * top_count // (2 * segment_count * chip_count)

    plan = Plan(grid_sides(chip_count))
    room = -(-capacity // 16) * 16
    units = expert_out.shape[1]
    scratch, sems, sizes = fused_scratch(plan, room, tok_rows, half, slot_count, units)
    if held_bytes(scratch) + VMEM_SPARE < VMEM_MOST:
        states, column = fused_call(
            plan,
            room,
            capacity,
            scratch,
            sems,
            sizes,
            rollout,
            norm_gain,
            router_first[0].T,
            gain_second,
            router_second[0].T,
            expert_ids.T,
            copy_pick.T,
            later_ids.T,
            slot_table[None, :],
            expert_in[0],
            expert_out[0],
        )
        return states[None], column.reshape(-1, 1)

    expert_cols = jnp.arange(experts_all, dtype=jnp.int32)
    slot_ids = jnp.arange(slot_count, dtype=jnp.int32)
    same = slot_table[:, None] == slot_table[None, :]
    earlier = slot_ids[:, None] < slot_ids[None, :]
    copy_rank = jnp.sum((same & earlier).astype(jnp.int32), axis=0)
    slot_holders = jnp.sum(same.astype(jnp.int32), axis=0)
    here = slot_table == expert_ids[..., None]
    copies = jnp.max(jnp.where(here, slot_holders, 1), axis=-1)
    wanted = copy_pick % copies
    match = here & (copy_rank == wanted[..., None])
    hit = jnp.sum(match.astype(jnp.bfloat16), axis=1)
    order = jnp.arange(tok_rows, dtype=jnp.int32)
    before_mask = (order[None, :] < order[:, None]).astype(jnp.bfloat16)
    before = jnp.dot(before_mask, hit, preferred_element_type=jnp.float32).astype(jnp.int32)
    other_half = swap_cores(rollout)
    first = position == 0
    left = jnp.where(first, rollout, other_half)
    right = jnp.where(first, other_half, rollout)
    whole = jnp.concatenate([left, right], axis=1)
    states_in = whole.astype(jnp.float32)
    factor = inverse_rms(states_in)
    normed = (states_in * factor * norm_gain[0].astype(jnp.float32)).astype(
        jnp.bfloat16
    )
    logits = jnp.dot(normed, router_first[0], preferred_element_type=jnp.float32)
    picked = expert_ids[..., None] == expert_cols
    chosen = jnp.sum(jnp.where(picked, logits[:, None, :], 0.0), axis=-1)
    lifted = jnp.exp(chosen - jnp.max(chosen, axis=1, keepdims=True))
    gates = (lifted / jnp.sum(lifted, axis=1, keepdims=True)).astype(jnp.bfloat16)
    place = jnp.where((hit > 0) & (before < capacity), before, -1).astype(jnp.float32)
    gate = jnp.sum(jnp.where(match, gates.astype(jnp.float32)[..., None], 0.0), axis=1)

    def by_core(values):
        cores = values.T.reshape(segment_count, chip_count, tok_rows)
        own = jnp.where(first, cores[0], cores[1])
        other = jnp.where(first, cores[1], cores[0])
        rows = [own, other]
        for bit in plan.leaf:
            for core in (own, other):
                paired = core.reshape(-1, 2, 1 << bit, tok_rows)
                rows.append(paired[:, ::-1].reshape(chip_count, tok_rows))
        return rows

    factors = jnp.broadcast_to(factor[:, 0], (chip_count, tok_rows))
    blank = jnp.zeros((chip_count, tok_rows), jnp.float32)
    info = jnp.stack(by_core(place) + by_core(gate) + [factors, blank, blank, blank], axis=1)
    gains = jnp.concatenate([swap_cores(norm_gain), norm_gain], axis=0).astype(jnp.float32)
    active, told = gather_call(plan, room, rollout, info, gains, expert_in[0])
    summed = return_call(plan, room, active, expert_out[0], told)
    mixed = states_in + summed
    later = (mixed * inverse_rms(mixed) * gain_second[0].astype(jnp.float32)).astype(jnp.bfloat16)
    logp = jax.nn.log_softmax(
        jnp.dot(later, router_second[0], preferred_element_type=jnp.float32), axis=-1
    )
    later_pick = later_ids[..., None] == expert_cols
    score = jnp.sum(jnp.where(later_pick, logp[:, None, :], 0.0), axis=(1, 2))
    partner = swap_cores(score)
    ratio = jnp.where(position == 1, score - partner, partner - score)
    paired = ratio.reshape(tok_rows // 2, 2)
    column = lax.dynamic_slice_in_dim(paired, position, 1, 1)
    return (mixed.astype(jnp.bfloat16)[None], column)


def solution(mesh):
    in_specs = (
        P("expert", "segment"),
        P("segment", None),
        P("segment", None, None),
        P("segment", None),
        P("segment", None, None),
        P("expert", None),
        P("expert", None),
        P("expert", None),
        P(),
        P(("segment", "expert"), None, None),
        P(("segment", "expert"), None, None),
    )
    out_specs = (P("segment", "expert", None), P("expert", "segment"))
    return jax.shard_map(
        per_device, mesh=mesh, in_specs=in_specs, out_specs=out_specs, check_vma=False
    )
```

```python
import functools
import math

import jax
import jax.numpy as jnp
from jax import lax
from jax.experimental import pallas as pl
from jax.experimental.pallas import tpu as pltpu
from jax.sharding import PartitionSpec as P

LANES = 128
VMEM_MOST = 67043328
MESH = pl.DeviceIdType.MESH
EPS = 1e-06
RING = 4
LONG_RING = 8
EXTRA_ROWS = 16
NEAR_SLOTS = 6
FACTOR_ROW = 6


def grid_sides(count):
    outer = 1
    while outer**3 < count:
        outer *= 2
    rest = count // outer
    middle = 1
    while middle**2 < rest:
        middle *= 2
    return outer, middle, rest // middle


class Plan:
    def __init__(self, sides):
        logs = [side.bit_length() - 1 for side in sides]
        n_a, n_b, n_c = logs
        bits_c = list(range(n_c))
        bits_b = list(range(n_c, n_c + n_b))
        bits_a = list(range(n_c + n_b, n_c + n_b + n_a))
        self.count = n_a + n_b + n_c
        self.blocks = 1 << self.count
        self.leaf = (bits_c[0], bits_b[0])
        orders = (
            (bits_c + bits_a + bits_b, bits_c + bits_b + bits_a),
            (bits_b + bits_a + bits_c, bits_b + bits_c + bits_a),
        )
        self.rest = [[order[1:] for order in pair] for pair in orders]
        self.stages = self.count - 1

    def split(self, rows):
        part = max(3 * rows // 8 // 16 * 16, 16)
        return part, rows - part

    def dims(self, which, order, done):
        used = [self.leaf[which]] + self.rest[which][order][:done]
        return [bit for bit in reversed(range(self.count)) if bit not in used]


def bit_of(index, bit):
    return (index // (1 << bit)) % 2


def flip(index, bit):
    return index + (1 << bit) * (1 - 2 * bit_of(index, bit))


def digits(value, count):
    return [(value // (1 << (count - 1 - i))) % 2 for i in range(count)]


def spread_index(value, bit, own):
    low = 1 << bit
    return (value // low) * (2 * low) + own * low + value % low


def remote(src, dst, send, recv, peer):
    return pltpu.make_async_remote_copy(
        src_ref=src,
        dst_ref=dst,
        send_sem=send,
        recv_sem=recv,
        device_id=peer,
        device_id_type=MESH,
    )


def run_stages(chunks, stages, early, late):
    depth = max(lag for lag, _ in stages)

    @pl.loop(0, chunks + depth)
    def _(step):
        for lag, stage in stages:
            if lag in early:

                @pl.when(step == lag)
                def _():
                    early[lag]()

            @pl.when((step >= lag) & (step - lag < chunks))
            def _():
                stage(step - lag)

        for when, hook in late.items():

            @pl.when(step == when)
            def _():
                hook()


def by_parity(stage):
    def run(j):
        for which in range(2):

            @pl.when(j % 2 == which)
            def _():
                stage(which, j)

    return run


def near_friends(plan, seg, me):
    friends = [(1 - seg, me)] + [(seg, flip(me, bit)) for bit in range(plan.count)]
    return friends + [(1 - seg, flip(me, bit)) for bit in plan.leaf]


def slots_of(plan, seg, me):
    chips = [me] + [flip(me, bit) for bit in plan.leaf]
    return [core * plan.blocks + chip for chip in chips for core in (seg, 1 - seg)]


def rows_of(which):
    return (0, 1, 2 + 2 * which, 3 + 2 * which)


def make_weights(plan, me, room, places, gates, wts):
    tok_rows = places.shape[-1]
    row = lax.broadcasted_iota(jnp.int32, (room, tok_rows), 0).astype(jnp.float32)
    for which in range(2):
        bit = plan.leaf[which]

        @pl.loop(0, plan.blocks // 2)
        def _(q):
            d = spread_index(q, bit, bit_of(me, bit))
            place, gate = places[d], gates[d]
            pieces = []
            for k in rows_of(which):
                hit = place[k : k + 1, :] == row
                pieces.append(jnp.where(hit, gate[k : k + 1, :], 0.0))
            pad = -(4 * room) % LANES
            if pad:
                pieces.append(jnp.zeros((pad, tok_rows), jnp.float32))
            turned = jnp.concatenate(pieces, axis=0).T
            wts[which, q] = turned[:, : 4 * room].astype(jnp.bfloat16)


def return_scratch(plan, room, tok_rows):
    def bf(*shape):
        return pltpu.VMEM(shape, jnp.bfloat16)

    def dma(*shape):
        return pltpu.SemaphoreType.DMA(shape)

    side = plan.blocks // 2
    low = (2,) * plan.stages
    split = plan.split(tok_rows)
    landing = [
        bf(2, side, tok_rows, 4 * room),
        bf(RING, 2, 2, *low, room, LANES),
        bf(RING, 2, *low, room, LANES),
    ]
    local = [
        bf(2, 2, 2, *((2,) * plan.count), room, LANES),
        bf(2, 2, *low, tok_rows, LANES),
    ]
    sems = [dma(2, 2, 3), dma(RING, 2, 3)]
    for t in range(plan.stages):
        for rows in split:
            left = (2,) * (plan.stages - 1 - t)
            landing.append(bf(RING, 2, *left, rows, LANES))
            if t + 1 < plan.stages:
                local.append(bf(2, 2, *left, rows, LANES))
        sems += [dma(2, 2, 2), dma(RING, 2, 2)]
    return landing, local, sems


def return_steps(plan, seg, me, act, weight_of, finish, landing, local, sems):
    wts, leaf, swapped = landing[:3]
    ys, first = local[:2]
    stages = plan.stages
    arrived = [landing[3 + 2 * t : 5 + 2 * t] for t in range(stages)]
    parts = [local[2 + 2 * t : 4 + 2 * t] for t in range(stages - 1)]
    side = plan.blocks // 2
    room = ys.shape[-2]
    slot_rows = plan.blocks * room
    tok_rows = first.shape[-2]
    split = plan.split(tok_rows)
    spans = (pl.ds(0, split[0]), pl.ds(split[0], split[1]))
    mine = [bit_of(me, bit) for bit in range(plan.count)]

    def region(which, own):
        bit = plan.leaf[which]
        place = plan.count - 1 - bit
        return tuple(
            (mine[bit] if own else 1 - mine[bit]) if i == place else slice(None)
            for i in range(plan.count)
        )

    def first_copies(which, j):
        nbr = flip(me, plan.leaf[which])
        sources = (
            (ys.at[(j % 2, which, 1) + region(which, False)], leaf.at[j % RING, which, 0], (seg, nbr)),
            (ys.at[(j % 2, which, 0) + region(which, False)], leaf.at[j % RING, which, 1], (1 - seg, nbr)),
            (ys.at[(j % 2, which, 0) + region(which, True)], swapped.at[j % RING, which], (1 - seg, me)),
        )
        return [
            remote(src, dst, sems[0].at[j % 2, which, k], sems[1].at[j % RING, which, k], peer)
            for k, (src, dst, peer) in enumerate(sources)
        ]

    def held_at(which, t, r, j, index):
        if t == 0:
            return (j % 2, which) + index + (spans[r],)
        return (j % 2, which) + index

    def send(which, t, r, j):
        bit = plan.rest[which][r][t]
        dims = plan.dims(which, r, t)
        index = tuple(1 - mine[d] if d == bit else slice(None) for d in dims)
        source = first if t == 0 else parts[t - 1][r]
        return remote(
            source.at[held_at(which, t, r, j, index)],
            arrived[t][r].at[j % RING, which],
            sems[2 + 2 * t].at[j % 2, which, r],
            sems[3 + 2 * t].at[j % RING, which, r],
            (seg, flip(me, bit)),
        )

    def project(j):
        weight = weight_of(j)
        blocks = (2,) * plan.count
        for section in range(2):
            result = jnp.dot(
                act[pl.ds(section * slot_rows, slot_rows), :],
                weight[...],
                preferred_element_type=jnp.float32,
            ).astype(jnp.bfloat16)
            for which in range(2):
                half = result[:, which * LANES : (which + 1) * LANES]
                ys[j % 2, which, section] = half.reshape(blocks + (room, LANES))
        for which in range(2):
            for copy in first_copies(which, j):
                copy.start()

    def combine(j):
        for which in range(2):
            for copy in first_copies(which, j):
                copy.wait()
            own = mine[plan.leaf[which]]
            place = plan.count - 1 - plan.leaf[which]

            @pl.loop(0, side, unroll=8)
            def _(q):
                ix = digits(q, stages)
                full = tuple(ix[:place] + [own] + ix[place:])
                ix = tuple(ix)
                both = jnp.concatenate(
                    [
                        ys[(j % 2, which, 1) + full],
                        swapped[(j % RING, which) + ix],
                        leaf[(j % RING, which, 0) + ix],
                        leaf[(j % RING, which, 1) + ix],
                    ],
                    axis=0,
                )
                part = jnp.dot(wts[which, q], both, preferred_element_type=jnp.float32)
                first[(j % 2, which) + ix] = part.astype(jnp.bfloat16)

            for r in range(2):
                send(which, 0, r, j).start()

    def reduce_stage(t, j):
        last = t == stages - 1
        left = stages - 1 - t
        for which in range(2):
            for r in range(2):
                send(which, t, r, j).wait()
                bit = plan.rest[which][r][t]
                place = plan.dims(which, r, t).index(bit)
                source = first if t == 0 else parts[t - 1][r]

                def total(ix):
                    full = tuple(ix[:place] + [mine[bit]] + ix[place:])
                    held = source[held_at(which, t, r, j, full)]
                    came = arrived[t][r][(j % RING, which) + tuple(ix)]
                    return held.astype(jnp.float32) + came.astype(jnp.float32)

                if last:
                    start = pl.multiple_of((2 * j + which) * LANES, LANES)
                    finish(spans[r], pl.ds(start, LANES), total([]))
                else:

                    @pl.loop(0, 1 << left, unroll=2)
                    def _(e):
                        ix = digits(e, left)
                        parts[t][r][(j % 2, which) + tuple(ix)] = total(ix).astype(jnp.bfloat16)

                    send(which, t + 1, r, j).start()

    steps = [(0, project), (1, combine)]
    for t in range(stages):
        steps.append((2 + t, functools.partial(reduce_stage, t)))
    return steps


def gather_scratch(plan, room, tok_rows, units):
    def bf(*shape):
        return pltpu.VMEM(shape, jnp.bfloat16)

    def f32(*shape):
        return pltpu.VMEM(shape, jnp.float32)

    def dma(*shape):
        return pltpu.SemaphoreType.DMA(shape)

    blocks = plan.blocks
    side = blocks // 2
    slot_rows = blocks * room
    landing = [
        bf(LONG_RING, *((2,) * plan.stages), tok_rows, LANES),
        bf(LONG_RING, 3, side, room, LANES),
    ]
    local = [
        bf(2, side, 4 * room, tok_rows),
        f32(slot_rows, LANES),
        bf(3, side, room, LANES),
        bf(3, 3, side, room, LANES),
        bf(2 * slot_rows, 2 * LANES),
        f32(2 * slot_rows, 2 * units),
        bf(3, 2 * LANES, 2 * units),
    ]
    sems = [dma(3, 3), dma(LONG_RING, 3), dma(3, 2)]
    for _ in range(plan.stages):
        sems += [dma(RING, 2), dma(RING, 2)]
    return landing, local, sems


def gather_steps(plan, seg, me, x, places, gates, gains, w_in, act, scratch, sems):
    (held, got, picks, scale, keep, give, lhs, hid, w_buf) = scratch
    blocks = plan.blocks
    side = blocks // 2
    mine = [bit_of(me, bit) for bit in range(plan.count)]
    tok_rows, half = x.shape
    split = plan.split(tok_rows)
    spans = (pl.ds(0, split[0]), pl.ds(split[0], split[1]))
    wide = LANES
    room = keep.shape[-2]
    slot_rows = blocks * room
    units = act.shape[1]
    tile = math.gcd(slot_rows, 256)

    def columns(j):
        return pl.ds(pl.multiple_of(j * wide, wide), wide)

    def send(which, t, r, j):
        order = plan.rest[which][r]
        bit = order[plan.stages - 1 - t]
        free = order[plan.stages - t :]
        rows = spans[r]
        index = tuple(slice(None) if d in free else mine[d] for d in plan.dims(which, r, 0))
        dst = held.at[(j % LONG_RING,) + index + (rows,)]
        return remote(
            x.at[rows, columns(j)] if t == 0 else dst,
            dst,
            sems[3 + 2 * t].at[j % RING, r],
            sems[4 + 2 * t].at[j % RING, r],
            (seg, flip(me, bit)),
        )

    def first_send(which, j):
        for r in range(2):
            send(which, 0, r, j).start()
        index = tuple(mine[d] for d in plan.dims(which, 0, 0))
        held[(j % LONG_RING,) + index] = x[:, columns(j)]

    def relay(t, which, j):
        for r in range(2):
            send(which, t - 1, r, j).wait()
            send(which, t, r, j).start()

    def last_copies(which, j):
        nbr = flip(me, plan.leaf[which])
        peers = ((1 - seg, me), (seg, nbr), (1 - seg, nbr))
        return [
            remote(
                give.at[j % 3, k],
                got.at[j % LONG_RING, k],
                sems[0].at[j % 3, k],
                sems[1].at[j % LONG_RING, k],
                peer,
            )
            for k, peer in enumerate(peers)
        ]

    def weight_copies(j):
        copies = []
        for which, owner in enumerate((seg, 1 - seg)):
            rows = pl.ds(pl.multiple_of(owner * half + j * wide, wide), wide)
            copies.append(
                pltpu.make_async_copy(
                    w_in.at[rows, :],
                    w_buf.at[j % 3, pl.ds(which * wide, wide)],
                    sems[2].at[j % 3, which],
                )
            )
        return copies

    row = lax.broadcasted_iota(jnp.int32, (room, tok_rows), 0).astype(jnp.float32)

    def read_places():
        for which in range(2):
            bit = plan.leaf[which]

            @pl.loop(0, side)
            def _(q):
                d = spread_index(q, bit, mine[bit])
                place = places[d]
                picks[which, q] = jnp.concatenate(
                    [jnp.where(place[k : k + 1, :] == row, 1.0, 0.0) for k in rows_of(which)],
                    axis=0,
                ).astype(jnp.bfloat16)

    def read_factors():
        @pl.loop(0, blocks)
        def _(d):
            own = places[d][0:1, :] == row
            line = gates[d][FACTOR_ROW : FACTOR_ROW + 1, :]
            factor = jnp.sum(jnp.where(own, line, 0.0), axis=1, keepdims=True)
            rows = pl.ds(pl.multiple_of(d * room, room), room)
            scale[rows, :] = jnp.broadcast_to(factor, (room, wide))

    def pick(which, j):
        for copy in weight_copies(j):
            copy.start()
        for r in range(2):
            send(which, plan.stages - 1, r, j).wait()

        @pl.loop(0, side, unroll=4)
        def _(q):
            there = held[(j % LONG_RING,) + tuple(digits(q, plan.stages))]
            taken = jnp.dot(picks[which, q], there, preferred_element_type=jnp.float32)
            taken = taken.astype(jnp.bfloat16)
            keep[j % 3, q] = taken[:room]
            for k in range(3):
                give[j % 3, k, q] = taken[(k + 1) * room : (k + 2) * room]

        for copy in last_copies(which, j):
            copy.start()

    def multiply(which, j):
        for copy in last_copies(which, j):
            copy.wait()
        for copy in weight_copies(j):
            copy.wait()
        bit = plan.leaf[which]
        places = [
            pl.ds(pl.multiple_of(owner * half + j * wide, wide), wide) for owner in (seg, 1 - seg)
        ]
        factors = [[gains[pl.ds(section, 1), place] for place in places] for section in range(2)]

        @pl.loop(0, side, unroll=2)
        def _(q):
            for own, sources in (
                (mine[bit], (keep.at[j % 3, q], got.at[j % LONG_RING, 0, q])),
                (1 - mine[bit], (got.at[j % LONG_RING, 1, q], got.at[j % LONG_RING, 2, q])),
            ):
                base = spread_index(q, bit, own) * room
                factor = scale[pl.ds(pl.multiple_of(base, room), room), :]
                for f, source in enumerate(sources):
                    scaled = source[...].astype(jnp.float32) * factor
                    for section in range(2):
                        to = pl.ds(pl.multiple_of(section * slot_rows + base, room), room)
                        lhs[to, pl.ds(f * wide, wide)] = (scaled * factors[section][f]).astype(
                            jnp.bfloat16
                        )

        for section in range(2):
            rows = pl.ds(section * slot_rows, slot_rows)
            hid[rows, :] += jnp.dot(
                lhs[rows, :], w_buf[j % 3], preferred_element_type=jnp.float32
            )

    def clear():
        @pl.loop(0, 2 * slot_rows // tile)
        def _(r):
            rows = pl.ds(pl.multiple_of(r * tile, tile), tile)
            hid[rows, :] = jnp.zeros((tile, 2 * units), jnp.float32)

    def activate():
        @pl.loop(0, 2 * slot_rows // tile)
        def _(r):
            rows = pl.ds(pl.multiple_of(r * tile, tile), tile)
            gate = hid[rows, :units]
            act[rows, :] = (gate / (1.0 + jnp.exp(-gate)) * hid[rows, units:]).astype(jnp.bfloat16)

    steps = [(0, by_parity(first_send))]
    for t in range(1, plan.stages):
        steps.append((t, by_parity(functools.partial(relay, t))))
    steps += [(plan.stages, by_parity(pick)), (plan.stages + 2, by_parity(multiply))]
    return steps, read_places, read_factors, clear, activate


def column_sum(values):
    return jnp.sum(values, axis=1, keepdims=True)


def fused_kernel(plan, room, capacity, sizes, *refs):
    (x, gain, gain2, ids, copies, later_ids, table, router_in, router2_in, w_in, w_out) = refs[:11]
    states, ratio = refs[11:13]
    n_own, n_gather, n_back, n_gather_sems = sizes
    own = refs[13 : 13 + n_own]
    whole, gain_got, gains, act, mixed, squares, normed, score, score_got = own[:9]
    router, router2, spots, weights, places, gates, wide, w_ring = own[9:]
    refs = refs[13 + n_own :]
    gather_landing, refs = refs[:n_gather], refs[n_gather:]
    back, sems = refs[:n_back], refs[n_back:]
    swap_sems, load_sems, share_sems, sems = sems[:2], sems[2], sems[3:5], sems[5:]
    gather_sems, return_sems = sems[:n_gather_sems], sems[n_gather_sems:]
    seg = lax.axis_index("segment")
    me = lax.axis_index("expert")
    mine = [bit_of(me, bit) for bit in range(plan.count)]
    blocks = plan.blocks
    count = plan.count
    tok_rows, half = x.shape
    full = 2 * half
    top = ids.shape[0]
    tiles = full // LANES
    slot_count = table.shape[1]
    f32 = jnp.float32
    partner = (1 - seg, me)
    at_home = tuple(reversed(mine))

    def tile_at(i):
        return pl.ds(pl.multiple_of(i * LANES, LANES), LANES)

    own_columns = pl.ds(pl.multiple_of(seg * half, half), half)
    swap_x = remote(x, whole.at[:, own_columns], swap_sems[0].at[0], swap_sems[1].at[0], partner)
    swap_gain = remote(gain, gain_got, swap_sems[0].at[1], swap_sems[1].at[1], partner)
    swap_score = remote(score, score_got, swap_sems[0].at[2], swap_sems[1].at[2], partner)
    load_router = pltpu.make_async_copy(router_in, router, load_sems.at[0])
    load_router2 = pltpu.make_async_copy(router2_in, router2, load_sems.at[1])

    def load_w_out(j):
        columns = pl.ds(pl.multiple_of(j * 2 * LANES, 2 * LANES), 2 * LANES)
        return pltpu.make_async_copy(
            w_out.at[:, columns], w_ring.at[j % 3], load_sems.at[2 + j % 3]
        )

    back_chunks = full // (2 * LANES)

    def weight_of(j):
        load_w_out(j).wait()

        @pl.when(j + 2 < back_chunks)
        def _():
            load_w_out(j + 2).start()

        return w_ring.at[j % 3]

    def share(kind, bit):
        ref = (spots, weights)[kind]
        index = tuple(slice(None) if d < bit else mine[d] for d in reversed(range(count)))
        return remote(
            ref.at[index],
            ref.at[index],
            share_sems[0].at[kind, bit],
            share_sems[1].at[kind, bit],
            (seg, flip(me, bit)),
        )

    def matches():
        line = table[...].astype(f32)
        i_row = lax.broadcasted_iota(jnp.int32, (slot_count, slot_count), 0)
        i_col = lax.broadcasted_iota(jnp.int32, (slot_count, slot_count), 1)
        column = column_sum(jnp.where(i_row == i_col, line, 0.0))
        same = column == line
        rank = column_sum(jnp.where(same & (i_col < i_row), 1.0, 0.0))
        holders = column_sum(jnp.where(same, 1.0, 0.0))
        wanted = ids[...].astype(f32)
        choice = copies[...].astype(f32)
        of_two = choice - 2.0 * jnp.floor(choice * 0.5)
        of_three = choice - 3.0 * jnp.floor((choice + 0.5) * (1.0 / 3.0))
        found = []
        for k in range(top):
            turn = jnp.where(
                holders == 1.0,
                0.0,
                jnp.where(holders == 2.0, of_two[k : k + 1, :], of_three[k : k + 1, :]),
            )
            found.append((column == wanted[k : k + 1, :]) & (rank == turn))
        return wanted, found

    def place_tokens():
        hit = jnp.zeros((slot_count, tok_rows), f32)
        for match in matches()[1]:
            hit += jnp.where(match, 1.0, 0.0)
        t_row = lax.broadcasted_iota(jnp.int32, (tok_rows, tok_rows), 0)
        t_col = lax.broadcasted_iota(jnp.int32, (tok_rows, tok_rows), 1)
        earlier = jnp.where(t_row < t_col, 1.0, 0.0).astype(jnp.bfloat16)
        before = jnp.dot(hit.astype(jnp.bfloat16), earlier, preferred_element_type=f32)
        place = jnp.where((hit > 0.0) & (before < capacity), before, -1.0)
        spots[at_home] = place.astype(jnp.bfloat16)

    def normalize():
        total = jnp.zeros((tok_rows, LANES), f32)
        for i in range(tiles):
            part = whole[:, i * LANES : (i + 1) * LANES].astype(f32)
            total += part * part
        return lax.rsqrt(column_sum(total) / full + EPS)

    def prologue():
        gains[1:2, :] = gain[...].astype(f32)
        swap_gain.wait()
        gains[0:1, :] = gain_got[...].astype(f32)
        swap_x.wait()
        squares[...] = jnp.broadcast_to(normalize(), (tok_rows, LANES))

        @pl.loop(0, tiles)
        def _(i):
            part = whole[:, tile_at(i)].astype(f32) * squares[...]
            normed[:, tile_at(i)] = (part * gains[1:2, tile_at(i)]).astype(jnp.bfloat16)

    def weigh_tokens():
        load_router.wait()
        logits = lax.dot_general(
            router[...], normed[...], (((1,), (1,)), ((), ())), preferred_element_type=f32
        )
        names = lax.broadcasted_iota(jnp.int32, logits.shape, 0).astype(f32)
        wanted, found = matches()
        chosen = [
            jnp.sum(jnp.where(names == wanted[k : k + 1, :], logits, 0.0), axis=0, keepdims=True)
            for k in range(top)
        ]
        most = functools.reduce(jnp.maximum, chosen)
        lifted = [jnp.exp(value - most) for value in chosen]
        weight = functools.reduce(jnp.add, lifted)
        gate = jnp.zeros((slot_count, tok_rows), f32)
        for k in range(top):
            rounded = (lifted[k] / weight).astype(jnp.bfloat16).astype(f32)
            gate += jnp.where(found[k], rounded, 0.0)
        rest = squares[...].T[0:1, :]
        rows = [gate]
        for _ in range(3):
            rows.append(rest.astype(jnp.bfloat16).astype(f32))
            rest = rest - rows[-1]
        rows.append(jnp.zeros((EXTRA_ROWS - 3, tok_rows), f32))
        weights[at_home] = jnp.concatenate(rows, axis=0).astype(jnp.bfloat16)

    def widen(kind):
        source, target = (spots, weights)[kind], (places, gates)[kind]

        @pl.loop(0, blocks)
        def _(d):
            wide[kind, : source.shape[-2]] = source[tuple(digits(d, count))].astype(f32)
            for k, slot in enumerate(slots_of(plan, seg, me)):
                target[d, k : k + 1, :] = wide[kind, pl.ds(slot, 1), :]
            if kind == 1:
                extra = wide[kind, slot_count : slot_count + 8, :]
                target[d, FACTOR_ROW : FACTOR_ROW + 1, :] = jnp.sum(extra, axis=0, keepdims=True)

    def pass_on(when):
        if when == 0:
            prologue()
        if when == 1:
            weigh_tokens()
            share(1, 0).start()
        if when <= count - 2:
            share(0, when).wait()
            share(0, when + 1).start()
        if 2 <= when <= count:
            share(1, when - 2).wait()
            share(1, when - 1).start()

    def combine_weights():
        make_weights(plan, me, room, places, gates, back[0])

    def gather_part(*local):
        steps, read_places, read_factors, clear, activate = gather_steps(
            plan, seg, me, x, places, gates, gains, w_in, act, gather_landing + local, gather_sems
        )

        def take_places():
            share(0, count - 1).wait()
            widen(0)
            read_places()

        def take_factors():
            share(1, count - 1).wait()
            widen(1)
            read_factors()

        place_tokens()
        whole[:, own_columns] = x[...]
        clear()
        pl.semaphore_wait(barrier, len(friends))
        swap_x.start()
        swap_gain.start()
        share(0, 0).start()
        late = {when: functools.partial(pass_on, when) for when in range(count + 1)}
        late[count + 3] = combine_weights
        early = {plan.stages: take_places, plan.stages + 2: take_factors}
        run_stages(half // LANES, steps, early, late)
        activate()

    def finish(rows, columns, total):
        value = whole[rows, columns].astype(f32) + total
        mixed[rows, columns] = value
        states[rows, columns] = value.astype(jnp.bfloat16)
        squares[rows, :] += value * value

    def return_part(*local):
        steps = return_steps(plan, seg, me, act, weight_of, finish, back, local, return_sems)
        run_stages(back_chunks, steps, {}, {})

    barrier = pltpu.get_barrier_semaphore()
    friends = near_friends(plan, seg, me)
    for friend in friends:
        pl.semaphore_signal(barrier, inc=1, device_id=friend, device_id_type=MESH)
    load_router.start()
    load_router2.start()
    load_w_out(0).start()
    load_w_out(1).start()
    pl.run_scoped(gather_part, *gather_scratch(plan, room, tok_rows, act.shape[1])[1])
    squares[...] = jnp.zeros((tok_rows, LANES), f32)
    pl.run_scoped(return_part, *return_scratch(plan, room, tok_rows)[1])
    inverse = lax.rsqrt(column_sum(squares[...]) / full + EPS)
    squares[...] = jnp.broadcast_to(inverse, (tok_rows, LANES))

    @pl.loop(0, tiles)
    def _(i):
        part = mixed[:, tile_at(i)] * squares[...]
        normed[:, tile_at(i)] = (part * gain2[:, tile_at(i)].astype(f32)).astype(jnp.bfloat16)

    load_router2.wait()
    logits = lax.dot_general(
        router2[...], normed[...], (((1,), (1,)), ((), ())), preferred_element_type=f32
    )
    shifted = logits - jnp.max(logits, axis=0, keepdims=True)
    logp = shifted - jnp.log(jnp.sum(jnp.exp(shifted), axis=0, keepdims=True))
    names = lax.broadcasted_iota(jnp.int32, logits.shape, 0).astype(f32)
    wanted = later_ids[...].astype(f32)
    total = jnp.zeros((1, tok_rows), f32)
    for k in range(top):
        total += jnp.sum(jnp.where(names == wanted[k : k + 1, :], logp, 0.0), axis=0, keepdims=True)
    score[...] = jnp.broadcast_to(total, score.shape)
    swap_score.start()
    swap_score.wait()
    sign = (2 * seg - 1).astype(f32)
    difference = (score[0:1, :] - score_got[0:1, :]) * sign
    turned = jnp.broadcast_to(difference, (tok_rows, tok_rows)).T
    t_row = lax.broadcasted_iota(jnp.int32, (tok_rows, tok_rows), 0)
    t_col = lax.broadcasted_iota(jnp.int32, (tok_rows, tok_rows), 1)
    picked = jnp.sum(jnp.where(t_row == 2 * t_col + seg, turned, 0.0), axis=0, keepdims=True)
    ratio[...] = picked[:, : tok_rows // 2]


def fused_scratch(plan, room, tok_rows, half, slot_count, units, experts):
    full = 2 * half
    rows = 2 * plan.blocks * room
    low = (2,) * plan.count

    def bf(*shape):
        return pltpu.VMEM(shape, jnp.bfloat16)

    def f32(*shape):
        return pltpu.VMEM(shape, jnp.float32)

    own = [
        bf(tok_rows, full),
        bf(1, full),
        f32(2, full),
        bf(rows, units),
        f32(tok_rows, full),
        f32(tok_rows, LANES),
        bf(tok_rows, full),
        f32(8, tok_rows),
        f32(8, tok_rows),
        bf(experts, full),
        bf(experts, full),
        bf(*low, slot_count, tok_rows),
        bf(*low, slot_count + EXTRA_ROWS, tok_rows),
        f32(plan.blocks, 8, tok_rows),
        f32(plan.blocks, 8, tok_rows),
        f32(2, slot_count + EXTRA_ROWS, tok_rows),
        bf(3, units, 2 * LANES),
    ]
    gather, _, gather_sems = gather_scratch(plan, room, tok_rows, units)
    back, _, back_sems = return_scratch(plan, room, tok_rows)
    shapes = ((3,), (3,), (5,), (2, plan.count), (2, plan.count))
    swap = [pltpu.SemaphoreType.DMA(shape) for shape in shapes]
    sizes = (len(own), len(gather), len(back), len(gather_sems))
    return own + gather + back, swap + gather_sems + back_sems, sizes


def fused_call(plan, room, capacity, scratch, sems, sizes, *args):
    tok_rows, half = args[0].shape
    vmem = pl.BlockSpec(memory_space=pltpu.VMEM)
    anywhere = pl.BlockSpec(memory_space=pl.ANY)
    return pl.pallas_call(
        functools.partial(fused_kernel, plan, room, capacity, sizes),
        out_shape=(
            jax.ShapeDtypeStruct((tok_rows, 2 * half), jnp.bfloat16),
            jax.ShapeDtypeStruct((1, tok_rows // 2), jnp.float32),
        ),
        in_specs=[vmem] * 7 + [anywhere] * 4,
        out_specs=(vmem, vmem),
        scratch_shapes=scratch + sems,
        compiler_params=pltpu.CompilerParams(
            collective_id=0, has_side_effects=True, vmem_limit_bytes=VMEM_MOST
        ),
        name="fused_layer",
    )(*args)


def per_device(
    rollout,
    norm_gain,
    router_first,
    gain_second,
    router_second,
    expert_ids,
    copy_pick,
    later_ids,
    slot_table,
    expert_in,
    expert_out,
):
    segment_count = lax.axis_size("segment")
    chip_count = lax.axis_size("expert")
    tok_rows, half = rollout.shape
    capacity = 3 * tok_rows * expert_ids.shape[1] // (2 * segment_count * chip_count)
    plan = Plan(grid_sides(chip_count))
    room = -(-capacity // 16) * 16
    scratch, sems, sizes = fused_scratch(
        plan,
        room,
        tok_rows,
        half,
        slot_table.shape[0],
        expert_out.shape[1],
        router_first.shape[2],
    )
    states, column = fused_call(
        plan,
        room,
        capacity,
        scratch,
        sems,
        sizes,
        rollout,
        norm_gain,
        gain_second,
        expert_ids.T,
        copy_pick.T,
        later_ids.T,
        slot_table[None, :],
        router_first[0].T,
        router_second[0].T,
        expert_in[0],
        expert_out[0],
    )
    return states[None], column.reshape(-1, 1)


def solution(mesh):
    in_specs = (
        P("expert", "segment"),
        P("segment", None),
        P("segment", None, None),
        P("segment", None),
        P("segment", None, None),
        P("expert", None),
        P("expert", None),
        P("expert", None),
        P(),
        P(("segment", "expert"), None, None),
        P(("segment", "expert"), None, None),
    )
    out_specs = (P("segment", "expert", None), P("expert", "segment"))
    return jax.shard_map(
        per_device, mesh=mesh, in_specs=in_specs, out_specs=out_specs, check_vma=False
    )
```

```python
import functools
import math

import jax
import jax.numpy as jnp
from jax import lax
from jax.experimental import pallas as pl
from jax.experimental.pallas import tpu as pltpu
from jax.sharding import PartitionSpec as P

LANES = 128
VMEM_MOST = 67043328
MESH = pl.DeviceIdType.MESH
EPS = 1e-06
RING = 4
EXTRA_ROWS = 16


def grid_sides(count):
    outer = 1
    while outer**3 < count:
        outer *= 2
    rest = count // outer
    middle = 1
    while middle**2 < rest:
        middle *= 2
    return outer, middle, rest // middle


class Plan:
    def __init__(self, sides):
        logs = [side.bit_length() - 1 for side in sides]
        n_a, n_b, n_c = logs
        bits_c = list(range(n_c))
        bits_b = list(range(n_c, n_c + n_b))
        bits_a = list(range(n_c + n_b, n_c + n_b + n_a))
        self.count = n_a + n_b + n_c
        self.blocks = 1 << self.count
        self.leaf = (bits_c[0], bits_b[0])
        orders = (
            (bits_c + bits_a + bits_b, bits_c + bits_b + bits_a),
            (bits_b + bits_a + bits_c, bits_b + bits_c + bits_a),
        )
        self.rest = [[order[1:] for order in pair] for pair in orders]
        self.stages = self.count - 1
        self.gap = 2 if self.count <= 4 else 1
        self.last_gap = self.gap + 1
        self.pick_lag = self.gap * self.stages
        self.multiply_lag = self.pick_lag + self.last_gap
        self.stage_ring = self.ring(self.gap, self.gap)
        self.held_ring = self.ring(self.pick_lag, self.gap)
        self.last_ring = self.ring(self.last_gap, self.last_gap)

    def ring(self, busy, gap):
        ahead = busy + 1 + (busy + 1) % 2
        return ahead + 1 + gap + (ahead + 1 + gap) % 2

    def split(self, rows):
        part = max(3 * rows // 8 // 16 * 16, 16)
        return part, rows - part

    def dims(self, which, order, done):
        used = [self.leaf[which]] + self.rest[which][order][:done]
        return [bit for bit in reversed(range(self.count)) if bit not in used]


def bit_of(index, bit):
    return (index // (1 << bit)) % 2


def flip(index, bit):
    return index + (1 << bit) * (1 - 2 * bit_of(index, bit))


def digits(value, count):
    return [(value // (1 << (count - 1 - i))) % 2 for i in range(count)]


def spread_index(value, bit, own):
    low = 1 << bit
    return (value // low) * (2 * low) + own * low + value % low


def remote(src, dst, send, recv, peer):
    return pltpu.make_async_remote_copy(
        src_ref=src,
        dst_ref=dst,
        send_sem=send,
        recv_sem=recv,
        device_id=peer,
        device_id_type=MESH,
    )


def run_stages(chunks, stages, early, late):
    depth = max(lag for lag, _ in stages)

    @pl.loop(0, chunks + depth)
    def _(step):
        for lag, stage in stages:
            if lag in early:

                @pl.when(step == lag)
                def _():
                    early[lag]()

            @pl.when((step >= lag) & (step - lag < chunks))
            def _():
                stage(step - lag)

        for when, hook in late.items():

            @pl.when(step == when)
            def _():
                hook()


def by_parity(stage):
    def run(j):
        for which in range(2):

            @pl.when(j % 2 == which)
            def _():
                stage(which, j)

    return run


def near_friends(plan, seg, me):
    friends = [(1 - seg, me)] + [(seg, flip(me, bit)) for bit in range(plan.count)]
    return friends + [(1 - seg, flip(me, bit)) for bit in plan.leaf]


def slots_of(plan, seg, me):
    chips = [me] + [flip(me, bit) for bit in plan.leaf]
    return [core * plan.blocks + chip for chip in chips for core in (seg, 1 - seg)]


def rows_of(which):
    return (0, 1, 2 + 2 * which, 3 + 2 * which)


def make_weights(plan, me, room, places, gates, wts):
    tok_rows = places.shape[-1]
    row = lax.broadcasted_iota(jnp.int32, (room, tok_rows), 0).astype(jnp.float32)
    for which in range(2):
        bit = plan.leaf[which]

        @pl.loop(0, plan.blocks // 2)
        def _(q):
            d = spread_index(q, bit, bit_of(me, bit))
            place, gate = places[d], gates[d]
            pieces = []
            for k in rows_of(which):
                hit = place[k : k + 1, :] == row
                pieces.append(jnp.where(hit, gate[k : k + 1, :], 0.0))
            pad = -(4 * room) % LANES
            if pad:
                pieces.append(jnp.zeros((pad, tok_rows), jnp.float32))
            turned = jnp.concatenate(pieces, axis=0).T
            wts[which, q] = turned[:, : 4 * room].astype(jnp.bfloat16)


def return_scratch(plan, room, tok_rows):
    def bf(*shape):
        return pltpu.VMEM(shape, jnp.bfloat16)

    def dma(*shape):
        return pltpu.SemaphoreType.DMA(shape)

    side = plan.blocks // 2
    low = (2,) * plan.stages
    split = plan.split(tok_rows)
    landing = [
        bf(2, side, tok_rows, 4 * room),
        bf(RING, 2, 2, *low, room, LANES),
        bf(RING, 2, *low, room, LANES),
    ]
    local = [
        bf(2, 2, 2, *((2,) * plan.count), room, LANES),
        bf(2, 2, *low, tok_rows, LANES),
    ]
    sems = [dma(2, 2, 3), dma(RING, 2, 3)]
    for t in range(plan.stages):
        for rows in split:
            left = (2,) * (plan.stages - 1 - t)
            landing.append(bf(RING, 2, *left, rows, LANES))
            if t + 1 < plan.stages:
                local.append(bf(2, 2, *left, rows, LANES))
        sems += [dma(2, 2, 2), dma(RING, 2, 2)]
    return landing, local, sems


def return_steps(plan, seg, me, act, weight_of, finish, landing, local, sems):
    wts, leaf, swapped = landing[:3]
    ys, first = local[:2]
    stages = plan.stages
    arrived = [landing[3 + 2 * t : 5 + 2 * t] for t in range(stages)]
    parts = [local[2 + 2 * t : 4 + 2 * t] for t in range(stages - 1)]
    side = plan.blocks // 2
    room = ys.shape[-2]
    slot_rows = plan.blocks * room
    tok_rows = first.shape[-2]
    split = plan.split(tok_rows)
    spans = (pl.ds(0, split[0]), pl.ds(split[0], split[1]))
    mine = [bit_of(me, bit) for bit in range(plan.count)]

    def region(which, own):
        bit = plan.leaf[which]
        place = plan.count - 1 - bit
        return tuple(
            (mine[bit] if own else 1 - mine[bit]) if i == place else slice(None)
            for i in range(plan.count)
        )

    def first_copies(which, j):
        nbr = flip(me, plan.leaf[which])
        sources = (
            (ys.at[(j % 2, which, 1) + region(which, False)], leaf.at[j % RING, which, 0], (seg, nbr)),
            (ys.at[(j % 2, which, 0) + region(which, False)], leaf.at[j % RING, which, 1], (1 - seg, nbr)),
            (ys.at[(j % 2, which, 0) + region(which, True)], swapped.at[j % RING, which], (1 - seg, me)),
        )
        return [
            remote(src, dst, sems[0].at[j % 2, which, k], sems[1].at[j % RING, which, k], peer)
            for k, (src, dst, peer) in enumerate(sources)
        ]

    def held_at(which, t, r, j, index):
        if t == 0:
            return (j % 2, which) + index + (spans[r],)
        return (j % 2, which) + index

    def send(which, t, r, j):
        bit = plan.rest[which][r][t]
        dims = plan.dims(which, r, t)
        index = tuple(1 - mine[d] if d == bit else slice(None) for d in dims)
        source = first if t == 0 else parts[t - 1][r]
        return remote(
            source.at[held_at(which, t, r, j, index)],
            arrived[t][r].at[j % RING, which],
            sems[2 + 2 * t].at[j % 2, which, r],
            sems[3 + 2 * t].at[j % RING, which, r],
            (seg, flip(me, bit)),
        )

    def project(j):
        weight = weight_of(j)
        blocks = (2,) * plan.count
        for section in range(2):
            result = jnp.dot(
                act[pl.ds(section * slot_rows, slot_rows), :],
                weight[...],
                preferred_element_type=jnp.float32,
            ).astype(jnp.bfloat16)
            for which in range(2):
                half = result[:, which * LANES : (which + 1) * LANES]
                ys[j % 2, which, section] = half.reshape(blocks + (room, LANES))
        for which in range(2):
            for copy in first_copies(which, j):
                copy.start()

    def combine(j):
        for which in range(2):
            for copy in first_copies(which, j):
                copy.wait()
            own = mine[plan.leaf[which]]
            place = plan.count - 1 - plan.leaf[which]

            @pl.loop(0, side, unroll=8)
            def _(q):
                ix = digits(q, stages)
                full = tuple(ix[:place] + [own] + ix[place:])
                ix = tuple(ix)
                both = jnp.concatenate(
                    [
                        ys[(j % 2, which, 1) + full],
                        swapped[(j % RING, which) + ix],
                        leaf[(j % RING, which, 0) + ix],
                        leaf[(j % RING, which, 1) + ix],
                    ],
                    axis=0,
                )
                part = jnp.dot(wts[which, q], both, preferred_element_type=jnp.float32)
                first[(j % 2, which) + ix] = part.astype(jnp.bfloat16)

            for r in range(2):
                send(which, 0, r, j).start()

    def reduce_stage(t, j):
        last = t == stages - 1
        left = stages - 1 - t
        for which in range(2):
            for r in range(2):
                send(which, t, r, j).wait()
                bit = plan.rest[which][r][t]
                place = plan.dims(which, r, t).index(bit)
                source = first if t == 0 else parts[t - 1][r]

                def total(ix):
                    full = tuple(ix[:place] + [mine[bit]] + ix[place:])
                    held = source[held_at(which, t, r, j, full)]
                    came = arrived[t][r][(j % RING, which) + tuple(ix)]
                    return held.astype(jnp.float32) + came.astype(jnp.float32)

                if last:
                    start = pl.multiple_of((2 * j + which) * LANES, LANES)
                    finish(spans[r], pl.ds(start, LANES), total([]))
                else:

                    @pl.loop(0, 1 << left, unroll=2)
                    def _(e):
                        ix = digits(e, left)
                        parts[t][r][(j % 2, which) + tuple(ix)] = total(ix).astype(jnp.bfloat16)

                    send(which, t + 1, r, j).start()

    steps = [(0, project), (1, combine)]
    for t in range(stages):
        steps.append((2 + t, functools.partial(reduce_stage, t)))
    return steps


def gather_scratch(plan, room, tok_rows, units):
    def bf(*shape):
        return pltpu.VMEM(shape, jnp.bfloat16)

    def f32(*shape):
        return pltpu.VMEM(shape, jnp.float32)

    def dma(*shape):
        return pltpu.SemaphoreType.DMA(shape)

    blocks = plan.blocks
    side = blocks // 2
    slot_rows = blocks * room
    near = plan.last_gap + 1
    landing = [
        bf(plan.held_ring, *((2,) * plan.stages), tok_rows, LANES),
        bf(plan.last_ring, 3, side, room, LANES),
    ]
    local = [
        bf(2, side, 4 * room, tok_rows),
        f32(slot_rows, LANES),
        bf(near, side, room, LANES),
        bf(near, 3, side, room, LANES),
        bf(2 * slot_rows, 2 * LANES),
        f32(2 * slot_rows, 2 * units),
        bf(near, 2 * LANES, 2 * units),
    ]
    sems = [dma(near, 3), dma(plan.last_ring, 3), dma(near, 2)]
    for _ in range(plan.stages):
        sems += [dma(plan.stage_ring, 2), dma(plan.stage_ring, 2)]
    return landing, local, sems


def gather_steps(plan, seg, me, x, places, squares, gains, w_in, act, scratch, sems):
    (held, got, picks, scale, keep, give, lhs, hid, w_buf) = scratch
    blocks = plan.blocks
    side = blocks // 2
    mine = [bit_of(me, bit) for bit in range(plan.count)]
    tok_rows, half = x.shape
    split = (tok_rows // 2, tok_rows // 2)
    spans = (pl.ds(0, split[0]), pl.ds(split[0], split[1]))
    wide = LANES
    room = keep.shape[-2]
    slot_rows = blocks * room
    units = act.shape[1]
    near = plan.last_gap + 1
    tile = math.gcd(slot_rows, 256)

    def columns(j):
        return pl.ds(pl.multiple_of(j * wide, wide), wide)

    def send(which, t, r, j):
        order = plan.rest[which][r]
        bit = order[plan.stages - 1 - t]
        free = order[plan.stages - t :]
        rows = spans[r]
        index = tuple(slice(None) if d in free else mine[d] for d in plan.dims(which, r, 0))
        dst = held.at[(j % plan.held_ring,) + index + (rows,)]
        return remote(
            x.at[rows, columns(j)] if t == 0 else dst,
            dst,
            sems[3 + 2 * t].at[j % plan.stage_ring, r],
            sems[4 + 2 * t].at[j % plan.stage_ring, r],
            (seg, flip(me, bit)),
        )

    def first_send(which, j):
        for r in range(2):
            send(which, 0, r, j).start()
        index = tuple(mine[d] for d in plan.dims(which, 0, 0))
        held[(j % plan.held_ring,) + index] = x[:, columns(j)]

    def relay(t, which, j):
        for r in range(2):
            send(which, t - 1, r, j).wait()
            send(which, t, r, j).start()

    def last_copies(which, j):
        nbr = flip(me, plan.leaf[which])
        peers = ((1 - seg, me), (seg, nbr), (1 - seg, nbr))
        return [
            remote(
                give.at[j % near, k],
                got.at[j % plan.last_ring, k],
                sems[0].at[j % near, k],
                sems[1].at[j % plan.last_ring, k],
                peer,
            )
            for k, peer in enumerate(peers)
        ]

    def weight_copies(j):
        copies = []
        for which, owner in enumerate((seg, 1 - seg)):
            rows = pl.ds(pl.multiple_of(owner * half + j * wide, wide), wide)
            copies.append(
                pltpu.make_async_copy(
                    w_in.at[rows, :],
                    w_buf.at[j % near, pl.ds(which * wide, wide)],
                    sems[2].at[j % near, which],
                )
            )
        return copies

    row = lax.broadcasted_iota(jnp.int32, (room, tok_rows), 0).astype(jnp.float32)

    def read_places():
        for which in range(2):
            bit = plan.leaf[which]

            @pl.loop(0, side)
            def _(q):
                d = spread_index(q, bit, mine[bit])
                place = places[d]
                picks[which, q] = jnp.concatenate(
                    [jnp.where(place[k : k + 1, :] == row, 1.0, 0.0) for k in rows_of(which)],
                    axis=0,
                ).astype(jnp.bfloat16)

    def read_factors():
        @pl.loop(0, blocks)
        def _(d):
            own = places[d][0:1, :] == row
            total = squares[0, pl.ds(d, 1), :] + squares[1, pl.ds(d, 1), :]
            line = lax.rsqrt(total / (2 * half) + EPS)
            factor = jnp.sum(jnp.where(own, line, 0.0), axis=1, keepdims=True)
            rows = pl.ds(pl.multiple_of(d * room, room), room)
            scale[rows, :] = jnp.broadcast_to(factor, (room, wide))

    def pick(which, j):
        for copy in weight_copies(j):
            copy.start()
        for r in range(2):
            send(which, plan.stages - 1, r, j).wait()

        @pl.loop(0, side, unroll=8)
        def _(q):
            there = held[(j % plan.held_ring,) + tuple(digits(q, plan.stages))]
            taken = jnp.dot(picks[which, q], there, preferred_element_type=jnp.float32)
            taken = taken.astype(jnp.bfloat16)
            keep[j % near, q] = taken[:room]
            for k in range(3):
                give[j % near, k, q] = taken[(k + 1) * room : (k + 2) * room]

        for copy in last_copies(which, j):
            copy.start()

    def multiply(which, j):
        for copy in last_copies(which, j):
            copy.wait()
        for copy in weight_copies(j):
            copy.wait()
        bit = plan.leaf[which]
        places = [
            pl.ds(pl.multiple_of(owner * half + j * wide, wide), wide) for owner in (seg, 1 - seg)
        ]
        factors = [[gains[pl.ds(section, 1), place] for place in places] for section in range(2)]

        @pl.loop(0, side, unroll=2)
        def _(q):
            for own, sources in (
                (mine[bit], (keep.at[j % near, q], got.at[j % plan.last_ring, 0, q])),
                (1 - mine[bit], (got.at[j % plan.last_ring, 1, q], got.at[j % plan.last_ring, 2, q])),
            ):
                base = spread_index(q, bit, own) * room
                factor = scale[pl.ds(pl.multiple_of(base, room), room), :]
                for f, source in enumerate(sources):
                    scaled = source[...].astype(jnp.float32) * factor
                    for section in range(2):
                        to = pl.ds(pl.multiple_of(section * slot_rows + base, room), room)
                        lhs[to, pl.ds(f * wide, wide)] = (scaled * factors[section][f]).astype(
                            jnp.bfloat16
                        )

        for section in range(2):
            rows = pl.ds(section * slot_rows, slot_rows)
            hid[rows, :] += jnp.dot(
                lhs[rows, :], w_buf[j % near], preferred_element_type=jnp.float32
            )

    def clear():
        @pl.loop(0, 2 * slot_rows // tile)
        def _(r):
            rows = pl.ds(pl.multiple_of(r * tile, tile), tile)
            hid[rows, :] = jnp.zeros((tile, 2 * units), jnp.float32)

    def activate():
        @pl.loop(0, 2 * slot_rows // tile)
        def _(r):
            rows = pl.ds(pl.multiple_of(r * tile, tile), tile)
            gate = hid[rows, :units]
            act[rows, :] = (gate / (1.0 + jnp.exp(-gate)) * hid[rows, units:]).astype(jnp.bfloat16)

    steps = [(0, by_parity(first_send))]
    for t in range(1, plan.stages):
        steps.append((plan.gap * t, by_parity(functools.partial(relay, t))))
    steps += [(plan.pick_lag, by_parity(pick)), (plan.multiply_lag, by_parity(multiply))]
    return steps, read_places, read_factors, clear, activate


def column_sum(values):
    return jnp.sum(values, axis=1, keepdims=True)


def fused_kernel(plan, room, capacity, sizes, *refs):
    (x, gain, gain2, ids, copies, later_ids, table, router_in, router2_in, w_in, w_out) = refs[:11]
    states, ratio = refs[11:13]
    n_own, n_gather, n_back, n_gather_sems = sizes
    own = refs[13 : 13 + n_own]
    whole, gain_got, gains, act, mixed, squares, normed, score, score_got = own[:9]
    router, router2, spots, weights, places, gates, wide, w_ring, halves = own[9:]
    refs = refs[13 + n_own :]
    gather_landing, refs = refs[:n_gather], refs[n_gather:]
    back, sems = refs[:n_back], refs[n_back:]
    swap_sems, load_sems, share_sems, sems = sems[:2], sems[2], sems[3:5], sems[5:]
    gather_sems, return_sems = sems[:n_gather_sems], sems[n_gather_sems:]
    seg = lax.axis_index("segment")
    me = lax.axis_index("expert")
    mine = [bit_of(me, bit) for bit in range(plan.count)]
    blocks = plan.blocks
    count = plan.count
    tok_rows, half = x.shape
    full = 2 * half
    top = ids.shape[0]
    tiles = full // LANES
    slot_count = table.shape[1]
    f32 = jnp.float32
    partner = (1 - seg, me)
    at_home = tuple(reversed(mine))

    def tile_at(i):
        return pl.ds(pl.multiple_of(i * LANES, LANES), LANES)

    own_columns = pl.ds(pl.multiple_of(seg * half, half), half)
    swap_x = remote(x, whole.at[:, own_columns], swap_sems[0].at[0], swap_sems[1].at[0], partner)
    swap_gain = remote(gain, gain_got, swap_sems[0].at[1], swap_sems[1].at[1], partner)
    swap_halves = remote(
        halves.at[0], halves.at[1], swap_sems[0].at[3], swap_sems[1].at[3], partner
    )
    swap_score = remote(score, score_got, swap_sems[0].at[2], swap_sems[1].at[2], partner)
    load_router = pltpu.make_async_copy(router_in, router, load_sems.at[0])
    load_router2 = pltpu.make_async_copy(router2_in, router2, load_sems.at[1])

    def load_w_out(j):
        columns = pl.ds(pl.multiple_of(j * 2 * LANES, 2 * LANES), 2 * LANES)
        return pltpu.make_async_copy(
            w_out.at[:, columns], w_ring.at[j % 3], load_sems.at[2 + j % 3]
        )

    back_chunks = full // (2 * LANES)

    def weight_of(j):
        load_w_out(j).wait()

        @pl.when(j + 2 < back_chunks)
        def _():
            load_w_out(j + 2).start()

        return w_ring.at[j % 3]

    def share(kind, bit):
        ref = (spots, weights)[kind]
        index = tuple(slice(None) if d < bit else mine[d] for d in reversed(range(count)))
        return remote(
            ref.at[index],
            ref.at[index],
            share_sems[0].at[kind, bit],
            share_sems[1].at[kind, bit],
            (seg, flip(me, bit)),
        )

    def matches():
        line = table[...].astype(f32)
        i_row = lax.broadcasted_iota(jnp.int32, (slot_count, slot_count), 0)
        i_col = lax.broadcasted_iota(jnp.int32, (slot_count, slot_count), 1)
        column = column_sum(jnp.where(i_row == i_col, line, 0.0))
        same = column == line
        rank = column_sum(jnp.where(same & (i_col < i_row), 1.0, 0.0))
        holders = column_sum(jnp.where(same, 1.0, 0.0))
        wanted = ids[...].astype(f32)
        choice = copies[...].astype(f32)
        of_two = choice - 2.0 * jnp.floor(choice * 0.5)
        of_three = choice - 3.0 * jnp.floor((choice + 0.5) * (1.0 / 3.0))
        found = []
        for k in range(top):
            turn = jnp.where(
                holders == 1.0,
                0.0,
                jnp.where(holders == 2.0, of_two[k : k + 1, :], of_three[k : k + 1, :]),
            )
            found.append((column == wanted[k : k + 1, :]) & (rank == turn))
        return wanted, found

    def place_tokens():
        hit = jnp.zeros((slot_count, tok_rows), f32)
        for match in matches()[1]:
            hit += jnp.where(match, 1.0, 0.0)
        t_row = lax.broadcasted_iota(jnp.int32, (tok_rows, tok_rows), 0)
        t_col = lax.broadcasted_iota(jnp.int32, (tok_rows, tok_rows), 1)
        earlier = jnp.where(t_row < t_col, 1.0, 0.0).astype(jnp.bfloat16)
        before = jnp.dot(hit.astype(jnp.bfloat16), earlier, preferred_element_type=f32)
        place = jnp.where((hit > 0.0) & (before < capacity), before, -1.0)
        total = jnp.zeros((tok_rows, LANES), f32)
        for i in range(half // LANES):
            part = x[:, i * LANES : (i + 1) * LANES].astype(f32)
            total += part * part
        rest = jnp.broadcast_to(column_sum(total), (tok_rows, LANES)).T[0:1, :]
        rows = [place]
        for _ in range(3):
            rows.append(rest.astype(jnp.bfloat16).astype(f32))
            rest = rest - rows[-1]
        rows.append(jnp.zeros((EXTRA_ROWS - 3, tok_rows), f32))
        spots[at_home] = jnp.concatenate(rows, axis=0).astype(jnp.bfloat16)

    def normalize():
        total = jnp.zeros((tok_rows, LANES), f32)
        for i in range(tiles):
            part = whole[:, i * LANES : (i + 1) * LANES].astype(f32)
            total += part * part
        return lax.rsqrt(column_sum(total) / full + EPS)

    def prologue():
        swap_x.wait()
        squares[...] = jnp.broadcast_to(normalize(), (tok_rows, LANES))

        @pl.loop(0, tiles)
        def _(i):
            part = whole[:, tile_at(i)].astype(f32) * squares[...]
            normed[:, tile_at(i)] = (part * gains[1:2, tile_at(i)]).astype(jnp.bfloat16)

    def weigh_tokens():
        load_router.wait()
        logits = lax.dot_general(
            router[...], normed[...], (((1,), (1,)), ((), ())), preferred_element_type=f32
        )
        names = lax.broadcasted_iota(jnp.int32, logits.shape, 0).astype(f32)
        wanted, found = matches()
        chosen = [
            jnp.sum(jnp.where(names == wanted[k : k + 1, :], logits, 0.0), axis=0, keepdims=True)
            for k in range(top)
        ]
        most = functools.reduce(jnp.maximum, chosen)
        lifted = [jnp.exp(value - most) for value in chosen]
        weight = functools.reduce(jnp.add, lifted)
        gate = jnp.zeros((slot_count, tok_rows), f32)
        for k in range(top):
            rounded = (lifted[k] / weight).astype(jnp.bfloat16).astype(f32)
            gate += jnp.where(found[k], rounded, 0.0)
        weights[at_home] = gate.astype(jnp.bfloat16)

    def widen(kind):
        source, target = (spots, weights)[kind], (places, gates)[kind]

        @pl.loop(0, blocks)
        def _(d):
            wide[kind, : source.shape[-2]] = source[tuple(digits(d, count))].astype(f32)
            for k, slot in enumerate(slots_of(plan, seg, me)):
                target[d, k : k + 1, :] = wide[kind, pl.ds(slot, 1), :]
            if kind == 0:
                extra = wide[kind, slot_count : slot_count + 8, :]
                halves[0, pl.ds(d, 1), :] = jnp.sum(extra, axis=0, keepdims=True)

    def pass_on(kind, bit):
        if bit:
            share(kind, bit - 1).wait()
        share(kind, bit).start()

    def combine_weights():
        share(1, count - 1).wait()
        widen(1)
        make_weights(plan, me, room, places, gates, back[0])

    def begin_weights():
        weigh_tokens()
        pass_on(1, 0)

    def gather_part(*local):
        steps, read_places, read_factors, clear, activate = gather_steps(
            plan, seg, me, x, places, halves, gains, w_in, act, gather_landing + local, gather_sems
        )

        def take_places():
            share(0, count - 1).wait()
            widen(0)
            swap_halves.start()
            read_places()

        def take_factors():
            swap_gain.wait()
            gains[0:1, :] = gain_got[...].astype(f32)
            swap_halves.wait()
            read_factors()

        place_tokens()
        whole[:, own_columns] = x[...]
        gains[1:2, :] = gain[...].astype(f32)
        clear()
        pl.semaphore_wait(barrier, len(friends))
        swap_x.start()
        swap_gain.start()
        share(0, 0).start()
        late = {bit - 1: functools.partial(pass_on, 0, bit) for bit in range(1, count)}
        last = half // LANES + plan.multiply_lag - 1
        pace = min(3, (last - count) // count)
        late[count - 1] = prologue
        late[count] = begin_weights
        for bit in range(1, count):
            late[count + pace * bit] = functools.partial(pass_on, 1, bit)
        late[count + pace * count] = combine_weights
        early = {plan.pick_lag: take_places, plan.multiply_lag: take_factors}
        run_stages(half // LANES, steps, early, late)
        activate()

    def finish(rows, columns, total):
        value = whole[rows, columns].astype(f32) + total
        mixed[rows, columns] = value
        states[rows, columns] = value.astype(jnp.bfloat16)
        squares[rows, :] += value * value

    def return_part(*local):
        steps = return_steps(plan, seg, me, act, weight_of, finish, back, local, return_sems)
        run_stages(back_chunks, steps, {}, {})

    barrier = pltpu.get_barrier_semaphore()
    friends = near_friends(plan, seg, me)
    for friend in friends:
        pl.semaphore_signal(barrier, inc=1, device_id=friend, device_id_type=MESH)
    load_router.start()
    load_router2.start()
    load_w_out(0).start()
    load_w_out(1).start()
    pl.run_scoped(gather_part, *gather_scratch(plan, room, tok_rows, act.shape[1])[1])
    squares[...] = jnp.zeros((tok_rows, LANES), f32)
    pl.run_scoped(return_part, *return_scratch(plan, room, tok_rows)[1])
    inverse = lax.rsqrt(column_sum(squares[...]) / full + EPS)
    squares[...] = jnp.broadcast_to(inverse, (tok_rows, LANES))

    @pl.loop(0, tiles)
    def _(i):
        part = mixed[:, tile_at(i)] * squares[...]
        normed[:, tile_at(i)] = (part * gain2[:, tile_at(i)].astype(f32)).astype(jnp.bfloat16)

    load_router2.wait()
    logits = lax.dot_general(
        router2[...], normed[...], (((1,), (1,)), ((), ())), preferred_element_type=f32
    )
    shifted = logits - jnp.max(logits, axis=0, keepdims=True)
    logp = shifted - jnp.log(jnp.sum(jnp.exp(shifted), axis=0, keepdims=True))
    names = lax.broadcasted_iota(jnp.int32, logits.shape, 0).astype(f32)
    wanted = later_ids[...].astype(f32)
    total = jnp.zeros((1, tok_rows), f32)
    for k in range(top):
        total += jnp.sum(jnp.where(names == wanted[k : k + 1, :], logp, 0.0), axis=0, keepdims=True)
    score[...] = jnp.broadcast_to(total, score.shape)
    swap_score.start()
    swap_score.wait()
    sign = (2 * seg - 1).astype(f32)
    difference = (score[0:1, :] - score_got[0:1, :]) * sign
    turned = jnp.broadcast_to(difference, (tok_rows, tok_rows)).T
    t_row = lax.broadcasted_iota(jnp.int32, (tok_rows, tok_rows), 0)
    t_col = lax.broadcasted_iota(jnp.int32, (tok_rows, tok_rows), 1)
    picked = jnp.sum(jnp.where(t_row == 2 * t_col + seg, turned, 0.0), axis=0, keepdims=True)
    ratio[...] = picked[:, : tok_rows // 2]


def fused_scratch(plan, room, tok_rows, half, slot_count, units, experts):
    full = 2 * half
    rows = 2 * plan.blocks * room
    low = (2,) * plan.count

    def bf(*shape):
        return pltpu.VMEM(shape, jnp.bfloat16)

    def f32(*shape):
        return pltpu.VMEM(shape, jnp.float32)

    own = [
        bf(tok_rows, full),
        bf(1, full),
        f32(2, full),
        bf(rows, units),
        f32(tok_rows, full),
        f32(tok_rows, LANES),
        bf(tok_rows, full),
        f32(8, tok_rows),
        f32(8, tok_rows),
        bf(experts, full),
        bf(experts, full),
        bf(*low, slot_count + EXTRA_ROWS, tok_rows),
        bf(*low, slot_count, tok_rows),
        f32(plan.blocks, 8, tok_rows),
        f32(plan.blocks, 8, tok_rows),
        f32(2, slot_count + EXTRA_ROWS, tok_rows),
        bf(3, units, 2 * LANES),
        f32(2, plan.blocks, tok_rows),
    ]
    gather, _, gather_sems = gather_scratch(plan, room, tok_rows, units)
    back, _, back_sems = return_scratch(plan, room, tok_rows)
    shapes = ((4,), (4,), (5,), (2, plan.count), (2, plan.count))
    swap = [pltpu.SemaphoreType.DMA(shape) for shape in shapes]
    sizes = (len(own), len(gather), len(back), len(gather_sems))
    return own + gather + back, swap + gather_sems + back_sems, sizes


def fused_call(plan, room, capacity, scratch, sems, sizes, *args):
    tok_rows, half = args[0].shape
    vmem = pl.BlockSpec(memory_space=pltpu.VMEM)
    anywhere = pl.BlockSpec(memory_space=pl.ANY)
    return pl.pallas_call(
        functools.partial(fused_kernel, plan, room, capacity, sizes),
        out_shape=(
            jax.ShapeDtypeStruct((tok_rows, 2 * half), jnp.bfloat16),
            jax.ShapeDtypeStruct((1, tok_rows // 2), jnp.float32),
        ),
        in_specs=[vmem] * 7 + [anywhere] * 4,
        out_specs=(vmem, vmem),
        scratch_shapes=scratch + sems,
        compiler_params=pltpu.CompilerParams(
            collective_id=0, has_side_effects=True, vmem_limit_bytes=VMEM_MOST
        ),
        name="fused_layer",
    )(*args)


def per_device(
    rollout,
    norm_gain,
    router_first,
    gain_second,
    router_second,
    expert_ids,
    copy_pick,
    later_ids,
    slot_table,
    expert_in,
    expert_out,
):
    segment_count = lax.axis_size("segment")
    chip_count = lax.axis_size("expert")
    tok_rows, half = rollout.shape
    capacity = 3 * tok_rows * expert_ids.shape[1] // (2 * segment_count * chip_count)
    plan = Plan(grid_sides(chip_count))
    room = -(-capacity // 16) * 16
    scratch, sems, sizes = fused_scratch(
        plan,
        room,
        tok_rows,
        half,
        slot_table.shape[0],
        expert_out.shape[1],
        router_first.shape[2],
    )
    states, column = fused_call(
        plan,
        room,
        capacity,
        scratch,
        sems,
        sizes,
        rollout,
        norm_gain,
        gain_second,
        expert_ids.T,
        copy_pick.T,
        later_ids.T,
        slot_table[None, :],
        router_first[0].T,
        router_second[0].T,
        expert_in[0],
        expert_out[0],
    )
    return states[None], column.reshape(-1, 1)


def solution(mesh):
    in_specs = (
        P("expert", "segment"),
        P("segment", None),
        P("segment", None, None),
        P("segment", None),
        P("segment", None, None),
        P("expert", None),
        P("expert", None),
        P("expert", None),
        P(),
        P(("segment", "expert"), None, None),
        P(("segment", "expert"), None, None),
    )
    out_specs = (P("segment", "expert", None), P("expert", "segment"))
    return jax.shard_map(
        per_device, mesh=mesh, in_specs=in_specs, out_specs=out_specs, check_vma=False
    )
```

```python
import functools
import math

import jax
import jax.numpy as jnp
from jax import lax
from jax.experimental import pallas as pl
from jax.experimental.pallas import tpu as pltpu
from jax.sharding import PartitionSpec as P

LANES = 128
VMEM_MOST = 67043328
MESH = pl.DeviceIdType.MESH
EPS = 1e-06
RING = 4
GAPS = (3, 3, 3)
LAST_GAP = 3
EXTRA_ROWS = 16


def grid_sides(count):
    outer = 1
    while outer**3 < count:
        outer *= 2
    rest = count // outer
    middle = 1
    while middle**2 < rest:
        middle *= 2
    return outer, middle, rest // middle


class Plan:
    def __init__(self, sides):
        logs = [side.bit_length() - 1 for side in sides]
        n_a, n_b, n_c = logs
        bits_c = list(range(n_c))
        bits_b = list(range(n_c, n_c + n_b))
        bits_a = list(range(n_c + n_b, n_c + n_b + n_a))
        self.count = n_a + n_b + n_c
        self.blocks = 1 << self.count
        self.leaf = (bits_c[0], bits_b[0])
        orders = (
            (bits_c + bits_a + bits_b, bits_c + bits_b + bits_a),
            (bits_b + bits_a + bits_c, bits_b + bits_c + bits_a),
        )
        self.rest = [[order[1:] for order in pair] for pair in orders]
        self.stages = self.count - 1
        short = self.stages == len(GAPS)
        gaps = GAPS if short else (1,) * self.stages
        self.lags = [sum(gaps[:t]) for t in range(self.stages + 1)]
        self.gap = max(gaps)
        self.last_gap = LAST_GAP if short else 2
        self.pick_lag = self.lags[-1]
        self.multiply_lag = self.pick_lag + self.last_gap
        self.stage_ring = self.ring(self.gap, self.gap)
        self.held_ring = self.ring(self.pick_lag, self.gap)
        self.last_ring = self.ring(self.last_gap, self.last_gap)

    def ring(self, busy, gap):
        ahead = busy + 1 + (busy + 1) % 2
        return ahead + 1 + gap + (ahead + 1 + gap) % 2

    def split(self, rows):
        part = max(3 * rows // 8 // 16 * 16, 16)
        return part, rows - part

    def dims(self, which, order, done):
        used = [self.leaf[which]] + self.rest[which][order][:done]
        return [bit for bit in reversed(range(self.count)) if bit not in used]


def bit_of(index, bit):
    return (index // (1 << bit)) % 2


def flip(index, bit):
    return index + (1 << bit) * (1 - 2 * bit_of(index, bit))


def digits(value, count):
    return [(value // (1 << (count - 1 - i))) % 2 for i in range(count)]


def spread_index(value, bit, own):
    low = 1 << bit
    return (value // low) * (2 * low) + own * low + value % low


def remote(src, dst, send, recv, peer):
    return pltpu.make_async_remote_copy(
        src_ref=src,
        dst_ref=dst,
        send_sem=send,
        recv_sem=recv,
        device_id=peer,
        device_id_type=MESH,
    )


def run_stages(chunks, stages, early, late):
    depth = max(lag for lag, _ in stages)

    @pl.loop(0, chunks + depth)
    def _(step):
        for lag, stage in stages:
            if lag in early:

                @pl.when(step == lag)
                def _():
                    early[lag]()

            @pl.when((step >= lag) & (step - lag < chunks))
            def _():
                stage(step - lag)

        for when, hook in late.items():

            @pl.when(step == when)
            def _():
                hook()


def by_parity(stage):
    def run(j):
        for which in range(2):

            @pl.when(j % 2 == which)
            def _():
                stage(which, j)

    return run


def near_friends(plan, seg, me):
    friends = [(1 - seg, me)] + [(seg, flip(me, bit)) for bit in range(plan.count)]
    return friends + [(1 - seg, flip(me, bit)) for bit in plan.leaf]


def slots_of(plan, seg, me):
    chips = [me] + [flip(me, bit) for bit in plan.leaf]
    return [core * plan.blocks + chip for chip in chips for core in (seg, 1 - seg)]


def rows_of(which):
    return (0, 1, 2 + 2 * which, 3 + 2 * which)


def make_weights(plan, me, room, places, gates, wts):
    tok_rows = places.shape[-1]
    row = lax.broadcasted_iota(jnp.int32, (room, tok_rows), 0).astype(jnp.float32)
    for which in range(2):
        bit = plan.leaf[which]

        @pl.loop(0, plan.blocks // 2)
        def _(q):
            d = spread_index(q, bit, bit_of(me, bit))
            place, gate = places[d], gates[d]
            pieces = []
            for k in rows_of(which):
                hit = place[k : k + 1, :] == row
                pieces.append(jnp.where(hit, gate[k : k + 1, :], 0.0))
            pad = -(4 * room) % LANES
            if pad:
                pieces.append(jnp.zeros((pad, tok_rows), jnp.float32))
            turned = jnp.concatenate(pieces, axis=0).T
            wts[which, q] = turned[:, : 4 * room].astype(jnp.bfloat16)


def return_scratch(plan, room, tok_rows):
    def bf(*shape):
        return pltpu.VMEM(shape, jnp.bfloat16)

    def dma(*shape):
        return pltpu.SemaphoreType.DMA(shape)

    side = plan.blocks // 2
    low = (2,) * plan.stages
    split = plan.split(tok_rows)
    landing = [
        bf(2, side, tok_rows, 4 * room),
        bf(RING, 2, 2, *low, room, LANES),
        bf(RING, 2, *low, room, LANES),
    ]
    local = [
        bf(2, 2, 2, *((2,) * plan.count), room, LANES),
        bf(2, 2, *low, tok_rows, LANES),
    ]
    sems = [dma(2, 2, 3), dma(RING, 2, 3)]
    for t in range(plan.stages):
        for rows in split:
            left = (2,) * (plan.stages - 1 - t)
            landing.append(bf(RING, 2, *left, rows, LANES))
            if t + 1 < plan.stages:
                local.append(bf(2, 2, *left, rows, LANES))
        sems += [dma(2, 2, 2), dma(RING, 2, 2)]
    return landing, local, sems


def return_steps(plan, seg, me, act, weight_of, finish, landing, local, sems):
    wts, leaf, swapped = landing[:3]
    ys, first = local[:2]
    stages = plan.stages
    arrived = [landing[3 + 2 * t : 5 + 2 * t] for t in range(stages)]
    parts = [local[2 + 2 * t : 4 + 2 * t] for t in range(stages - 1)]
    side = plan.blocks // 2
    room = ys.shape[-2]
    slot_rows = plan.blocks * room
    tok_rows = first.shape[-2]
    split = plan.split(tok_rows)
    spans = (pl.ds(0, split[0]), pl.ds(split[0], split[1]))
    mine = [bit_of(me, bit) for bit in range(plan.count)]

    def region(which, own):
        bit = plan.leaf[which]
        place = plan.count - 1 - bit
        return tuple(
            (mine[bit] if own else 1 - mine[bit]) if i == place else slice(None)
            for i in range(plan.count)
        )

    def first_copies(which, j):
        nbr = flip(me, plan.leaf[which])
        sources = (
            (ys.at[(j % 2, which, 1) + region(which, False)], leaf.at[j % RING, which, 0], (seg, nbr)),
            (ys.at[(j % 2, which, 0) + region(which, False)], leaf.at[j % RING, which, 1], (1 - seg, nbr)),
            (ys.at[(j % 2, which, 0) + region(which, True)], swapped.at[j % RING, which], (1 - seg, me)),
        )
        return [
            remote(src, dst, sems[0].at[j % 2, which, k], sems[1].at[j % RING, which, k], peer)
            for k, (src, dst, peer) in enumerate(sources)
        ]

    def held_at(which, t, r, j, index):
        if t == 0:
            return (j % 2, which) + index + (spans[r],)
        return (j % 2, which) + index

    def send(which, t, r, j):
        bit = plan.rest[which][r][t]
        dims = plan.dims(which, r, t)
        index = tuple(1 - mine[d] if d == bit else slice(None) for d in dims)
        source = first if t == 0 else parts[t - 1][r]
        return remote(
            source.at[held_at(which, t, r, j, index)],
            arrived[t][r].at[j % RING, which],
            sems[2 + 2 * t].at[j % 2, which, r],
            sems[3 + 2 * t].at[j % RING, which, r],
            (seg, flip(me, bit)),
        )

    def project(j):
        weight = weight_of(j)
        blocks = (2,) * plan.count
        for section in range(2):
            result = jnp.dot(
                act[pl.ds(section * slot_rows, slot_rows), :],
                weight[...],
                preferred_element_type=jnp.float32,
            ).astype(jnp.bfloat16)
            for which in range(2):
                half = result[:, which * LANES : (which + 1) * LANES]
                ys[j % 2, which, section] = half.reshape(blocks + (room, LANES))
        for which in range(2):
            for copy in first_copies(which, j):
                copy.start()

    def combine(j):
        for which in range(2):
            for copy in first_copies(which, j):
                copy.wait()
            own = mine[plan.leaf[which]]
            place = plan.count - 1 - plan.leaf[which]

            @pl.loop(0, side, unroll=8)
            def _(q):
                ix = digits(q, stages)
                full = tuple(ix[:place] + [own] + ix[place:])
                ix = tuple(ix)
                both = jnp.concatenate(
                    [
                        ys[(j % 2, which, 1) + full],
                        swapped[(j % RING, which) + ix],
                        leaf[(j % RING, which, 0) + ix],
                        leaf[(j % RING, which, 1) + ix],
                    ],
                    axis=0,
                )
                part = jnp.dot(wts[which, q], both, preferred_element_type=jnp.float32)
                first[(j % 2, which) + ix] = part.astype(jnp.bfloat16)

            for r in range(2):
                send(which, 0, r, j).start()

    def reduce_stage(t, j):
        last = t == stages - 1
        left = stages - 1 - t
        for which in range(2):
            for r in range(2):
                send(which, t, r, j).wait()
                bit = plan.rest[which][r][t]
                place = plan.dims(which, r, t).index(bit)
                source = first if t == 0 else parts[t - 1][r]

                def total(ix):
                    full = tuple(ix[:place] + [mine[bit]] + ix[place:])
                    held = source[held_at(which, t, r, j, full)]
                    came = arrived[t][r][(j % RING, which) + tuple(ix)]
                    return held.astype(jnp.float32) + came.astype(jnp.float32)

                if last:
                    start = pl.multiple_of((2 * j + which) * LANES, LANES)
                    finish(spans[r], pl.ds(start, LANES), total([]))
                else:

                    @pl.loop(0, 1 << left, unroll=2)
                    def _(e):
                        ix = digits(e, left)
                        parts[t][r][(j % 2, which) + tuple(ix)] = total(ix).astype(jnp.bfloat16)

                    send(which, t + 1, r, j).start()

    steps = [(0, project), (1, combine)]
    for t in range(stages):
        steps.append((2 + t, functools.partial(reduce_stage, t)))
    return steps


def gather_scratch(plan, room, tok_rows, units):
    def bf(*shape):
        return pltpu.VMEM(shape, jnp.bfloat16)

    def f32(*shape):
        return pltpu.VMEM(shape, jnp.float32)

    def dma(*shape):
        return pltpu.SemaphoreType.DMA(shape)

    blocks = plan.blocks
    side = blocks // 2
    slot_rows = blocks * room
    near = plan.last_gap + 1
    landing = [
        bf(plan.held_ring, *((2,) * plan.stages), tok_rows, LANES),
        bf(plan.last_ring, 3, side, room, LANES),
    ]
    local = [
        bf(2, side, 4 * room, tok_rows),
        f32(slot_rows, LANES),
        bf(near, side, room, LANES),
        bf(near, 3, side, room, LANES),
        bf(2 * slot_rows, 2 * LANES),
        f32(2 * slot_rows, 2 * units),
        bf(near, 2 * LANES, 2 * units),
    ]
    sems = [dma(near, 3), dma(plan.last_ring, 3), dma(near, 2)]
    for _ in range(plan.stages):
        sems += [dma(plan.stage_ring, 2), dma(plan.stage_ring, 2)]
    return landing, local, sems


def gather_steps(plan, seg, me, x, places, squares, gains, w_in, act, scratch, sems):
    (held, got, picks, scale, keep, give, lhs, hid, w_buf) = scratch
    blocks = plan.blocks
    side = blocks // 2
    mine = [bit_of(me, bit) for bit in range(plan.count)]
    tok_rows, half = x.shape
    split = (tok_rows // 2, tok_rows // 2)
    spans = (pl.ds(0, split[0]), pl.ds(split[0], split[1]))
    wide = LANES
    room = keep.shape[-2]
    slot_rows = blocks * room
    units = act.shape[1]
    near = plan.last_gap + 1
    tile = math.gcd(slot_rows, 256)

    def columns(j):
        return pl.ds(pl.multiple_of(j * wide, wide), wide)

    def send(which, t, r, j):
        order = plan.rest[which][r]
        bit = order[plan.stages - 1 - t]
        free = order[plan.stages - t :]
        rows = spans[r]
        index = tuple(slice(None) if d in free else mine[d] for d in plan.dims(which, r, 0))
        dst = held.at[(j % plan.held_ring,) + index + (rows,)]
        return remote(
            x.at[rows, columns(j)] if t == 0 else dst,
            dst,
            sems[3 + 2 * t].at[j % plan.stage_ring, r],
            sems[4 + 2 * t].at[j % plan.stage_ring, r],
            (seg, flip(me, bit)),
        )

    def first_send(which, j):
        for r in range(2):
            send(which, 0, r, j).start()
        index = tuple(mine[d] for d in plan.dims(which, 0, 0))
        held[(j % plan.held_ring,) + index] = x[:, columns(j)]

    def relay(t, which, j):
        for r in range(2):
            send(which, t - 1, r, j).wait()
            send(which, t, r, j).start()

    def last_copies(which, j):
        nbr = flip(me, plan.leaf[which])
        peers = ((1 - seg, me), (seg, nbr), (1 - seg, nbr))
        return [
            remote(
                give.at[j % near, k],
                got.at[j % plan.last_ring, k],
                sems[0].at[j % near, k],
                sems[1].at[j % plan.last_ring, k],
                peer,
            )
            for k, peer in enumerate(peers)
        ]

    def weight_copies(j):
        copies = []
        for which, owner in enumerate((seg, 1 - seg)):
            rows = pl.ds(pl.multiple_of(owner * half + j * wide, wide), wide)
            copies.append(
                pltpu.make_async_copy(
                    w_in.at[rows, :],
                    w_buf.at[j % near, pl.ds(which * wide, wide)],
                    sems[2].at[j % near, which],
                )
            )
        return copies

    row = lax.broadcasted_iota(jnp.int32, (room, tok_rows), 0).astype(jnp.float32)

    def read_places():
        for which in range(2):
            bit = plan.leaf[which]

            @pl.loop(0, side)
            def _(q):
                d = spread_index(q, bit, mine[bit])
                place = places[d]
                picks[which, q] = jnp.concatenate(
                    [jnp.where(place[k : k + 1, :] == row, 1.0, 0.0) for k in rows_of(which)],
                    axis=0,
                ).astype(jnp.bfloat16)

    def read_factors():
        @pl.loop(0, blocks)
        def _(d):
            own = places[d][0:1, :] == row
            total = squares[0, pl.ds(d, 1), :] + squares[1, pl.ds(d, 1), :]
            line = lax.rsqrt(total / (2 * half) + EPS)
            factor = jnp.sum(jnp.where(own, line, 0.0), axis=1, keepdims=True)
            rows = pl.ds(pl.multiple_of(d * room, room), room)
            scale[rows, :] = jnp.broadcast_to(factor, (room, wide))

    def pick(which, j):
        for copy in weight_copies(j):
            copy.start()
        for r in range(2):
            send(which, plan.stages - 1, r, j).wait()

        @pl.loop(0, side, unroll=8)
        def _(q):
            there = held[(j % plan.held_ring,) + tuple(digits(q, plan.stages))]
            taken = jnp.dot(picks[which, q], there, preferred_element_type=jnp.float32)
            taken = taken.astype(jnp.bfloat16)
            keep[j % near, q] = taken[:room]
            for k in range(3):
                give[j % near, k, q] = taken[(k + 1) * room : (k + 2) * room]

        for copy in last_copies(which, j):
            copy.start()

    def multiply(which, j):
        for copy in last_copies(which, j):
            copy.wait()
        for copy in weight_copies(j):
            copy.wait()
        bit = plan.leaf[which]
        places = [
            pl.ds(pl.multiple_of(owner * half + j * wide, wide), wide) for owner in (seg, 1 - seg)
        ]
        factors = [[gains[pl.ds(section, 1), place] for place in places] for section in range(2)]

        @pl.loop(0, side, unroll=2)
        def _(q):
            for own, sources in (
                (mine[bit], (keep.at[j % near, q], got.at[j % plan.last_ring, 0, q])),
                (1 - mine[bit], (got.at[j % plan.last_ring, 1, q], got.at[j % plan.last_ring, 2, q])),
            ):
                base = spread_index(q, bit, own) * room
                factor = scale[pl.ds(pl.multiple_of(base, room), room), :]
                for f, source in enumerate(sources):
                    scaled = source[...].astype(jnp.float32) * factor
                    for section in range(2):
                        to = pl.ds(pl.multiple_of(section * slot_rows + base, room), room)
                        lhs[to, pl.ds(f * wide, wide)] = (scaled * factors[section][f]).astype(
                            jnp.bfloat16
                        )

        for section in range(2):
            rows = pl.ds(section * slot_rows, slot_rows)
            hid[rows, :] += jnp.dot(
                lhs[rows, :], w_buf[j % near], preferred_element_type=jnp.float32
            )

    def clear():
        @pl.loop(0, 2 * slot_rows // tile)
        def _(r):
            rows = pl.ds(pl.multiple_of(r * tile, tile), tile)
            hid[rows, :] = jnp.zeros((tile, 2 * units), jnp.float32)

    def activate():
        @pl.loop(0, 2 * slot_rows // tile)
        def _(r):
            rows = pl.ds(pl.multiple_of(r * tile, tile), tile)
            gate = hid[rows, :units]
            act[rows, :] = (gate / (1.0 + jnp.exp(-gate)) * hid[rows, units:]).astype(jnp.bfloat16)

    steps = [(0, by_parity(first_send))]
    for t in range(1, plan.stages):
        steps.append((plan.lags[t], by_parity(functools.partial(relay, t))))
    steps += [(plan.pick_lag, by_parity(pick)), (plan.multiply_lag, by_parity(multiply))]
    return steps, read_places, read_factors, clear, activate


def column_sum(values):
    return jnp.sum(values, axis=1, keepdims=True)


def fused_kernel(plan, room, capacity, sizes, *refs):
    (x, gain, gain2, ids, copies, later_ids, table, router_in, router2_in, w_in, w_out) = refs[:11]
    states, ratio = refs[11:13]
    n_own, n_gather, n_back, n_gather_sems = sizes
    own = refs[13 : 13 + n_own]
    whole, gain_got, gains, act, mixed, squares, normed, score, score_got = own[:9]
    router, router2, spots, weights, places, gates, wide, w_ring, halves = own[9:]
    refs = refs[13 + n_own :]
    gather_landing, refs = refs[:n_gather], refs[n_gather:]
    back, sems = refs[:n_back], refs[n_back:]
    swap_sems, load_sems, share_sems, sems = sems[:2], sems[2], sems[3:5], sems[5:]
    gather_sems, return_sems = sems[:n_gather_sems], sems[n_gather_sems:]
    seg = lax.axis_index("segment")
    me = lax.axis_index("expert")
    mine = [bit_of(me, bit) for bit in range(plan.count)]
    blocks = plan.blocks
    count = plan.count
    tok_rows, half = x.shape
    full = 2 * half
    top = ids.shape[0]
    tiles = full // LANES
    slot_count = table.shape[1]
    f32 = jnp.float32
    partner = (1 - seg, me)
    at_home = tuple(reversed(mine))

    def tile_at(i):
        return pl.ds(pl.multiple_of(i * LANES, LANES), LANES)

    own_columns = pl.ds(pl.multiple_of(seg * half, half), half)
    swap_x = remote(x, whole.at[:, own_columns], swap_sems[0].at[0], swap_sems[1].at[0], partner)
    swap_gain = remote(gain, gain_got, swap_sems[0].at[1], swap_sems[1].at[1], partner)
    swap_halves = remote(
        halves.at[0], halves.at[1], swap_sems[0].at[3], swap_sems[1].at[3], partner
    )
    swap_score = remote(score, score_got, swap_sems[0].at[2], swap_sems[1].at[2], partner)
    load_router = pltpu.make_async_copy(router_in, router, load_sems.at[0])
    load_router2 = pltpu.make_async_copy(router2_in, router2, load_sems.at[1])

    def load_w_out(j):
        columns = pl.ds(pl.multiple_of(j * 2 * LANES, 2 * LANES), 2 * LANES)
        return pltpu.make_async_copy(
            w_out.at[:, columns], w_ring.at[j % 3], load_sems.at[2 + j % 3]
        )

    back_chunks = full // (2 * LANES)

    def weight_of(j):
        load_w_out(j).wait()

        @pl.when(j + 2 < back_chunks)
        def _():
            load_w_out(j + 2).start()

        return w_ring.at[j % 3]

    def share(kind, bit):
        ref = (spots, weights)[kind]
        index = tuple(slice(None) if d < bit else mine[d] for d in reversed(range(count)))
        return remote(
            ref.at[index],
            ref.at[index],
            share_sems[0].at[kind, bit],
            share_sems[1].at[kind, bit],
            (seg, flip(me, bit)),
        )

    def matches():
        line = table[...].astype(f32)
        i_row = lax.broadcasted_iota(jnp.int32, (slot_count, slot_count), 0)
        i_col = lax.broadcasted_iota(jnp.int32, (slot_count, slot_count), 1)
        column = column_sum(jnp.where(i_row == i_col, line, 0.0))
        same = column == line
        rank = column_sum(jnp.where(same & (i_col < i_row), 1.0, 0.0))
        holders = column_sum(jnp.where(same, 1.0, 0.0))
        wanted = ids[...].astype(f32)
        choice = copies[...].astype(f32)
        of_two = choice - 2.0 * jnp.floor(choice * 0.5)
        of_three = choice - 3.0 * jnp.floor((choice + 0.5) * (1.0 / 3.0))
        found = []
        for k in range(top):
            turn = jnp.where(
                holders == 1.0,
                0.0,
                jnp.where(holders == 2.0, of_two[k : k + 1, :], of_three[k : k + 1, :]),
            )
            found.append((column == wanted[k : k + 1, :]) & (rank == turn))
        return wanted, found

    def place_tokens():
        hit = jnp.zeros((slot_count, tok_rows), f32)
        for match in matches()[1]:
            hit += jnp.where(match, 1.0, 0.0)
        t_row = lax.broadcasted_iota(jnp.int32, (tok_rows, tok_rows), 0)
        t_col = lax.broadcasted_iota(jnp.int32, (tok_rows, tok_rows), 1)
        earlier = jnp.where(t_row < t_col, 1.0, 0.0).astype(jnp.bfloat16)
        before = jnp.dot(hit.astype(jnp.bfloat16), earlier, preferred_element_type=f32)
        place = jnp.where((hit > 0.0) & (before < capacity), before, -1.0)
        total = jnp.zeros((tok_rows, LANES), f32)
        for i in range(half // LANES):
            part = x[:, i * LANES : (i + 1) * LANES].astype(f32)
            total += part * part
        rest = jnp.broadcast_to(column_sum(total), (tok_rows, LANES)).T[0:1, :]
        rows = [place]
        for _ in range(3):
            rows.append(rest.astype(jnp.bfloat16).astype(f32))
            rest = rest - rows[-1]
        rows.append(jnp.zeros((EXTRA_ROWS - 3, tok_rows), f32))
        spots[at_home] = jnp.concatenate(rows, axis=0).astype(jnp.bfloat16)

    def normalize():
        total = jnp.zeros((tok_rows, LANES), f32)
        for i in range(tiles):
            part = whole[:, i * LANES : (i + 1) * LANES].astype(f32)
            total += part * part
        return lax.rsqrt(column_sum(total) / full + EPS)

    def prologue():
        swap_x.wait()
        squares[...] = jnp.broadcast_to(normalize(), (tok_rows, LANES))

        @pl.loop(0, tiles)
        def _(i):
            part = whole[:, tile_at(i)].astype(f32) * squares[...]
            normed[:, tile_at(i)] = (part * gains[1:2, tile_at(i)]).astype(jnp.bfloat16)

    def weigh_tokens():
        load_router.wait()
        logits = lax.dot_general(
            router[...], normed[...], (((1,), (1,)), ((), ())), preferred_element_type=f32
        )
        names = lax.broadcasted_iota(jnp.int32, logits.shape, 0).astype(f32)
        wanted, found = matches()
        chosen = [
            jnp.sum(jnp.where(names == wanted[k : k + 1, :], logits, 0.0), axis=0, keepdims=True)
            for k in range(top)
        ]
        most = functools.reduce(jnp.maximum, chosen)
        lifted = [jnp.exp(value - most) for value in chosen]
        weight = functools.reduce(jnp.add, lifted)
        gate = jnp.zeros((slot_count, tok_rows), f32)
        for k in range(top):
            rounded = (lifted[k] / weight).astype(jnp.bfloat16).astype(f32)
            gate += jnp.where(found[k], rounded, 0.0)
        weights[at_home] = gate.astype(jnp.bfloat16)

    def widen(kind):
        source, target = (spots, weights)[kind], (places, gates)[kind]

        @pl.loop(0, blocks)
        def _(d):
            wide[kind, : source.shape[-2]] = source[tuple(digits(d, count))].astype(f32)
            for k, slot in enumerate(slots_of(plan, seg, me)):
                target[d, k : k + 1, :] = wide[kind, pl.ds(slot, 1), :]
            if kind == 0:
                extra = wide[kind, slot_count : slot_count + 8, :]
                halves[0, pl.ds(d, 1), :] = jnp.sum(extra, axis=0, keepdims=True)

    def pass_on(kind, bit):
        if bit:
            share(kind, bit - 1).wait()
        share(kind, bit).start()

    def combine_weights():
        share(1, count - 1).wait()
        widen(1)
        make_weights(plan, me, room, places, gates, back[0])

    def begin_weights():
        weigh_tokens()
        pass_on(1, 0)

    def gather_part(*local):
        steps, read_places, read_factors, clear, activate = gather_steps(
            plan, seg, me, x, places, halves, gains, w_in, act, gather_landing + local, gather_sems
        )

        def take_places():
            share(0, count - 1).wait()
            widen(0)
            swap_halves.start()
            read_places()

        def take_factors():
            swap_gain.wait()
            gains[0:1, :] = gain_got[...].astype(f32)
            swap_halves.wait()
            read_factors()

        place_tokens()
        whole[:, own_columns] = x[...]
        gains[1:2, :] = gain[...].astype(f32)
        clear()
        pl.semaphore_wait(barrier, len(friends))
        swap_x.start()
        swap_gain.start()
        share(0, 0).start()
        late = {plan.lags[bit] - 1: functools.partial(pass_on, 0, bit) for bit in range(1, count)}
        last = half // LANES + plan.multiply_lag - 1
        start = plan.pick_lag + 2
        pace = min(3, (last - start) // count)
        late[start - 1] = prologue
        late[start] = begin_weights
        for bit in range(1, count):
            late[start + pace * bit] = functools.partial(pass_on, 1, bit)
        late[start + pace * count] = combine_weights
        early = {plan.pick_lag: take_places, plan.multiply_lag: take_factors}
        run_stages(half // LANES, steps, early, late)
        activate()

    def finish(rows, columns, total):
        value = whole[rows, columns].astype(f32) + total
        mixed[rows, columns] = value
        states[rows, columns] = value.astype(jnp.bfloat16)
        squares[rows, :] += value * value

    def return_part(*local):
        steps = return_steps(plan, seg, me, act, weight_of, finish, back, local, return_sems)
        run_stages(back_chunks, steps, {}, {})

    barrier = pltpu.get_barrier_semaphore()
    friends = near_friends(plan, seg, me)
    for friend in friends:
        pl.semaphore_signal(barrier, inc=1, device_id=friend, device_id_type=MESH)
    load_router.start()
    load_router2.start()
    load_w_out(0).start()
    load_w_out(1).start()
    pl.run_scoped(gather_part, *gather_scratch(plan, room, tok_rows, act.shape[1])[1])
    squares[...] = jnp.zeros((tok_rows, LANES), f32)
    pl.run_scoped(return_part, *return_scratch(plan, room, tok_rows)[1])
    inverse = lax.rsqrt(column_sum(squares[...]) / full + EPS)
    squares[...] = jnp.broadcast_to(inverse, (tok_rows, LANES))

    @pl.loop(0, tiles)
    def _(i):
        part = mixed[:, tile_at(i)] * squares[...]
        normed[:, tile_at(i)] = (part * gain2[:, tile_at(i)].astype(f32)).astype(jnp.bfloat16)

    load_router2.wait()
    logits = lax.dot_general(
        router2[...], normed[...], (((1,), (1,)), ((), ())), preferred_element_type=f32
    )
    shifted = logits - jnp.max(logits, axis=0, keepdims=True)
    logp = shifted - jnp.log(jnp.sum(jnp.exp(shifted), axis=0, keepdims=True))
    names = lax.broadcasted_iota(jnp.int32, logits.shape, 0).astype(f32)
    wanted = later_ids[...].astype(f32)
    total = jnp.zeros((1, tok_rows), f32)
    for k in range(top):
        total += jnp.sum(jnp.where(names == wanted[k : k + 1, :], logp, 0.0), axis=0, keepdims=True)
    score[...] = jnp.broadcast_to(total, score.shape)
    swap_score.start()
    swap_score.wait()
    sign = (2 * seg - 1).astype(f32)
    difference = (score[0:1, :] - score_got[0:1, :]) * sign
    turned = jnp.broadcast_to(difference, (tok_rows, tok_rows)).T
    t_row = lax.broadcasted_iota(jnp.int32, (tok_rows, tok_rows), 0)
    t_col = lax.broadcasted_iota(jnp.int32, (tok_rows, tok_rows), 1)
    picked = jnp.sum(jnp.where(t_row == 2 * t_col + seg, turned, 0.0), axis=0, keepdims=True)
    ratio[...] = picked[:, : tok_rows // 2]


def fused_scratch(plan, room, tok_rows, half, slot_count, units, experts):
    full = 2 * half
    rows = 2 * plan.blocks * room
    low = (2,) * plan.count

    def bf(*shape):
        return pltpu.VMEM(shape, jnp.bfloat16)

    def f32(*shape):
        return pltpu.VMEM(shape, jnp.float32)

    own = [
        bf(tok_rows, full),
        bf(1, full),
        f32(2, full),
        bf(rows, units),
        f32(tok_rows, full),
        f32(tok_rows, LANES),
        bf(tok_rows, full),
        f32(8, tok_rows),
        f32(8, tok_rows),
        bf(experts, full),
        bf(experts, full),
        bf(*low, slot_count + EXTRA_ROWS, tok_rows),
        bf(*low, slot_count, tok_rows),
        f32(plan.blocks, 8, tok_rows),
        f32(plan.blocks, 8, tok_rows),
        f32(2, slot_count + EXTRA_ROWS, tok_rows),
        bf(3, units, 2 * LANES),
        f32(2, plan.blocks, tok_rows),
    ]
    gather, _, gather_sems = gather_scratch(plan, room, tok_rows, units)
    back, _, back_sems = return_scratch(plan, room, tok_rows)
    shapes = ((4,), (4,), (5,), (2, plan.count), (2, plan.count))
    swap = [pltpu.SemaphoreType.DMA(shape) for shape in shapes]
    sizes = (len(own), len(gather), len(back), len(gather_sems))
    return own + gather + back, swap + gather_sems + back_sems, sizes


def fused_call(plan, room, capacity, scratch, sems, sizes, *args):
    tok_rows, half = args[0].shape
    vmem = pl.BlockSpec(memory_space=pltpu.VMEM)
    anywhere = pl.BlockSpec(memory_space=pl.ANY)
    return pl.pallas_call(
        functools.partial(fused_kernel, plan, room, capacity, sizes),
        out_shape=(
            jax.ShapeDtypeStruct((tok_rows, 2 * half), jnp.bfloat16),
            jax.ShapeDtypeStruct((1, tok_rows // 2), jnp.float32),
        ),
        in_specs=[vmem] * 7 + [anywhere] * 4,
        out_specs=(vmem, vmem),
        scratch_shapes=scratch + sems,
        compiler_params=pltpu.CompilerParams(
            collective_id=0, has_side_effects=True, vmem_limit_bytes=VMEM_MOST
        ),
        name="fused_layer",
    )(*args)


def per_device(
    rollout,
    norm_gain,
    router_first,
    gain_second,
    router_second,
    expert_ids,
    copy_pick,
    later_ids,
    slot_table,
    expert_in,
    expert_out,
):
    segment_count = lax.axis_size("segment")
    chip_count = lax.axis_size("expert")
    tok_rows, half = rollout.shape
    capacity = 3 * tok_rows * expert_ids.shape[1] // (2 * segment_count * chip_count)
    plan = Plan(grid_sides(chip_count))
    room = -(-capacity // 16) * 16
    scratch, sems, sizes = fused_scratch(
        plan,
        room,
        tok_rows,
        half,
        slot_table.shape[0],
        expert_out.shape[1],
        router_first.shape[2],
    )
    states, column = fused_call(
        plan,
        room,
        capacity,
        scratch,
        sems,
        sizes,
        rollout,
        norm_gain,
        gain_second,
        expert_ids.T,
        copy_pick.T,
        later_ids.T,
        slot_table[None, :],
        router_first[0].T,
        router_second[0].T,
        expert_in[0],
        expert_out[0],
    )
    return states[None], column.reshape(-1, 1)


def solution(mesh):
    in_specs = (
        P("expert", "segment"),
        P("segment", None),
        P("segment", None, None),
        P("segment", None),
        P("segment", None, None),
        P("expert", None),
        P("expert", None),
        P("expert", None),
        P(),
        P(("segment", "expert"), None, None),
        P(("segment", "expert"), None, None),
    )
    out_specs = (P("segment", "expert", None), P("expert", "segment"))
    return jax.shard_map(
        per_device, mesh=mesh, in_specs=in_specs, out_specs=out_specs, check_vma=False
    )
```

```python
import functools
import math

import jax
import jax.numpy as jnp
from jax import lax
from jax.experimental import pallas as pl
from jax.experimental.pallas import tpu as pltpu
from jax.sharding import PartitionSpec as P

LANES = 128
VMEM_MOST = 67043328
MESH = pl.DeviceIdType.MESH
EPS = 1e-06
RING = 4
GAPS = (3, 3, 3)
LAST_GAP = 3
EXTRA_ROWS = 16


def grid_sides(count):
    outer = 1
    while outer**3 < count:
        outer *= 2
    rest = count // outer
    middle = 1
    while middle**2 < rest:
        middle *= 2
    return outer, middle, rest // middle


class Plan:
    def __init__(self, sides):
        logs = [side.bit_length() - 1 for side in sides]
        n_a, n_b, n_c = logs
        bits_c = list(range(n_c))
        bits_b = list(range(n_c, n_c + n_b))
        bits_a = list(range(n_c + n_b, n_c + n_b + n_a))
        self.count = n_a + n_b + n_c
        self.blocks = 1 << self.count
        self.leaf = (bits_c[0], bits_b[0])
        orders = (
            (bits_c + bits_a + bits_b, bits_c + bits_b + bits_a),
            (bits_b + bits_a + bits_c, bits_b + bits_c + bits_a),
        )
        self.rest = [[order[1:] for order in pair] for pair in orders]
        self.stages = self.count - 1
        short = self.stages == len(GAPS)
        gaps = GAPS if short else (1,) * self.stages
        self.lags = [sum(gaps[:t]) for t in range(self.stages + 1)]
        self.gap = max(gaps)
        self.last_gap = LAST_GAP if short else 2
        self.pick_lag = self.lags[-1]
        self.multiply_lag = self.pick_lag + self.last_gap
        self.stage_ring = self.ring(self.gap, self.gap)
        self.held_ring = self.ring(self.pick_lag, self.gap)
        self.last_ring = self.ring(self.last_gap, self.last_gap)

    def ring(self, busy, gap):
        ahead = busy + 1 + (busy + 1) % 2
        return ahead + 1 + gap + (ahead + 1 + gap) % 2

    def split(self, rows):
        part = max(3 * rows // 8 // 16 * 16, 16)
        return part, rows - part

    def dims(self, which, order, done):
        used = [self.leaf[which]] + self.rest[which][order][:done]
        return [bit for bit in reversed(range(self.count)) if bit not in used]


def bit_of(index, bit):
    return (index // (1 << bit)) % 2


def flip(index, bit):
    return index + (1 << bit) * (1 - 2 * bit_of(index, bit))


def digits(value, count):
    return [(value // (1 << (count - 1 - i))) % 2 for i in range(count)]


def spread_index(value, bit, own):
    low = 1 << bit
    return (value // low) * (2 * low) + own * low + value % low


def remote(src, dst, send, recv, peer):
    return pltpu.make_async_remote_copy(
        src_ref=src,
        dst_ref=dst,
        send_sem=send,
        recv_sem=recv,
        device_id=peer,
        device_id_type=MESH,
    )


def run_stages(chunks, stages, early, late):
    depth = max(lag for lag, _ in stages)

    @pl.loop(0, chunks + depth)
    def _(step):
        for lag, stage in stages:
            if lag in early:

                @pl.when(step == lag)
                def _():
                    early[lag]()

            @pl.when((step >= lag) & (step - lag < chunks))
            def _():
                stage(step - lag)

        for when, hook in late.items():

            @pl.when(step == when)
            def _():
                hook()


def by_parity(stage):
    def run(j):
        for which in range(2):

            @pl.when(j % 2 == which)
            def _():
                stage(which, j)

    return run


def near_friends(plan, seg, me):
    friends = [(1 - seg, me)] + [(seg, flip(me, bit)) for bit in range(plan.count)]
    return friends + [(1 - seg, flip(me, bit)) for bit in plan.leaf]


def slots_of(plan, seg, me):
    chips = [me] + [flip(me, bit) for bit in plan.leaf]
    return [core * plan.blocks + chip for chip in chips for core in (seg, 1 - seg)]


def rows_of(which):
    return (0, 1, 2 + 2 * which, 3 + 2 * which)


def make_weights(plan, me, room, places, gates, wts):
    tok_rows = places.shape[-1]
    row = lax.broadcasted_iota(jnp.int32, (room, tok_rows), 0).astype(jnp.float32)
    for which in range(2):
        bit = plan.leaf[which]

        @pl.loop(0, plan.blocks // 2)
        def _(q):
            d = spread_index(q, bit, bit_of(me, bit))
            place, gate = places[d], gates[d]
            pieces = []
            for k in rows_of(which):
                hit = place[k : k + 1, :] == row
                pieces.append(jnp.where(hit, gate[k : k + 1, :], 0.0))
            pad = -(4 * room) % LANES
            if pad:
                pieces.append(jnp.zeros((pad, tok_rows), jnp.float32))
            turned = jnp.concatenate(pieces, axis=0).T
            wts[which, q] = turned[:, : 4 * room].astype(jnp.bfloat16)


def return_scratch(plan, room, tok_rows):
    def bf(*shape):
        return pltpu.VMEM(shape, jnp.bfloat16)

    def dma(*shape):
        return pltpu.SemaphoreType.DMA(shape)

    side = plan.blocks // 2
    low = (2,) * plan.stages
    split = plan.split(tok_rows)
    landing = [
        bf(2, side, tok_rows, 4 * room),
        bf(RING, 2, 2, *low, room, LANES),
        bf(RING, 2, *low, room, LANES),
    ]
    local = [
        bf(2, 2, 2, *((2,) * plan.count), room, LANES),
        bf(2, 2, *low, tok_rows, LANES),
    ]
    sems = [dma(2, 2, 3), dma(RING, 2, 3)]
    for t in range(plan.stages):
        for rows in split:
            left = (2,) * (plan.stages - 1 - t)
            landing.append(bf(RING, 2, *left, rows, LANES))
            if t + 1 < plan.stages:
                local.append(bf(2, 2, *left, rows, LANES))
        sems += [dma(2, 2, 2), dma(RING, 2, 2)]
    return landing, local, sems


def return_steps(plan, seg, me, act, weight_of, finish, landing, local, sems):
    wts, leaf, swapped = landing[:3]
    ys, first = local[:2]
    stages = plan.stages
    arrived = [landing[3 + 2 * t : 5 + 2 * t] for t in range(stages)]
    parts = [local[2 + 2 * t : 4 + 2 * t] for t in range(stages - 1)]
    side = plan.blocks // 2
    room = ys.shape[-2]
    slot_rows = plan.blocks * room
    tok_rows = first.shape[-2]
    split = plan.split(tok_rows)
    spans = (pl.ds(0, split[0]), pl.ds(split[0], split[1]))
    mine = [bit_of(me, bit) for bit in range(plan.count)]

    def region(which, own):
        bit = plan.leaf[which]
        place = plan.count - 1 - bit
        return tuple(
            (mine[bit] if own else 1 - mine[bit]) if i == place else slice(None)
            for i in range(plan.count)
        )

    def first_copies(which, j, kept=(0, 1, 2)):
        nbr = flip(me, plan.leaf[which])
        sources = (
            (ys.at[(j % 2, which, 1) + region(which, False)], leaf.at[j % RING, which, 0], (seg, nbr)),
            (ys.at[(j % 2, which, 0) + region(which, False)], leaf.at[j % RING, which, 1], (1 - seg, nbr)),
            (ys.at[(j % 2, which, 0) + region(which, True)], swapped.at[j % RING, which], (1 - seg, me)),
        )
        return [
            remote(src, dst, sems[0].at[j % 2, which, k], sems[1].at[j % RING, which, k], peer)
            for k, (src, dst, peer) in enumerate(sources)
            if k in kept
        ]

    def held_at(which, t, r, j, index):
        if t == 0:
            return (j % 2, which) + index + (spans[r],)
        return (j % 2, which) + index

    def send(which, t, r, j):
        bit = plan.rest[which][r][t]
        dims = plan.dims(which, r, t)
        index = tuple(1 - mine[d] if d == bit else slice(None) for d in dims)
        source = first if t == 0 else parts[t - 1][r]
        return remote(
            source.at[held_at(which, t, r, j, index)],
            arrived[t][r].at[j % RING, which],
            sems[2 + 2 * t].at[j % 2, which, r],
            sems[3 + 2 * t].at[j % RING, which, r],
            (seg, flip(me, bit)),
        )

    def project(j):
        weight = weight_of(j)
        blocks = (2,) * plan.count
        for section in range(2):
            result = jnp.dot(
                act[pl.ds(section * slot_rows, slot_rows), :],
                weight[...],
                preferred_element_type=jnp.float32,
            ).astype(jnp.bfloat16)
            for which in range(2):
                half = result[:, which * LANES : (which + 1) * LANES]
                ys[j % 2, which, section] = half.reshape(blocks + (room, LANES))
            for which in range(2):
                for k in ((1, 2), (0,))[section]:
                    first_copies(which, j, (k,))[0].start()
    def combine(j):
        for which in range(2):
            for copy in first_copies(which, j):
                copy.wait()
            own = mine[plan.leaf[which]]
            place = plan.count - 1 - plan.leaf[which]

            @pl.loop(0, side, unroll=8)
            def _(q):
                ix = digits(q, stages)
                full = tuple(ix[:place] + [own] + ix[place:])
                ix = tuple(ix)
                both = jnp.concatenate(
                    [
                        ys[(j % 2, which, 1) + full],
                        swapped[(j % RING, which) + ix],
                        leaf[(j % RING, which, 0) + ix],
                        leaf[(j % RING, which, 1) + ix],
                    ],
                    axis=0,
                )
                part = jnp.dot(wts[which, q], both, preferred_element_type=jnp.float32)
                first[(j % 2, which) + ix] = part.astype(jnp.bfloat16)

            for r in range(2):
                send(which, 0, r, j).start()

    def reduce_stage(t, j):
        last = t == stages - 1
        left = stages - 1 - t
        for which in range(2):
            for r in range(2):
                send(which, t, r, j).wait()
                bit = plan.rest[which][r][t]
                place = plan.dims(which, r, t).index(bit)
                source = first if t == 0 else parts[t - 1][r]

                def total(ix):
                    full = tuple(ix[:place] + [mine[bit]] + ix[place:])
                    held = source[held_at(which, t, r, j, full)]
                    came = arrived[t][r][(j % RING, which) + tuple(ix)]
                    return held.astype(jnp.float32) + came.astype(jnp.float32)

                if last:
                    start = pl.multiple_of((2 * j + which) * LANES, LANES)
                    finish(spans[r], pl.ds(start, LANES), total([]))
                else:

                    @pl.loop(0, 1 << left, unroll=2)
                    def _(e):
                        ix = digits(e, left)
                        parts[t][r][(j % 2, which) + tuple(ix)] = total(ix).astype(jnp.bfloat16)

                    send(which, t + 1, r, j).start()

    steps = [(0, project), (1, combine)]
    for t in range(stages):
        steps.append((2 + t, functools.partial(reduce_stage, t)))
    return steps


def gather_scratch(plan, room, tok_rows, units):
    def bf(*shape):
        return pltpu.VMEM(shape, jnp.bfloat16)

    def f32(*shape):
        return pltpu.VMEM(shape, jnp.float32)

    def dma(*shape):
        return pltpu.SemaphoreType.DMA(shape)

    blocks = plan.blocks
    side = blocks // 2
    slot_rows = blocks * room
    near = plan.last_gap + 1
    landing = [
        bf(plan.held_ring, *((2,) * plan.stages), tok_rows, LANES),
        bf(plan.last_ring, 3, side, room, LANES),
    ]
    local = [
        bf(2, side, 4 * room, tok_rows),
        f32(slot_rows, LANES),
        bf(near, side, room, LANES),
        bf(near, 3, side, room, LANES),
        bf(2 * slot_rows, 2 * LANES),
        f32(2 * slot_rows, 2 * units),
        bf(near, 2 * LANES, 2 * units),
    ]
    sems = [dma(near, 3), dma(plan.last_ring, 3), dma(near, 2)]
    for _ in range(plan.stages):
        sems += [dma(plan.stage_ring, 2), dma(plan.stage_ring, 2)]
    return landing, local, sems


def gather_steps(plan, seg, me, x, places, squares, gains, w_in, act, scratch, sems):
    (held, got, picks, scale, keep, give, lhs, hid, w_buf) = scratch
    blocks = plan.blocks
    side = blocks // 2
    mine = [bit_of(me, bit) for bit in range(plan.count)]
    tok_rows, half = x.shape
    split = (tok_rows // 2, tok_rows // 2)
    spans = (pl.ds(0, split[0]), pl.ds(split[0], split[1]))
    wide = LANES
    room = keep.shape[-2]
    slot_rows = blocks * room
    units = act.shape[1]
    near = plan.last_gap + 1
    tile = math.gcd(slot_rows, 256)

    def columns(j):
        return pl.ds(pl.multiple_of(j * wide, wide), wide)

    def send(which, t, r, j):
        order = plan.rest[which][r]
        bit = order[plan.stages - 1 - t]
        free = order[plan.stages - t :]
        rows = spans[r]
        index = tuple(slice(None) if d in free else mine[d] for d in plan.dims(which, r, 0))
        dst = held.at[(j % plan.held_ring,) + index + (rows,)]
        return remote(
            x.at[rows, columns(j)] if t == 0 else dst,
            dst,
            sems[3 + 2 * t].at[j % plan.stage_ring, r],
            sems[4 + 2 * t].at[j % plan.stage_ring, r],
            (seg, flip(me, bit)),
        )

    def first_send(which, j):
        for r in range(2):
            send(which, 0, r, j).start()
        index = tuple(mine[d] for d in plan.dims(which, 0, 0))
        held[(j % plan.held_ring,) + index] = x[:, columns(j)]

    def relay(t, which, j):
        for r in range(2):
            send(which, t - 1, r, j).wait()
            send(which, t, r, j).start()

    def last_copies(which, j):
        nbr = flip(me, plan.leaf[which])
        peers = ((1 - seg, me), (seg, nbr), (1 - seg, nbr))
        return [
            remote(
                give.at[j % near, k],
                got.at[j % plan.last_ring, k],
                sems[0].at[j % near, k],
                sems[1].at[j % plan.last_ring, k],
                peer,
            )
            for k, peer in enumerate(peers)
        ]

    def weight_copies(j):
        copies = []
        for which, owner in enumerate((seg, 1 - seg)):
            rows = pl.ds(pl.multiple_of(owner * half + j * wide, wide), wide)
            copies.append(
                pltpu.make_async_copy(
                    w_in.at[rows, :],
                    w_buf.at[j % near, pl.ds(which * wide, wide)],
                    sems[2].at[j % near, which],
                )
            )
        return copies

    row = lax.broadcasted_iota(jnp.int32, (room, tok_rows), 0).astype(jnp.float32)

    def read_places():
        for which in range(2):
            bit = plan.leaf[which]

            @pl.loop(0, side)
            def _(q):
                d = spread_index(q, bit, mine[bit])
                place = places[d]
                picks[which, q] = jnp.concatenate(
                    [jnp.where(place[k : k + 1, :] == row, 1.0, 0.0) for k in rows_of(which)],
                    axis=0,
                ).astype(jnp.bfloat16)

    def read_factors():
        @pl.loop(0, blocks)
        def _(d):
            own = places[d][0:1, :] == row
            total = squares[0, pl.ds(d, 1), :] + squares[1, pl.ds(d, 1), :]
            line = lax.rsqrt(total / (2 * half) + EPS)
            factor = jnp.sum(jnp.where(own, line, 0.0), axis=1, keepdims=True)
            rows = pl.ds(pl.multiple_of(d * room, room), room)
            scale[rows, :] = jnp.broadcast_to(factor, (room, wide))

    def pick(which, j):
        for copy in weight_copies(j):
            copy.start()
        for r in range(2):
            send(which, plan.stages - 1, r, j).wait()

        @pl.loop(0, side, unroll=8)
        def _(q):
            there = held[(j % plan.held_ring,) + tuple(digits(q, plan.stages))]
            taken = jnp.dot(picks[which, q], there, preferred_element_type=jnp.float32)
            taken = taken.astype(jnp.bfloat16)
            keep[j % near, q] = taken[:room]
            for k in range(3):
                give[j % near, k, q] = taken[(k + 1) * room : (k + 2) * room]

        for copy in last_copies(which, j):
            copy.start()

    def multiply(which, j):
        for copy in last_copies(which, j):
            copy.wait()
        for copy in weight_copies(j):
            copy.wait()
        bit = plan.leaf[which]
        places = [
            pl.ds(pl.multiple_of(owner * half + j * wide, wide), wide) for owner in (seg, 1 - seg)
        ]
        factors = [[gains[pl.ds(section, 1), place] for place in places] for section in range(2)]

        @pl.loop(0, side, unroll=2)
        def _(q):
            for own, sources in (
                (mine[bit], (keep.at[j % near, q], got.at[j % plan.last_ring, 0, q])),
                (1 - mine[bit], (got.at[j % plan.last_ring, 1, q], got.at[j % plan.last_ring, 2, q])),
            ):
                base = spread_index(q, bit, own) * room
                factor = scale[pl.ds(pl.multiple_of(base, room), room), :]
                for f, source in enumerate(sources):
                    scaled = source[...].astype(jnp.float32) * factor
                    for section in range(2):
                        to = pl.ds(pl.multiple_of(section * slot_rows + base, room), room)
                        lhs[to, pl.ds(f * wide, wide)] = (scaled * factors[section][f]).astype(
                            jnp.bfloat16
                        )

        for section in range(2):
            rows = pl.ds(section * slot_rows, slot_rows)
            hid[rows, :] += jnp.dot(
                lhs[rows, :], w_buf[j % near], preferred_element_type=jnp.float32
            )

    def clear():
        @pl.loop(0, 2 * slot_rows // tile)
        def _(r):
            rows = pl.ds(pl.multiple_of(r * tile, tile), tile)
            hid[rows, :] = jnp.zeros((tile, 2 * units), jnp.float32)

    def activate():
        @pl.loop(0, 2 * slot_rows // tile)
        def _(r):
            rows = pl.ds(pl.multiple_of(r * tile, tile), tile)
            gate = hid[rows, :units]
            act[rows, :] = (gate / (1.0 + jnp.exp(-gate)) * hid[rows, units:]).astype(jnp.bfloat16)

    steps = [(0, by_parity(first_send))]
    for t in range(1, plan.stages):
        steps.append((plan.lags[t], by_parity(functools.partial(relay, t))))
    steps += [(plan.pick_lag, by_parity(pick)), (plan.multiply_lag, by_parity(multiply))]
    return steps, read_places, read_factors, clear, activate


def column_sum(values):
    return jnp.sum(values, axis=1, keepdims=True)


def fused_kernel(plan, room, capacity, sizes, *refs):
    (x, gain, gain2, ids, copies, later_ids, table, router_in, router2_in, w_in, w_out) = refs[:11]
    states, ratio = refs[11:13]
    n_own, n_gather, n_back, n_gather_sems = sizes
    own = refs[13 : 13 + n_own]
    whole, gain_got, gains, act, mixed, squares, normed, score, score_got = own[:9]
    router, router2, spots, weights, places, gates, wide, w_ring, halves = own[9:]
    refs = refs[13 + n_own :]
    gather_landing, refs = refs[:n_gather], refs[n_gather:]
    back, sems = refs[:n_back], refs[n_back:]
    swap_sems, load_sems, share_sems, sems = sems[:2], sems[2], sems[3:5], sems[5:]
    gather_sems, return_sems = sems[:n_gather_sems], sems[n_gather_sems:]
    seg = lax.axis_index("segment")
    me = lax.axis_index("expert")
    mine = [bit_of(me, bit) for bit in range(plan.count)]
    blocks = plan.blocks
    count = plan.count
    tok_rows, half = x.shape
    full = 2 * half
    top = ids.shape[0]
    tiles = full // LANES
    slot_count = table.shape[1]
    f32 = jnp.float32
    partner = (1 - seg, me)
    at_home = tuple(reversed(mine))

    def tile_at(i):
        return pl.ds(pl.multiple_of(i * LANES, LANES), LANES)

    own_columns = pl.ds(pl.multiple_of(seg * half, half), half)
    swap_x = remote(x, whole.at[:, own_columns], swap_sems[0].at[0], swap_sems[1].at[0], partner)
    swap_gain = remote(gain, gain_got, swap_sems[0].at[1], swap_sems[1].at[1], partner)
    swap_halves = remote(
        halves.at[0], halves.at[1], swap_sems[0].at[3], swap_sems[1].at[3], partner
    )
    swap_score = remote(score, score_got, swap_sems[0].at[2], swap_sems[1].at[2], partner)
    load_router = pltpu.make_async_copy(router_in, router, load_sems.at[0])
    load_router2 = pltpu.make_async_copy(router2_in, router2, load_sems.at[1])

    def load_w_out(j):
        columns = pl.ds(pl.multiple_of(j * 2 * LANES, 2 * LANES), 2 * LANES)
        return pltpu.make_async_copy(
            w_out.at[:, columns], w_ring.at[j % 3], load_sems.at[2 + j % 3]
        )

    back_chunks = full // (2 * LANES)

    def weight_of(j):
        load_w_out(j).wait()

        @pl.when(j + 2 < back_chunks)
        def _():
            load_w_out(j + 2).start()

        return w_ring.at[j % 3]

    def share(kind, bit):
        ref = (spots, weights)[kind]
        index = tuple(slice(None) if d < bit else mine[d] for d in reversed(range(count)))
        return remote(
            ref.at[index],
            ref.at[index],
            share_sems[0].at[kind, bit],
            share_sems[1].at[kind, bit],
            (seg, flip(me, bit)),
        )

    def matches():
        line = table[...].astype(f32)
        i_row = lax.broadcasted_iota(jnp.int32, (slot_count, slot_count), 0)
        i_col = lax.broadcasted_iota(jnp.int32, (slot_count, slot_count), 1)
        column = column_sum(jnp.where(i_row == i_col, line, 0.0))
        same = column == line
        rank = column_sum(jnp.where(same & (i_col < i_row), 1.0, 0.0))
        holders = column_sum(jnp.where(same, 1.0, 0.0))
        wanted = ids[...].astype(f32)
        choice = copies[...].astype(f32)
        of_two = choice - 2.0 * jnp.floor(choice * 0.5)
        of_three = choice - 3.0 * jnp.floor((choice + 0.5) * (1.0 / 3.0))
        found = []
        for k in range(top):
            turn = jnp.where(
                holders == 1.0,
                0.0,
                jnp.where(holders == 2.0, of_two[k : k + 1, :], of_three[k : k + 1, :]),
            )
            found.append((column == wanted[k : k + 1, :]) & (rank == turn))
        return wanted, found

    def place_tokens():
        hit = jnp.zeros((slot_count, tok_rows), f32)
        for match in matches()[1]:
            hit += jnp.where(match, 1.0, 0.0)
        t_row = lax.broadcasted_iota(jnp.int32, (tok_rows, tok_rows), 0)
        t_col = lax.broadcasted_iota(jnp.int32, (tok_rows, tok_rows), 1)
        earlier = jnp.where(t_row < t_col, 1.0, 0.0).astype(jnp.bfloat16)
        before = jnp.dot(hit.astype(jnp.bfloat16), earlier, preferred_element_type=f32)
        place = jnp.where((hit > 0.0) & (before < capacity), before, -1.0)
        total = jnp.zeros((tok_rows, LANES), f32)
        for i in range(half // LANES):
            part = x[:, i * LANES : (i + 1) * LANES].astype(f32)
            total += part * part
        rest = jnp.broadcast_to(column_sum(total), (tok_rows, LANES)).T[0:1, :]
        rows = [place]
        for _ in range(3):
            rows.append(rest.astype(jnp.bfloat16).astype(f32))
            rest = rest - rows[-1]
        rows.append(jnp.zeros((EXTRA_ROWS - 3, tok_rows), f32))
        spots[at_home] = jnp.concatenate(rows, axis=0).astype(jnp.bfloat16)

    def normalize():
        total = jnp.zeros((tok_rows, LANES), f32)
        for i in range(tiles):
            part = whole[:, i * LANES : (i + 1) * LANES].astype(f32)
            total += part * part
        return lax.rsqrt(column_sum(total) / full + EPS)

    def prologue():
        swap_x.wait()
        squares[...] = jnp.broadcast_to(normalize(), (tok_rows, LANES))

        @pl.loop(0, tiles)
        def _(i):
            part = whole[:, tile_at(i)].astype(f32) * squares[...]
            normed[:, tile_at(i)] = (part * gains[1:2, tile_at(i)]).astype(jnp.bfloat16)

    def weigh_tokens():
        load_router.wait()
        logits = lax.dot_general(
            router[...], normed[...], (((1,), (1,)), ((), ())), preferred_element_type=f32
        )
        names = lax.broadcasted_iota(jnp.int32, logits.shape, 0).astype(f32)
        wanted, found = matches()
        chosen = [
            jnp.sum(jnp.where(names == wanted[k : k + 1, :], logits, 0.0), axis=0, keepdims=True)
            for k in range(top)
        ]
        most = functools.reduce(jnp.maximum, chosen)
        lifted = [jnp.exp(value - most) for value in chosen]
        weight = functools.reduce(jnp.add, lifted)
        gate = jnp.zeros((slot_count, tok_rows), f32)
        for k in range(top):
            rounded = (lifted[k] / weight).astype(jnp.bfloat16).astype(f32)
            gate += jnp.where(found[k], rounded, 0.0)
        weights[at_home] = gate.astype(jnp.bfloat16)

    def widen(kind):
        source, target = (spots, weights)[kind], (places, gates)[kind]

        @pl.loop(0, blocks)
        def _(d):
            wide[kind, : source.shape[-2]] = source[tuple(digits(d, count))].astype(f32)
            for k, slot in enumerate(slots_of(plan, seg, me)):
                target[d, k : k + 1, :] = wide[kind, pl.ds(slot, 1), :]
            if kind == 0:
                extra = wide[kind, slot_count : slot_count + 8, :]
                halves[0, pl.ds(d, 1), :] = jnp.sum(extra, axis=0, keepdims=True)

    def pass_on(kind, bit):
        if bit:
            share(kind, bit - 1).wait()
        share(kind, bit).start()

    def combine_weights():
        share(1, count - 1).wait()
        widen(1)
        make_weights(plan, me, room, places, gates, back[0])

    def begin_weights():
        weigh_tokens()
        pass_on(1, 0)

    def gather_part(*local):
        steps, read_places, read_factors, clear, activate = gather_steps(
            plan, seg, me, x, places, halves, gains, w_in, act, gather_landing + local, gather_sems
        )

        def take_places():
            share(0, count - 1).wait()
            widen(0)
            swap_halves.start()
            read_places()

        def take_factors():
            swap_gain.wait()
            gains[0:1, :] = gain_got[...].astype(f32)
            swap_halves.wait()
            read_factors()

        place_tokens()
        whole[:, own_columns] = x[...]
        gains[1:2, :] = gain[...].astype(f32)
        clear()
        pl.semaphore_wait(barrier, len(friends))
        swap_x.start()
        swap_gain.start()
        share(0, 0).start()
        late = {plan.lags[bit] - 1: functools.partial(pass_on, 0, bit) for bit in range(1, count)}
        last = half // LANES + plan.multiply_lag - 1
        start = plan.pick_lag + 2
        pace = min(3, (last - start) // count)
        late[start - 1] = prologue
        late[start] = begin_weights
        for bit in range(1, count):
            late[start + pace * bit] = functools.partial(pass_on, 1, bit)
        late[start + pace * count] = combine_weights
        early = {plan.pick_lag: take_places, plan.multiply_lag: take_factors}
        run_stages(half // LANES, steps, early, late)
        activate()

    def finish(rows, columns, total):
        value = whole[rows, columns].astype(f32) + total
        mixed[rows, columns] = value
        states[rows, columns] = value.astype(jnp.bfloat16)
        squares[rows, :] += value * value

    def return_part(*local):
        steps = return_steps(plan, seg, me, act, weight_of, finish, back, local, return_sems)
        run_stages(back_chunks, steps, {}, {})

    barrier = pltpu.get_barrier_semaphore()
    friends = near_friends(plan, seg, me)
    for friend in friends:
        pl.semaphore_signal(barrier, inc=1, device_id=friend, device_id_type=MESH)
    load_router.start()
    load_router2.start()
    load_w_out(0).start()
    load_w_out(1).start()
    pl.run_scoped(gather_part, *gather_scratch(plan, room, tok_rows, act.shape[1])[1])
    squares[...] = jnp.zeros((tok_rows, LANES), f32)
    pl.run_scoped(return_part, *return_scratch(plan, room, tok_rows)[1])
    inverse = lax.rsqrt(column_sum(squares[...]) / full + EPS)
    squares[...] = jnp.broadcast_to(inverse, (tok_rows, LANES))

    @pl.loop(0, tiles)
    def _(i):
        part = mixed[:, tile_at(i)] * squares[...]
        normed[:, tile_at(i)] = (part * gain2[:, tile_at(i)].astype(f32)).astype(jnp.bfloat16)

    load_router2.wait()
    logits = lax.dot_general(
        router2[...], normed[...], (((1,), (1,)), ((), ())), preferred_element_type=f32
    )
    shifted = logits - jnp.max(logits, axis=0, keepdims=True)
    logp = shifted - jnp.log(jnp.sum(jnp.exp(shifted), axis=0, keepdims=True))
    names = lax.broadcasted_iota(jnp.int32, logits.shape, 0).astype(f32)
    wanted = later_ids[...].astype(f32)
    total = jnp.zeros((1, tok_rows), f32)
    for k in range(top):
        total += jnp.sum(jnp.where(names == wanted[k : k + 1, :], logp, 0.0), axis=0, keepdims=True)
    score[...] = jnp.broadcast_to(total, score.shape)
    swap_score.start()
    swap_score.wait()
    sign = (2 * seg - 1).astype(f32)
    difference = (score[0:1, :] - score_got[0:1, :]) * sign
    turned = jnp.broadcast_to(difference, (tok_rows, tok_rows)).T
    t_row = lax.broadcasted_iota(jnp.int32, (tok_rows, tok_rows), 0)
    t_col = lax.broadcasted_iota(jnp.int32, (tok_rows, tok_rows), 1)
    picked = jnp.sum(jnp.where(t_row == 2 * t_col + seg, turned, 0.0), axis=0, keepdims=True)
    ratio[...] = picked[:, : tok_rows // 2]


def fused_scratch(plan, room, tok_rows, half, slot_count, units, experts):
    full = 2 * half
    rows = 2 * plan.blocks * room
    low = (2,) * plan.count

    def bf(*shape):
        return pltpu.VMEM(shape, jnp.bfloat16)

    def f32(*shape):
        return pltpu.VMEM(shape, jnp.float32)

    own = [
        bf(tok_rows, full),
        bf(1, full),
        f32(2, full),
        bf(rows, units),
        f32(tok_rows, full),
        f32(tok_rows, LANES),
        bf(tok_rows, full),
        f32(8, tok_rows),
        f32(8, tok_rows),
        bf(experts, full),
        bf(experts, full),
        bf(*low, slot_count + EXTRA_ROWS, tok_rows),
        bf(*low, slot_count, tok_rows),
        f32(plan.blocks, 8, tok_rows),
        f32(plan.blocks, 8, tok_rows),
        f32(2, slot_count + EXTRA_ROWS, tok_rows),
        bf(3, units, 2 * LANES),
        f32(2, plan.blocks, tok_rows),
    ]
    gather, _, gather_sems = gather_scratch(plan, room, tok_rows, units)
    back, _, back_sems = return_scratch(plan, room, tok_rows)
    shapes = ((4,), (4,), (5,), (2, plan.count), (2, plan.count))
    swap = [pltpu.SemaphoreType.DMA(shape) for shape in shapes]
    sizes = (len(own), len(gather), len(back), len(gather_sems))
    return own + gather + back, swap + gather_sems + back_sems, sizes


def fused_call(plan, room, capacity, scratch, sems, sizes, *args):
    tok_rows, half = args[0].shape
    vmem = pl.BlockSpec(memory_space=pltpu.VMEM)
    anywhere = pl.BlockSpec(memory_space=pl.ANY)
    return pl.pallas_call(
        functools.partial(fused_kernel, plan, room, capacity, sizes),
        out_shape=(
            jax.ShapeDtypeStruct((tok_rows, 2 * half), jnp.bfloat16),
            jax.ShapeDtypeStruct((1, tok_rows // 2), jnp.float32),
        ),
        in_specs=[vmem] * 7 + [anywhere] * 4,
        out_specs=(vmem, vmem),
        scratch_shapes=scratch + sems,
        compiler_params=pltpu.CompilerParams(
            collective_id=0, has_side_effects=True, vmem_limit_bytes=VMEM_MOST
        ),
        name="fused_layer",
    )(*args)


def per_device(
    rollout,
    norm_gain,
    router_first,
    gain_second,
    router_second,
    expert_ids,
    copy_pick,
    later_ids,
    slot_table,
    expert_in,
    expert_out,
):
    segment_count = lax.axis_size("segment")
    chip_count = lax.axis_size("expert")
    tok_rows, half = rollout.shape
    capacity = 3 * tok_rows * expert_ids.shape[1] // (2 * segment_count * chip_count)
    plan = Plan(grid_sides(chip_count))
    room = -(-capacity // 16) * 16
    scratch, sems, sizes = fused_scratch(
        plan,
        room,
        tok_rows,
        half,
        slot_table.shape[0],
        expert_out.shape[1],
        router_first.shape[2],
    )
    states, column = fused_call(
        plan,
        room,
        capacity,
        scratch,
        sems,
        sizes,
        rollout,
        norm_gain,
        gain_second,
        expert_ids.T,
        copy_pick.T,
        later_ids.T,
        slot_table[None, :],
        router_first[0].T,
        router_second[0].T,
        expert_in[0],
        expert_out[0],
    )
    return states[None], column.reshape(-1, 1)


def solution(mesh):
    in_specs = (
        P("expert", "segment"),
        P("segment", None),
        P("segment", None, None),
        P("segment", None),
        P("segment", None, None),
        P("expert", None),
        P("expert", None),
        P("expert", None),
        P(),
        P(("segment", "expert"), None, None),
        P(("segment", "expert"), None, None),
    )
    out_specs = (P("segment", "expert", None), P("expert", "segment"))
    return jax.shard_map(
        per_device, mesh=mesh, in_specs=in_specs, out_specs=out_specs, check_vma=False
    )
```
